128 devices in a mesh: inner: 16 (over x_lo, z, core), outer: 8 (over x_hi, y).
Axes of the slice: x: 4 (x_hi: 2, x_lo: 2; x = x_hi * 2 + x_lo), y: 4, z: 4, core: 2. Of those that a mesh axis runs over, the one named last changes fastest.
Arguments:
- layer_input: bfloat16 [16384, 6144], P(('inner', 'outer')), may hold values from -0.25 to 0.25
- queries: bfloat16 [16384, 768], P(('inner', 'outer')), may hold values from -6 to 6
- keys_values: bfloat16 [16384, 256], P(('inner', 'outer')), may hold values from -6 to 6
- attn_out: bfloat16 [16384, 768], P(('inner', 'outer')), may hold values from -6 to 6
- out_grad: bfloat16 [16384, 768], P(('inner', 'outer')), may hold values from -6 to 6
- log_sums: float32 [6, 16384], P(None, ('inner', 'outer')), may hold values from 5 to 8
- doc_ids: int32 [16384], replicated, may hold values from 0 to 15, never falling along the last dimension, each value on 1 to 2048 neighbouring positions
- span_order: int32 [256], replicated, may hold values from 0 to 255, each once
Outputs:
- query_grad: bfloat16 [16384, 768], P(('inner', 'outer'))
- kv_grad: bfloat16 [16384, 256], P(('inner', 'outer'))
- weight_grad: float32 [6144, 256], P(('inner', 'outer'))
The draws below stay inside these ranges and needn't reach their ends.
Inputs may be any that keep to these rules, and one draw needn't show every extreme that they name: `doc_ids`: never falling; each document holds 1 to 2048 positions. `span_order`: each span number once.
All inputs are finite; a program needn't handle non-finite values.
Results may differ from the reference program's by a relative error of at most 0.015.
Values may be sent and summed in bfloat16 or wider, within the bound.
A program may use at most 64 MiB of HBM per device.

```python
import math
import jax
import jax.numpy as jnp
import numpy as np
from jax import lax

D = 6144
HD = 128
HEADS = 6
TOK_DEV = 128
DOCS = 16
TOKENS = 16384
SPANS = 256
MOST_DOC = 2048


def with_spikes(values, stream_key, source, target, shards_of, factor):
    def block_of(position):
        return (jnp.arange(values.shape[position]) // (values.shape[position] // shards_of)).reshape((-1,) + (1,) * (values.ndim - 1 - position))

    one_side = jax.random.permutation(stream_key, shards_of)[block_of(target)]
    other_side = (block_of(target) + shards_of // 2) % shards_of
    return jnp.where((block_of(source) == one_side) | (block_of(source) == other_side), factor * values, values)


def levels(stream_key, shape, cuts, least, top_value):
    loudness = 1.0
    for dim, blocks in cuts:
        steps = jax.random.uniform(jax.random.fold_in(jax.random.fold_in(stream_key, 6), dim), (blocks,), jnp.float32, least / len(cuts), top_value / len(cuts))
        loudness = loudness * jnp.repeat(jnp.exp(steps), shape[dim] // blocks).reshape((-1,) + (1,) * (len(shape) - 1 - dim))
    return loudness


def split_up(amount, total, bound, slope):
    portions = [(1 << 20) // math.isqrt(rank ** slope) + 1 for rank in range(2, amount + 1)]
    spare, holding = total - bound - (amount - 1), [1] * (amount - 1)
    while spare > 0:
        candidates = [i for i in range(amount - 1) if holding[i] < bound]
        whole, budget = sum([portions[i] for i in candidates]), spare
        for i in candidates:
            extra = min(bound - holding[i], max(1, budget * portions[i] // whole), spare)
            holding[i] = holding[i] + extra
            spare = spare - extra
    return np.array([bound] + holding)


def uneven(rng, count, total, limit, skew):
    if count == 2:
        one = jax.random.randint(rng, (), max(1, total - limit), min(limit, total - 1) + 1)
        return jnp.stack([one, total - one])
    lengths = jnp.asarray(split_up(count, total, limit, skew), jnp.int32)
    pairs = (count - 1) // 2
    source_of, sink = lengths[1:1 + 2 * pairs:2], lengths[2:2 + 2 * pairs:2]
    margin = jnp.minimum(source_of - 1, limit - sink)
    shifted = jax.random.randint(jax.random.fold_in(rng, 1), (pairs,), 0, 1 << 20) % (margin + 1)
    lengths = lengths.at[1:1 + 2 * pairs:2].set(source_of - shifted).at[2:2 + 2 * pairs:2].set(sink + shifted)
    return lengths[jax.random.permutation(jax.random.fold_in(rng, 2), count)]


def scatter_about(key, shape, scale, most, cuts=(), kind=jnp.bfloat16):
    values = jax.random.normal(key, shape, jnp.float32) * scale
    if len(cuts) > 0:
        values = levels(key, shape, cuts, -0.22, 0.18) * values
    return jnp.clip(values, min=-most, max=most).astype(kind)


def gaussian_with(key, extent, scale, most, pieces, heavy, kind=jnp.bfloat16):
    result = scale * jax.random.normal(key, extent, jnp.float32)
    if pieces:
        result = result * levels(key, extent, pieces, -0.22, 0.18)
    return jnp.clip(with_spikes(result, jax.random.fold_in(key, 3), *heavy), -most, most).astype(kind)


def setup_inputs(seed: int = 0) -> dict:
    key_of = jax.random.split(jax.random.key(seed), 9)
    layer_input = gaussian_with(key_of[0], (TOKENS, D), 0.01, 0.25, ((0, 128),), (0, 1, 128, 5.5))
    queries = scatter_about(key_of[1], (TOKENS, HEADS * HD), 1.0, 6.0, ((0, 128),))
    keys_values = scatter_about(key_of[2], (TOKENS, 2 * HD), 1.0, 6.0, ((0, 128),))
    attn_out = scatter_about(key_of[3], (TOKENS, HEADS * HD), 1.0, 6.0, ((0, 128),))
    out_grad = scatter_about(key_of[4], (TOKENS, HEADS * HD), 1.0, 6.0, ((0, 128),))
    log_sums = jnp.clip(5.0 + 3.0 * jax.random.uniform(key_of[5], (HEADS, TOKENS), jnp.float32) ** levels(key_of[5], (HEADS, TOKENS), ((1, 128),), -0.2, 0.2), 5.0, 8.0)
    doc_ids = jnp.searchsorted(jnp.cumsum(uneven(key_of[6], DOCS, TOKENS, MOST_DOC, 1)), jnp.arange(TOKENS), side="right").astype(jnp.int32)
    span_order = jax.random.permutation(key_of[7], SPANS).astype(jnp.int32)
    return {"layer_input": layer_input, "queries": queries, "keys_values": keys_values, "attn_out": attn_out, "out_grad": out_grad, "log_sums": log_sums, "doc_ids": doc_ids, "span_order": span_order}


def reference(layer_input, queries, keys_values, attn_out, out_grad, log_sums, doc_ids, span_order):
    half_len = TOK_DEV // 2
    row_ids = jnp.arange(TOKENS, dtype=jnp.int32)
    seq_pos = (span_order[row_ids // half_len] * half_len + row_ids % half_len).astype(jnp.int32)
    seq_doc = doc_ids[seq_pos]
    score_scale = HD ** -0.5
    query_heads = queries.astype(jnp.float32).reshape(TOKENS, HEADS, HD)
    grad_heads = out_grad.astype(jnp.float32).reshape(TOKENS, HEADS, HD)
    out_heads = attn_out.astype(jnp.float32).reshape(TOKENS, HEADS, HD)
    row_delta = jnp.einsum("ihc,ihc->hi", grad_heads, out_heads)
    key_rows = keys_values[:, :HD].astype(jnp.float32)
    value_rows = keys_values[:, HD:].astype(jnp.float32)
    block_len = 256 if TOKENS % 256 == 0 else TOKENS
    block_count = TOKENS // block_len

    def block_step(kv_total, block_idx):
        first = (block_idx * block_len).astype(jnp.int32)
        query_blk = lax.dynamic_slice_in_dim(query_heads, first, block_len, 0)
        grad_blk = lax.dynamic_slice_in_dim(grad_heads, first, block_len, 0)
        lse_blk = lax.dynamic_slice_in_dim(log_sums, first, block_len, 1)
        delta_blk = lax.dynamic_slice_in_dim(row_delta, first, block_len, 1)
        pos_blk = lax.dynamic_slice_in_dim(seq_pos, first, block_len, 0)
        doc_blk = lax.dynamic_slice_in_dim(seq_doc, first, block_len, 0)
        scores = jnp.einsum("ihc,jc->hij", query_blk, key_rows) * score_scale
        allowed = (seq_pos[None, :] <= pos_blk[:, None]) & (seq_doc[None, :] == doc_blk[:, None])
        probs = jnp.exp(jnp.where(allowed[None], scores - lse_blk[:, :, None], -1e30))
        probs_low = lax.optimization_barrier(probs.astype(jnp.bfloat16)).astype(jnp.float32)
        prob_grads = jnp.einsum("ihc,jc->hij", grad_blk, value_rows)
        score_grads = (score_scale * probs * (prob_grads - delta_blk[:, :, None])).astype(jnp.bfloat16)
        score_grads = lax.optimization_barrier(score_grads).astype(jnp.float32)
        query_part = jnp.einsum("hij,jc->ihc", score_grads, key_rows).astype(jnp.bfloat16)
        key_part = jnp.einsum("hij,ihc->jc", score_grads, query_blk)
        value_part = jnp.einsum("hij,ihc->jc", probs_low, grad_blk)
        return kv_total + jnp.concatenate([key_part, value_part], axis=1), query_part.reshape(block_len, HEADS * HD)

    kv_total, query_blocks = lax.scan(block_step, jnp.zeros((TOKENS, 2 * HD), jnp.float32), jnp.arange(block_count, dtype=jnp.int32))
    query_grad = query_blocks.reshape(TOKENS, HEADS * HD)
    kv_grad = kv_total.astype(jnp.bfloat16)
    weight_grad = jnp.dot(layer_input.T, kv_grad, preferred_element_type=jnp.float32)
    return query_grad, kv_grad, weight_grad
```

```python
import functools

import jax
import jax.numpy as jnp
from jax import lax
from jax.experimental import pallas as pl
from jax.experimental.pallas import tpu as pltpu
from jax.sharding import PartitionSpec as P

CH = 4
SPAN = 64
HD = 128
HEADS = 6
NQ = SPAN * HEADS
MOST_DOC = 2048


def window_kernel(
    tab,
    q_ref,
    og_ref,
    ao_ref,
    lse_ref,
    pos_ref,
    start_ref,
    kv_hbm,
    dq_ref,
    dkv_hbm,
    kbuf,
    acc,
    obuf,
    zbuf,
    qs,
    gs,
    qt,
    gt,
    delta,
    dqt,
    ksem,
    zsem,
    osem,
    *,
    spans,
    wmax,
):
    scale = HD ** (-0.5)
    base = spans
    zrows = zbuf.shape[0]
    zcount = dkv_hbm.shape[0] // zrows
    p = [tab[base + s] for s in range(2)]
    lo = [tab[base + 2 + s] for s in range(2)]
    nch = [(p[s] - lo[s] + CH) // CH for s in range(2)]
    end = [lo[s] + nch[s] * CH for s in range(2)]

    def key_copy(s, i):
        c = tab[jnp.minimum(lo[s] + i, spans - 1)]
        return pltpu.make_async_copy(
            kv_hbm.at[pl.ds(pl.multiple_of(c * SPAN, SPAN), SPAN)],
            kbuf.at[s, pl.ds(pl.multiple_of(i * SPAN, SPAN), SPAN)],
            ksem.at[s, i],
        )

    for s in range(2):

        @pl.loop(0, nch[s] * CH)
        def _(i):
            key_copy(s, i).start()

    zbuf[...] = jnp.zeros_like(zbuf)

    def zero_copy(i):
        return pltpu.make_async_copy(zbuf, dkv_hbm.at[pl.ds(i * zrows, zrows)], zsem.at[i])

    for i in range(zcount):
        zero_copy(i).start()

    for s in range(2):
        rows = slice(s * SPAN, (s + 1) * SPAN)
        for h in range(HEADS):
            cols = slice(h * HD, (h + 1) * HD)
            dst = slice(h * SPAN, (h + 1) * SPAN)
            qs[s, dst, :] = q_ref[rows, cols]
            gs[s, dst, :] = og_ref[rows, cols]
            prod = og_ref[rows, cols].astype(jnp.float32) * ao_ref[rows, cols].astype(jnp.float32)
            dqt[dst, :] = prod
        delta[s] = jnp.sum(dqt[...].T, axis=0, keepdims=True)
        qt[s] = qs[s].T
        gt[s] = gs[s].T

    for s in range(2):
        lse = lse_ref[pl.ds(s, 1), :]
        qpos = pos_ref[pl.ds(s, 1), :]
        qstart = start_ref[pl.ds(s, 1), :]

        def block(j, dq_acc):
            for i in range(CH):
                key_copy(s, j * CH + i).wait()
            first = pl.multiple_of(j * CH * SPAN, CH * SPAN)
            kc = kbuf[s, pl.ds(first, CH * SPAN), :HD]
            vc = kbuf[s, pl.ds(first, CH * SPAN), HD:]
            st = jnp.dot(kc, qt[s], preferred_element_type=jnp.float32)
            dp = jnp.dot(vc, gt[s], preferred_element_type=jnp.float32)
            kpos = (lo[s] + j * CH) * SPAN + lax.broadcasted_iota(jnp.int32, (CH * SPAN, NQ), 0)
            keep = (kpos >= qstart) & (kpos <= qpos)
            prob = jnp.exp(jnp.where(keep, st * scale - lse, -1e30))
            ds = (scale * prob * (dp - delta[s])).astype(jnp.bfloat16)
            pb = prob.astype(jnp.bfloat16)
            dk = jnp.dot(ds, qs[s], preferred_element_type=jnp.float32)
            dv = jnp.dot(pb, gs[s], preferred_element_type=jnp.float32)
            row0 = pl.multiple_of((lo[s] + j * CH) * SPAN, SPAN)
            at = pl.ds(row0, CH * SPAN)
            if s == 0:
                acc[at, :HD] = dk
                acc[at, HD:] = dv
            else:
                krow = row0 + lax.broadcasted_iota(jnp.int32, (CH * SPAN, HD), 0)
                seen = (krow >= lo[0] * SPAN) & (krow < end[0] * SPAN)
                acc[at, :HD] = dk + jnp.where(seen, acc[at, :HD], 0.0)
                acc[at, HD:] = dv + jnp.where(seen, acc[at, HD:], 0.0)
            return dq_acc + lax.dot_general(
                kc, ds, (((0,), (0,)), ((), ())), preferred_element_type=jnp.float32
            )

        total = lax.fori_loop(0, nch[s], block, jnp.zeros((HD, NQ), jnp.float32))
        dqt[...] = total.T
        for h in range(HEADS):
            dq_ref[s * SPAN : (s + 1) * SPAN, h * HD : (h + 1) * HD] = dqt[
                h * SPAN : (h + 1) * SPAN, :
            ].astype(dq_ref.dtype)

    for i in range(zcount):
        zero_copy(i).wait()

    def out_copy(s, i):
        c = tab[jnp.minimum(lo[s] + i, spans - 1)]
        return pltpu.make_async_copy(
            obuf.at[s, pl.ds(pl.multiple_of(i * SPAN, SPAN), SPAN)],
            dkv_hbm.at[pl.ds(pl.multiple_of(c * SPAN, SPAN), SPAN)],
            osem.at[s, i],
        )

    def mine(s, i):
        k = lo[s] + i
        if s == 1:
            return k < spans
        return (k < spans) & ((k < lo[1]) | (k >= end[1]))

    for s in range(2):

        @pl.loop(0, nch[s] * CH)
        def _(i):
            @pl.when(mine(s, i))
            def _():
                row = pl.multiple_of((lo[s] + i) * SPAN, SPAN)
                obuf[s, pl.ds(pl.multiple_of(i * SPAN, SPAN), SPAN), :] = acc[
                    pl.ds(row, SPAN), :
                ].astype(obuf.dtype)
                out_copy(s, i).start()

    for s in range(2):

        @pl.loop(0, nch[s] * CH)
        def _(i):
            @pl.when(mine(s, i))
            def _():
                out_copy(s, i).wait()


def window_grads(tab, q, og, ao, lse2, pos2, start2, kv_all):
    tokens = kv_all.shape[0]
    spans = tokens // SPAN
    wmax = MOST_DOC // SPAN + 1
    wmax = -(-wmax // CH) * CH
    vmem = pl.BlockSpec(memory_space=pltpu.VMEM)
    anyspace = pl.BlockSpec(memory_space=pl.ANY)
    zrows = 1024
    return pl.pallas_call(
        functools.partial(window_kernel, spans=spans, wmax=wmax),
        out_shape=(
            jax.ShapeDtypeStruct(q.shape, jnp.bfloat16),
            jax.ShapeDtypeStruct((tokens, 2 * HD), jnp.bfloat16),
        ),
        in_specs=[pl.BlockSpec(memory_space=pltpu.SMEM)] + [vmem] * 6 + [anyspace],
        out_specs=(vmem, anyspace),
        scratch_shapes=[
            pltpu.VMEM((2, wmax * SPAN, 2 * HD), jnp.bfloat16),
            pltpu.VMEM((tokens + CH * SPAN, 2 * HD), jnp.float32),
            pltpu.VMEM((2, wmax * SPAN, 2 * HD), jnp.bfloat16),
            pltpu.VMEM((zrows, 2 * HD), jnp.bfloat16),
            pltpu.VMEM((2, NQ, HD), jnp.bfloat16),
            pltpu.VMEM((2, NQ, HD), jnp.bfloat16),
            pltpu.VMEM((2, HD, NQ), jnp.bfloat16),
            pltpu.VMEM((2, HD, NQ), jnp.bfloat16),
            pltpu.VMEM((2, 1, NQ), jnp.float32),
            pltpu.VMEM((NQ, HD), jnp.float32),
            pltpu.SemaphoreType.DMA((2, wmax)),
            pltpu.SemaphoreType.DMA((tokens // zrows,)),
            pltpu.SemaphoreType.DMA((2, wmax)),
        ],
        name="window_grads",
    )(tab, q, og, ao, lse2, pos2, start2, kv_all)


def tables(my_index, log_sums, doc_ids, span_order):
    spans = span_order.shape[0]
    ids = jnp.arange(spans, dtype=jnp.int32)
    inverse = jnp.sum(jnp.where(span_order[None, :] == ids[:, None], ids[None, :], 0), axis=1)
    my_spans = lax.dynamic_slice_in_dim(span_order, 2 * my_index, 2)
    docs = jnp.arange(1, 16, dtype=jnp.int32)
    doc_start = jnp.sum((doc_ids[None, :] < docs[:, None]).astype(jnp.int32), axis=1)
    pos = my_spans[:, None] * SPAN + jnp.arange(SPAN, dtype=jnp.int32)[None, :]
    start = jnp.max(
        jnp.where(doc_start[:, None, None] <= pos[None], doc_start[:, None, None], 0), axis=0
    )
    low = start[:, 0] // SPAN
    tab = jnp.concatenate([inverse, my_spans, low]).astype(jnp.int32)
    pos2 = jnp.tile(pos, (1, HEADS))
    start2 = jnp.tile(start, (1, HEADS))
    lse2 = log_sums.reshape(HEADS, 2, SPAN).transpose(1, 0, 2).reshape(2, NQ)
    return tab, lse2, pos2, start2


def per_device(
    layer_input, queries, keys_values, attn_out, out_grad, log_sums, doc_ids, span_order
):
    axes = ("inner", "outer")
    my_index = lax.axis_index(axes)
    kv_all = lax.all_gather(keys_values, axes, axis=0, tiled=True)
    tab, lse2, pos2, start2 = tables(my_index, log_sums, doc_ids, span_order)
    query_grad, kv_part = window_grads(
        tab, queries, out_grad, attn_out, lse2, pos2, start2, kv_all
    )
    kv_total = lax.psum_scatter(kv_part, axes, scatter_dimension=0, tiled=True)
    weight_grad = lax.psum_scatter(
        lax.dot_general(
            layer_input, kv_total, (((0,), (0,)), ((), ())), preferred_element_type=jnp.float32
        ),
        axes,
        scatter_dimension=0,
        tiled=True,
    )
    return (query_grad, kv_total, weight_grad)


def solution(mesh):
    rows = P(("inner", "outer"), None)
    return jax.shard_map(
        per_device,
        mesh=mesh,
        in_specs=(rows, rows, rows, rows, rows, P(None, ("inner", "outer")), P(), P()),
        out_specs=(rows, rows, rows),
        check_vma=False,
    )
```

```python
import functools

import jax
import jax.numpy as jnp
from jax import lax
from jax.experimental import pallas as pl
from jax.experimental.pallas import tpu as pltpu
from jax.sharding import PartitionSpec as P

CH = 4
SPAN = 64
HD = 128
HEADS = 6
NQ = SPAN * HEADS
MOST_DOC = 2048


def window_kernel(
    tab,
    q_ref,
    og_ref,
    ao_ref,
    lse_ref,
    pos_ref,
    start_ref,
    kv_hbm,
    dq_ref,
    dkv_hbm,
    kbuf,
    acc,
    obuf,
    zbuf,
    qs,
    gs,
    qt,
    gt,
    delta,
    dqt,
    ksem,
    zsem,
    osem,
    *,
    spans,
    wmax,
):
    scale = HD ** (-0.5)
    base = spans
    zrows = zbuf.shape[0]
    zcount = dkv_hbm.shape[0] // zrows
    p = [tab[base + s] for s in range(2)]
    lo = [tab[base + 2 + s] for s in range(2)]
    nch = [(p[s] - lo[s] + CH) // CH for s in range(2)]
    end = [lo[s] + nch[s] * CH for s in range(2)]

    def key_copy(s, i):
        c = tab[jnp.minimum(lo[s] + i, spans - 1)]
        return pltpu.make_async_copy(
            kv_hbm.at[pl.ds(pl.multiple_of(c * SPAN, SPAN), SPAN)],
            kbuf.at[s, pl.ds(pl.multiple_of(i * SPAN, SPAN), SPAN)],
            ksem.at[s, i],
        )

    for s in range(2):

        @pl.loop(0, nch[s] * CH)
        def _(i):
            key_copy(s, i).start()

    zbuf[...] = jnp.zeros_like(zbuf)

    def zero_copy(i):
        return pltpu.make_async_copy(zbuf, dkv_hbm.at[pl.ds(i * zrows, zrows)], zsem.at[i])

    for i in range(zcount):
        zero_copy(i).start()

    for s in range(2):
        rows = slice(s * SPAN, (s + 1) * SPAN)
        for h in range(HEADS):
            cols = slice(h * HD, (h + 1) * HD)
            dst = slice(h * SPAN, (h + 1) * SPAN)
            qs[s, dst, :] = q_ref[rows, cols]
            gs[s, dst, :] = og_ref[rows, cols]
            prod = og_ref[rows, cols].astype(jnp.float32) * ao_ref[rows, cols].astype(jnp.float32)
            dqt[dst, :] = prod
        delta[s] = jnp.sum(dqt[...].T, axis=0, keepdims=True)
        qt[s] = qs[s].T
        gt[s] = gs[s].T

    for s in range(2):
        lse = lse_ref[pl.ds(s, 1), :]
        qpos = pos_ref[pl.ds(s, 1), :]
        qstart = start_ref[pl.ds(s, 1), :]

        def block(j, dq_acc):
            for i in range(CH):
                key_copy(s, j * CH + i).wait()
            first = pl.multiple_of(j * CH * SPAN, CH * SPAN)
            kc = kbuf[s, pl.ds(first, CH * SPAN), :HD]
            vc = kbuf[s, pl.ds(first, CH * SPAN), HD:]
            st = jnp.dot(kc, qt[s], preferred_element_type=jnp.float32)
            dp = jnp.dot(vc, gt[s], preferred_element_type=jnp.float32)
            kpos = (lo[s] + j * CH) * SPAN + lax.broadcasted_iota(jnp.int32, (CH * SPAN, NQ), 0)
            keep = (kpos >= qstart) & (kpos <= qpos)
            prob = jnp.exp(jnp.where(keep, st * scale - lse, -1e30))
            ds = (scale * prob * (dp - delta[s])).astype(jnp.bfloat16)
            pb = prob.astype(jnp.bfloat16)
            dk = jnp.dot(ds, qs[s], preferred_element_type=jnp.float32)
            dv = jnp.dot(pb, gs[s], preferred_element_type=jnp.float32)
            row0 = pl.multiple_of((lo[s] + j * CH) * SPAN, SPAN)
            at = pl.ds(row0, CH * SPAN)
            if s == 0:
                acc[at, :HD] = dk
                acc[at, HD:] = dv
            else:
                krow = row0 + lax.broadcasted_iota(jnp.int32, (CH * SPAN, HD), 0)
                seen = (krow >= lo[0] * SPAN) & (krow < end[0] * SPAN)
                acc[at, :HD] = dk + jnp.where(seen, acc[at, :HD], 0.0)
                acc[at, HD:] = dv + jnp.where(seen, acc[at, HD:], 0.0)
            return dq_acc + lax.dot_general(
                kc, ds, (((0,), (0,)), ((), ())), preferred_element_type=jnp.float32
            )

        total = lax.fori_loop(0, nch[s], block, jnp.zeros((HD, NQ), jnp.float32))
        dqt[...] = total.T
        for h in range(HEADS):
            dq_ref[s * SPAN : (s + 1) * SPAN, h * HD : (h + 1) * HD] = dqt[
                h * SPAN : (h + 1) * SPAN, :
            ].astype(dq_ref.dtype)

    for i in range(zcount):
        zero_copy(i).wait()

    def out_copy(s, i):
        c = tab[jnp.minimum(lo[s] + i, spans - 1)]
        return pltpu.make_async_copy(
            obuf.at[s, pl.ds(pl.multiple_of(i * SPAN, SPAN), SPAN)],
            dkv_hbm.at[pl.ds(pl.multiple_of(c * SPAN, SPAN), SPAN)],
            osem.at[s, i],
        )

    def mine(s, i):
        k = lo[s] + i
        if s == 1:
            return k < spans
        return (k < spans) & ((k < lo[1]) | (k >= end[1]))

    for s in range(2):

        @pl.loop(0, nch[s] * CH)
        def _(i):
            @pl.when(mine(s, i))
            def _():
                row = pl.multiple_of((lo[s] + i) * SPAN, SPAN)
                obuf[s, pl.ds(pl.multiple_of(i * SPAN, SPAN), SPAN), :] = acc[
                    pl.ds(row, SPAN), :
                ].astype(obuf.dtype)
                out_copy(s, i).start()

    for s in range(2):

        @pl.loop(0, nch[s] * CH)
        def _(i):
            @pl.when(mine(s, i))
            def _():
                out_copy(s, i).wait()


def window_grads(tab, q, og, ao, lse2, pos2, start2, kv_all):
    tokens = kv_all.shape[0]
    spans = tokens // SPAN
    wmax = MOST_DOC // SPAN + 1
    wmax = -(-wmax // CH) * CH
    vmem = pl.BlockSpec(memory_space=pltpu.VMEM)
    anyspace = pl.BlockSpec(memory_space=pl.ANY)
    zrows = 1024
    return pl.pallas_call(
        functools.partial(window_kernel, spans=spans, wmax=wmax),
        out_shape=(
            jax.ShapeDtypeStruct(q.shape, jnp.bfloat16),
            jax.ShapeDtypeStruct((tokens, 2 * HD), jnp.bfloat16),
        ),
        in_specs=[pl.BlockSpec(memory_space=pltpu.SMEM)] + [vmem] * 6 + [anyspace],
        out_specs=(vmem, anyspace),
        scratch_shapes=[
            pltpu.VMEM((2, wmax * SPAN, 2 * HD), jnp.bfloat16),
            pltpu.VMEM((tokens + CH * SPAN, 2 * HD), jnp.float32),
            pltpu.VMEM((2, wmax * SPAN, 2 * HD), jnp.bfloat16),
            pltpu.VMEM((zrows, 2 * HD), jnp.bfloat16),
            pltpu.VMEM((2, NQ, HD), jnp.bfloat16),
            pltpu.VMEM((2, NQ, HD), jnp.bfloat16),
            pltpu.VMEM((2, HD, NQ), jnp.bfloat16),
            pltpu.VMEM((2, HD, NQ), jnp.bfloat16),
            pltpu.VMEM((2, 1, NQ), jnp.float32),
            pltpu.VMEM((NQ, HD), jnp.float32),
            pltpu.SemaphoreType.DMA((2, wmax)),
            pltpu.SemaphoreType.DMA((tokens // zrows,)),
            pltpu.SemaphoreType.DMA((2, wmax)),
        ],
        name="window_grads",
    )(tab, q, og, ao, lse2, pos2, start2, kv_all)


def tables(my_index, log_sums, doc_ids, span_order):
    spans = span_order.shape[0]
    ids = jnp.arange(spans, dtype=jnp.int32)
    inner, outer = ids // 16, ids // 2 % 8
    x, z, core, y = outer // 4 * 2 + inner // 8, inner // 2 % 4, inner % 2, outer % 4
    kept_at = (((core * 4 + x) * 4 + z) * 4 + y) * 2 + ids % 2
    inverse = jnp.sum(jnp.where(span_order[None, :] == ids[:, None], kept_at[None, :], 0), axis=1)
    my_spans = lax.dynamic_slice_in_dim(span_order, 2 * my_index, 2)
    docs = jnp.arange(1, 16, dtype=jnp.int32)
    doc_start = jnp.sum((doc_ids[None, :] < docs[:, None]).astype(jnp.int32), axis=1)
    pos = my_spans[:, None] * SPAN + jnp.arange(SPAN, dtype=jnp.int32)[None, :]
    start = jnp.max(
        jnp.where(doc_start[:, None, None] <= pos[None], doc_start[:, None, None], 0), axis=0
    )
    low = start[:, 0] // SPAN
    tab = jnp.concatenate([inverse, my_spans, low]).astype(jnp.int32)
    pos2 = jnp.tile(pos, (1, HEADS))
    start2 = jnp.tile(start, (1, HEADS))
    lse2 = log_sums.reshape(HEADS, 2, SPAN).transpose(1, 0, 2).reshape(2, NQ)
    return tab, lse2, pos2, start2


ORDERS = (("x", "y", "z"), ("y", "z", "x"), ("z", "x", "y"))
COLS = 2 * HD
HALF = {1: pl.ds(0, HD), -1: pl.ds(HD, HD)}
FULL = pl.ds(0, COLS)


def here():
    i, o = lax.axis_index("inner"), lax.axis_index("outer")
    return {"x": (o // 4) * 2 + i // 8, "y": o % 4, "z": (i // 2) % 4, "core": i % 2}


def device(c):
    return ((c["x"] % 2) * 8 + c["z"] * 2 + c["core"], (c["x"] // 2) * 4 + c["y"])


def moved(c, axis, by):
    out = dict(c)
    out[axis] = (c[axis] + by + 4) % 4
    return out


def place(sel, core=None):
    where = tuple(slice(None) if sel[a] is None else sel[a] for a in "xzy")
    return where if core is None else (core, *where)


def row_parts(rows):
    first = -(-rows // 3 // 16) * 16
    sizes = (first, first, rows - 2 * first)
    return [(sum(sizes[:i]), sizes[i]) for i in range(3)]


class Copies:
    def __init__(self, send_sem, recv_sem):
        self.send_sem, self.recv_sem, self.all = send_sem, recv_sem, []

    def send(self, src, dst, target):
        k = len(self.all)
        copy = pltpu.make_async_remote_copy(
            src_ref=src,
            dst_ref=dst,
            send_sem=self.send_sem.at[k],
            recv_sem=self.recv_sem.at[k],
            device_id=device(target),
            device_id_type=pl.DeviceIdType.MESH,
        )
        copy.start()
        self.all.append(copy)
        return copy

    def drain(self):
        for copy in self.all:
            copy.wait_send()


def meet(me):
    barrier = pltpu.get_barrier_semaphore()
    partner = dict(me, core=1 - me["core"])
    others = [moved(me, a, d) for a in "xyz" for d in (1, -1)] + [partner]
    for other in others:
        pl.semaphore_signal(
            barrier, inc=1, device_id=device(other), device_id_type=pl.DeviceIdType.MESH
        )
    pl.semaphore_wait(barrier, len(others))
    return partner


GATHER_COPIES = 3 * 40


def gather_kernel(kv_ref, out, send_sem, recv_sem, own_sem):
    me = here()
    core = me["core"]
    own = pltpu.make_async_copy(kv_ref, out.at[place(me, core)], own_sem)
    own.start()
    partner = meet(me)
    net = Copies(send_sem, recv_sem)
    parts = row_parts(kv_ref.shape[0])

    def block(part, sel, cols=FULL):
        return out.at[(*place(sel, core), pl.ds(*parts[part]), cols)]

    def push(part, sel, axis, by, cols=FULL, src=None):
        ref = block(part, sel, cols)
        return net.send(ref if src is None else src, ref, moved(me, axis, by))

    across = []

    def cross(part, sel):
        ref = block(part, sel)
        across.append(net.send(ref, ref, partner))

    def both(part, sel, axis):
        return {d: push(part, sel, axis, d) for d in (1, -1)}

    def relay(part, sel, axis, copies, keep=True):
        out_copies = {}
        for d in (1, -1):
            copies[d].wait_recv()
            got = dict(sel, **{axis: moved(me, axis, -d)[axis]})
            out_copies[d] = push(part, got, axis, d, HALF[d])
            if keep:
                cross(part, got)
        return out_copies

    def settle(copies):
        for d in (1, -1):
            copies[d].wait_recv()

    colors = range(3)
    mine = {a: me[a] for a in "xyz"}
    first = [
        {
            d: push(i, mine, ORDERS[i][0], d, src=kv_ref.at[pl.ds(*parts[i]), :])
            for d in (1, -1)
        }
        for i in colors
    ]
    second = [relay(i, mine, ORDERS[i][0], first[i], keep=False) for i in colors]
    own.wait()
    line = [dict(mine, **{ORDERS[i][0]: None}) for i in colors]
    plane = []
    wave = [{} for i in colors]

    def piece(i, by):
        return dict(line[i], **{ORDERS[i][1]: moved(me, ORDERS[i][1], by)[ORDERS[i][1]]})

    for i in colors:
        settle(second[i])
        plane.append(both(i, line[i], ORDERS[i][1]))
        wave[i][0] = both(i, piece(i, 0), ORDERS[i][2])
        cross(i, line[i])
    turn = []
    for i in colors:
        turn.append(relay(i, line[i], ORDERS[i][1], plane[i]))
        for by in (1, -1):
            wave[i][by] = both(i, piece(i, by), ORDERS[i][2])
    last = [{} for i in colors]
    for i in colors:
        last[i][0] = relay(i, piece(i, 0), ORDERS[i][2], wave[i][0])
    for i in colors:
        settle(turn[i])
        wave[i][2] = both(i, piece(i, 2), ORDERS[i][2])
        cross(i, piece(i, 2))
    for by in (1, -1, 2):
        for i in colors:
            last[i][by] = relay(i, piece(i, by), ORDERS[i][2], wave[i][by])
    for by in (0, 1, -1, 2):
        for i in colors:
            settle(last[i][by])
            a3 = ORDERS[i][2]
            cross(i, dict(piece(i, by), **{a3: moved(me, a3, 2)[a3]}))
    for copy in across:
        copy.wait_recv()
    net.drain()


def gather_keys(keys_values):
    rows = keys_values.shape[0]
    out = pl.pallas_call(
        gather_kernel,
        out_shape=jax.ShapeDtypeStruct((2, 4, 4, 4, rows, COLS), keys_values.dtype),
        in_specs=[pl.BlockSpec(memory_space=pltpu.VMEM)],
        out_specs=pl.BlockSpec(memory_space=pl.ANY),
        scratch_shapes=[
            pltpu.SemaphoreType.DMA((GATHER_COPIES,)),
            pltpu.SemaphoreType.DMA((GATHER_COPIES,)),
            pltpu.SemaphoreType.DMA,
        ],
        compiler_params=pltpu.CompilerParams(collective_id=0, has_side_effects=True),
        name="gather_keys",
    )(keys_values)
    return out.reshape(128 * rows, COLS)


class Scatter:
    STEPS = 4 * 2 + 4

    def __init__(self, me, net, mine, other, near, far, near2, far2, near1, far1, rows):
        self.me, self.net, self.mine, self.other = me, net, mine, other
        self.buffers = {3: (near, far), 2: (near2, far2), 1: (near1, far1)}
        self.parts = row_parts(rows)
        self.spot = {a: me[a] for a in "xyz"}
        self.flight = {}

    def at(self, i, d1, d2, d3):
        a1, a2, a3 = ORDERS[i]
        sel = dict(self.spot)
        for a, d in ((a1, d1), (a2, d2), (a3, d3)):
            sel[a] = None if d is None else moved(self.me, a, d)[a]
        return sel

    def ref(self, buf, i, sel, cols=FULL):
        return buf.at[(*place(sel), pl.ds(*self.parts[i]), cols)]

    def line(self, i, d2, d3):
        a1 = ORDERS[i][0]
        for v in range(4):
            yield v, dict(self.at(i, 0, d2, d3), **{a1: v})

    def add_core(self, i, d2, d3):
        for _, sel in self.line(i, d2, d3):
            ix = (*place(sel), pl.ds(*self.parts[i]), FULL)
            self.mine[ix] = self.mine[ix] + self.other[ix]

    def slot(self, level, i, key, kind, d):
        near, far = self.buffers[level]
        n = self.parts[i][1]
        side = 0 if d == 1 else 1
        lead = (i, key, side) if level == 3 else (i, side)
        if level == 1:
            tail = (pl.ds(0, n), slice(None))
        else:
            tail = (slice(None), pl.ds(0, n), slice(None))
        return (near if kind == 0 else far).at[(*lead, *tail)], (near if kind == 0 else far), lead

    def level_sel(self, level, i, key, d):
        if level == 3:
            return self.at(i, None, key, d)
        if level == 2:
            return self.at(i, None, d, 0)
        return self.at(i, d, 0, 0)

    def blocks(self, level, i, key, d):
        if level == 3:
            return list(self.line(i, key, d))
        if level == 2:
            return list(self.line(i, d, 0))
        return [(None, self.at(i, d, 0, 0))]

    def start(self, level, i, key=0):
        axis = ORDERS[i][level - 1]
        sel = self.level_sel(level, i, key, 2)
        for d in (1, -1):
            dst, _, _ = self.slot(level, i, KEYS.index(key), 0, d)
            src = self.ref(self.mine, i, sel, HALF[d])
            self.flight[level, i, key, 0, d] = self.net.send(src, dst, moved(self.me, axis, d))

    def turn(self, level, i, key=0):
        axis = ORDERS[i][level - 1]
        n = self.parts[i][1]
        for d in (1, -1):
            self.flight[level, i, key, 0, d].wait_recv()
            _, buf, lead = self.slot(level, i, KEYS.index(key), 0, d)
            for v, sel in self.blocks(level, i, key, d):
                ix = (*place(sel), pl.ds(*self.parts[i]), HALF[d])
                row = (*lead, pl.ds(0, n), slice(None)) if v is None else (*lead, v, pl.ds(0, n), slice(None))
                self.mine[ix] = self.mine[ix] + buf[row]
            dst, _, _ = self.slot(level, i, KEYS.index(key), 1, d)
            src = self.ref(self.mine, i, self.level_sel(level, i, key, d))
            self.flight[level, i, key, 1, d] = self.net.send(src, dst, moved(self.me, axis, d))

    def close(self, level, i, key=0, write=None):
        n = self.parts[i][1]
        for d in (1, -1):
            self.flight[level, i, key, 1, d].wait_recv()
        for v, sel in self.blocks(level, i, key, 0):
            ix = (*place(sel), pl.ds(*self.parts[i]), FULL)
            total = self.mine[ix].astype(jnp.float32)
            if level == 3:
                total = total + self.other[ix].astype(jnp.float32)
            for d in (1, -1):
                _, buf, lead = self.slot(level, i, KEYS.index(key), 1, d)
                row = (*lead, pl.ds(0, n), slice(None)) if v is None else (*lead, v, pl.ds(0, n), slice(None))
                total = total + buf[row].astype(jnp.float32)
            if write is not None:
                write(self.parts[i], total)
            else:
                self.mine[ix] = total.astype(self.mine.dtype)

    def run(self, ready, write):
        colors = range(3)
        for n, key in enumerate(KEYS):
            for i in colors:
                ready(i, key)
                self.add_core(i, key, 2)
                self.start(3, i, key)
                self.add_core(i, key, 1)
                self.add_core(i, key, -1)
            if n >= 1:
                for i in colors:
                    self.turn(3, i, KEYS[n - 1])
            if n >= 2:
                for i in colors:
                    self.close(3, i, KEYS[n - 2])
                    if n == 2:
                        self.start(2, i)
        for i in colors:
            self.turn(3, i, KEYS[3])
        for i in colors:
            self.close(3, i, KEYS[2])
            self.turn(2, i)
        for i in colors:
            self.close(3, i, KEYS[3])
        for i in colors:
            self.close(2, i)
            self.start(1, i)
        for i in colors:
            self.turn(1, i)
        for i in colors:
            self.close(1, i, write=write)


KEYS = (2, 1, -1, 0)
SCATTER_COPIES = 3 * (4 * 4 + 4 + 4)


def scatter_scratch(rows):
    top = row_parts(rows)[0][1]
    return [
        pltpu.VMEM((4, 4, 4, rows, COLS), jnp.bfloat16),
        pltpu.VMEM((4, 4, 4, rows, COLS), jnp.bfloat16),
        pltpu.VMEM((3, 4, 2, 4, top, HD), jnp.bfloat16),
        pltpu.VMEM((3, 4, 2, 4, top, COLS), jnp.bfloat16),
        pltpu.VMEM((3, 2, 4, top, HD), jnp.bfloat16),
        pltpu.VMEM((3, 2, 4, top, COLS), jnp.bfloat16),
        pltpu.VMEM((3, 2, top, HD), jnp.bfloat16),
        pltpu.VMEM((3, 2, top, COLS), jnp.bfloat16),
    ]


def scatter_kernel(part_ref, x_ref, kv_out, w_out, *scratch):
    kv_bufs, w_bufs, w_theirs = scratch[:8], scratch[8:16], scratch[16]
    send_sem, recv_sem, load_sem = scratch[17:]
    me = here()
    core = me["core"]
    rows, w_rows = kv_out.shape[0], w_out.shape[0]
    net = Copies(send_sem, recv_sem)
    job = Scatter(me, net, *kv_bufs, rows)
    loads, swaps = {}, {}
    for n, key in enumerate(KEYS):
        for i in range(3):
            sel = job.at(i, None, key, None)
            src = part_ref.at[(*place(sel, core), pl.ds(*job.parts[i]), FULL)]
            loads[i, key] = pltpu.make_async_copy(
                src, job.ref(job.mine, i, sel), load_sem.at[3 * n + i]
            )
            loads[i, key].start()
    partner = meet(me)
    for key in KEYS:
        for i in range(3):
            sel = job.at(i, None, key, None)
            src = part_ref.at[(*place(sel, 1 - core), pl.ds(*job.parts[i]), FULL)]
            swaps[i, key] = net.send(src, job.ref(job.other, i, sel), partner)

    def ready(i, key):
        loads[i, key].wait()
        swaps[i, key].wait_recv()

    def write(part, total):
        kv_out[pl.ds(*part), :] = total.astype(kv_out.dtype)

    job.run(ready, write)

    kv = kv_out[...]
    w_job = Scatter(me, net, *w_bufs, w_rows)
    wide = 8 * w_rows

    def product(buf, which):
        for xl in range(2):
            for z in range(4):
                col = pl.multiple_of((xl * 8 + z * 2 + which) * wide, 128)
                out = lax.dot_general(
                    x_ref[:, pl.ds(col, wide)],
                    kv,
                    (((0,), (0,)), ((), ())),
                    preferred_element_type=jnp.float32,
                ).astype(jnp.bfloat16)
                for xh in range(2):
                    for y in range(4):
                        at = (xh * 4 + y) * w_rows
                        buf[2 * xh + xl, z, y] = out[at : at + w_rows]

    product(w_theirs, 1 - core)
    swap = net.send(w_theirs, w_job.other, partner)
    product(w_job.mine, core)
    waited = []

    def w_ready(i, key):
        if not waited:
            swap.wait_recv()
            waited.append(1)

    def w_write(part, total):
        w_out[pl.ds(*part), :] = total

    w_job.run(w_ready, w_write)
    net.drain()


def scatter_grads(kv_part, layer_input):
    tokens, width = kv_part.shape[0], layer_input.shape[1]
    rows, w_rows = tokens // 128, width // 128
    vmem = pl.BlockSpec(memory_space=pltpu.VMEM)
    copies = 2 * SCATTER_COPIES + 13
    return pl.pallas_call(
        scatter_kernel,
        out_shape=(
            jax.ShapeDtypeStruct((rows, COLS), jnp.bfloat16),
            jax.ShapeDtypeStruct((w_rows, COLS), jnp.float32),
        ),
        in_specs=[pl.BlockSpec(memory_space=pl.ANY), vmem],
        out_specs=(vmem, vmem),
        scratch_shapes=scatter_scratch(rows)
        + scatter_scratch(w_rows)
        + [
            pltpu.VMEM((4, 4, 4, w_rows, COLS), jnp.bfloat16),
            pltpu.SemaphoreType.DMA((copies,)),
            pltpu.SemaphoreType.DMA((copies,)),
            pltpu.SemaphoreType.DMA((12,)),
        ],
        compiler_params=pltpu.CompilerParams(collective_id=1, has_side_effects=True),
        name="scatter_grads",
    )(kv_part.reshape(2, 4, 4, 4, rows, COLS), layer_input)


def per_device(
    layer_input, queries, keys_values, attn_out, out_grad, log_sums, doc_ids, span_order
):
    my_index = lax.axis_index(("inner", "outer"))
    kv_all = gather_keys(keys_values)
    tab, lse2, pos2, start2 = tables(my_index, log_sums, doc_ids, span_order)
    query_grad, kv_part = window_grads(
        tab, queries, out_grad, attn_out, lse2, pos2, start2, kv_all
    )
    kv_total, weight_grad = scatter_grads(kv_part, layer_input)
    return (query_grad, kv_total, weight_grad)


def solution(mesh):
    rows = P(("inner", "outer"), None)
    return jax.shard_map(
        per_device,
        mesh=mesh,
        in_specs=(rows, rows, rows, rows, rows, P(None, ("inner", "outer")), P(), P()),
        out_specs=(rows, rows, rows),
        check_vma=False,
    )
```

```python
import functools

import jax
import jax.numpy as jnp
from jax import lax
from jax.experimental import pallas as pl
from jax.experimental.pallas import tpu as pltpu
from jax.sharding import PartitionSpec as P

CH = 4
SPAN = 64
HD = 128
HEADS = 6
NQ = SPAN * HEADS
MOST_DOC = 2048


def window_kernel(
    tab,
    q_ref,
    og_ref,
    ao_ref,
    lse_ref,
    pos_ref,
    start_ref,
    kv_hbm,
    dq_ref,
    dkv_hbm,
    kbuf,
    acc,
    obuf,
    zbuf,
    qs,
    gs,
    qt,
    gt,
    delta,
    dqt,
    ksem,
    zsem,
    osem,
    *,
    spans,
    wmax,
):
    scale = HD ** (-0.5)
    base = spans
    zrows = zbuf.shape[0]
    zcount = dkv_hbm.shape[0] // zrows
    p = [tab[base + s] for s in range(2)]
    lo = [tab[base + 2 + s] for s in range(2)]
    nch = [(p[s] - lo[s] + CH) // CH for s in range(2)]
    end = [lo[s] + nch[s] * CH for s in range(2)]

    def key_copy(s, i):
        c = tab[jnp.minimum(lo[s] + i, spans - 1)]
        return pltpu.make_async_copy(
            kv_hbm.at[pl.ds(pl.multiple_of(c * SPAN, SPAN), SPAN)],
            kbuf.at[s, pl.ds(pl.multiple_of(i * SPAN, SPAN), SPAN)],
            ksem.at[s, i],
        )

    for s in range(2):

        @pl.loop(0, nch[s] * CH)
        def _(i):
            key_copy(s, i).start()

    zbuf[...] = jnp.zeros_like(zbuf)

    def zero_copy(i):
        return pltpu.make_async_copy(zbuf, dkv_hbm.at[pl.ds(i * zrows, zrows)], zsem.at[i])

    for i in range(zcount):
        zero_copy(i).start()

    for s in range(2):
        rows = slice(s * SPAN, (s + 1) * SPAN)
        for h in range(HEADS):
            cols = slice(h * HD, (h + 1) * HD)
            dst = slice(h * SPAN, (h + 1) * SPAN)
            qs[s, dst, :] = q_ref[rows, cols]
            gs[s, dst, :] = og_ref[rows, cols]
            prod = og_ref[rows, cols].astype(jnp.float32) * ao_ref[rows, cols].astype(jnp.float32)
            dqt[dst, :] = prod
        delta[s] = jnp.sum(dqt[...].T, axis=0, keepdims=True)
        qt[s] = qs[s].T
        gt[s] = gs[s].T

    for s in range(2):
        lse = lse_ref[pl.ds(s, 1), :]
        qpos = pos_ref[pl.ds(s, 1), :]
        qstart = start_ref[pl.ds(s, 1), :]

        def block(j, dq_acc):
            for i in range(CH):
                key_copy(s, j * CH + i).wait()
            first = pl.multiple_of(j * CH * SPAN, CH * SPAN)
            kc = kbuf[s, pl.ds(first, CH * SPAN), :HD]
            vc = kbuf[s, pl.ds(first, CH * SPAN), HD:]
            st = jnp.dot(kc, qt[s], preferred_element_type=jnp.float32)
            dp = jnp.dot(vc, gt[s], preferred_element_type=jnp.float32)
            kpos = (lo[s] + j * CH) * SPAN + lax.broadcasted_iota(jnp.int32, (CH * SPAN, NQ), 0)
            keep = (kpos >= qstart) & (kpos <= qpos)
            prob = jnp.exp(jnp.where(keep, st * scale - lse, -1e30))
            ds = (scale * prob * (dp - delta[s])).astype(jnp.bfloat16)
            pb = prob.astype(jnp.bfloat16)
            dk = jnp.dot(ds, qs[s], preferred_element_type=jnp.float32)
            dv = jnp.dot(pb, gs[s], preferred_element_type=jnp.float32)
            row0 = pl.multiple_of((lo[s] + j * CH) * SPAN, SPAN)
            at = pl.ds(row0, CH * SPAN)
            if s == 0:
                acc[at, :HD] = dk
                acc[at, HD:] = dv
            else:
                krow = row0 + lax.broadcasted_iota(jnp.int32, (CH * SPAN, HD), 0)
                seen = (krow >= lo[0] * SPAN) & (krow < end[0] * SPAN)
                acc[at, :HD] = dk + jnp.where(seen, acc[at, :HD], 0.0)
                acc[at, HD:] = dv + jnp.where(seen, acc[at, HD:], 0.0)
            return dq_acc + lax.dot_general(
                kc, ds, (((0,), (0,)), ((), ())), preferred_element_type=jnp.float32
            )

        total = lax.fori_loop(0, nch[s], block, jnp.zeros((HD, NQ), jnp.float32))
        dqt[...] = total.T
        for h in range(HEADS):
            dq_ref[s * SPAN : (s + 1) * SPAN, h * HD : (h + 1) * HD] = dqt[
                h * SPAN : (h + 1) * SPAN, :
            ].astype(dq_ref.dtype)

    for i in range(zcount):
        zero_copy(i).wait()

    def out_copy(s, i):
        c = tab[jnp.minimum(lo[s] + i, spans - 1)]
        return pltpu.make_async_copy(
            obuf.at[s, pl.ds(pl.multiple_of(i * SPAN, SPAN), SPAN)],
            dkv_hbm.at[pl.ds(pl.multiple_of(c * SPAN, SPAN), SPAN)],
            osem.at[s, i],
        )

    def mine(s, i):
        k = lo[s] + i
        if s == 1:
            return k < spans
        return (k < spans) & ((k < lo[1]) | (k >= end[1]))

    for s in range(2):

        @pl.loop(0, nch[s] * CH)
        def _(i):
            @pl.when(mine(s, i))
            def _():
                row = pl.multiple_of((lo[s] + i) * SPAN, SPAN)
                obuf[s, pl.ds(pl.multiple_of(i * SPAN, SPAN), SPAN), :] = acc[
                    pl.ds(row, SPAN), :
                ].astype(obuf.dtype)
                out_copy(s, i).start()

    for s in range(2):

        @pl.loop(0, nch[s] * CH)
        def _(i):
            @pl.when(mine(s, i))
            def _():
                out_copy(s, i).wait()


def window_grads(tab, q, og, ao, lse2, pos2, start2, kv_all):
    tokens = kv_all.shape[0]
    spans = tokens // SPAN
    wmax = MOST_DOC // SPAN + 1
    wmax = -(-wmax // CH) * CH
    vmem = pl.BlockSpec(memory_space=pltpu.VMEM)
    anyspace = pl.BlockSpec(memory_space=pl.ANY)
    zrows = 1024
    return pl.pallas_call(
        functools.partial(window_kernel, spans=spans, wmax=wmax),
        out_shape=(
            jax.ShapeDtypeStruct(q.shape, jnp.bfloat16),
            jax.ShapeDtypeStruct((tokens, 2 * HD), jnp.bfloat16),
        ),
        in_specs=[pl.BlockSpec(memory_space=pltpu.SMEM)] + [vmem] * 6 + [anyspace],
        out_specs=(vmem, anyspace),
        scratch_shapes=[
            pltpu.VMEM((2, wmax * SPAN, 2 * HD), jnp.bfloat16),
            pltpu.VMEM((tokens + CH * SPAN, 2 * HD), jnp.float32),
            pltpu.VMEM((2, wmax * SPAN, 2 * HD), jnp.bfloat16),
            pltpu.VMEM((zrows, 2 * HD), jnp.bfloat16),
            pltpu.VMEM((2, NQ, HD), jnp.bfloat16),
            pltpu.VMEM((2, NQ, HD), jnp.bfloat16),
            pltpu.VMEM((2, HD, NQ), jnp.bfloat16),
            pltpu.VMEM((2, HD, NQ), jnp.bfloat16),
            pltpu.VMEM((2, 1, NQ), jnp.float32),
            pltpu.VMEM((NQ, HD), jnp.float32),
            pltpu.SemaphoreType.DMA((2, wmax)),
            pltpu.SemaphoreType.DMA((tokens // zrows,)),
            pltpu.SemaphoreType.DMA((2, wmax)),
        ],
        name="window_grads",
    )(tab, q, og, ao, lse2, pos2, start2, kv_all)


def tables(my_index, log_sums, doc_ids, span_order):
    spans = span_order.shape[0]
    ids = jnp.arange(spans, dtype=jnp.int32)
    inner, outer = ids // 16, ids // 2 % 8
    x, z, core, y = outer // 4 * 2 + inner // 8, inner // 2 % 4, inner % 2, outer % 4
    kept_at = (((core * 4 + x) * 4 + z) * 4 + y) * 2 + ids % 2
    inverse = jnp.sum(jnp.where(span_order[None, :] == ids[:, None], kept_at[None, :], 0), axis=1)
    my_spans = lax.dynamic_slice_in_dim(span_order, 2 * my_index, 2)
    docs = jnp.arange(1, 16, dtype=jnp.int32)
    doc_start = jnp.sum((doc_ids[None, :] < docs[:, None]).astype(jnp.int32), axis=1)
    pos = my_spans[:, None] * SPAN + jnp.arange(SPAN, dtype=jnp.int32)[None, :]
    start = jnp.max(
        jnp.where(doc_start[:, None, None] <= pos[None], doc_start[:, None, None], 0), axis=0
    )
    low = start[:, 0] // SPAN
    tab = jnp.concatenate([inverse, my_spans, low]).astype(jnp.int32)
    pos2 = jnp.tile(pos, (1, HEADS))
    start2 = jnp.tile(start, (1, HEADS))
    lse2 = log_sums.reshape(HEADS, 2, SPAN).transpose(1, 0, 2).reshape(2, NQ)
    return tab, lse2, pos2, start2


ORDERS = (("x", "y", "z"), ("y", "z", "x"), ("z", "x", "y"))
COLS = 2 * HD
HALF = {1: pl.ds(0, HD), -1: pl.ds(HD, HD)}
FULL = pl.ds(0, COLS)


def here():
    i, o = lax.axis_index("inner"), lax.axis_index("outer")
    return {"x": (o // 4) * 2 + i // 8, "y": o % 4, "z": (i // 2) % 4, "core": i % 2}


def device(c):
    return ((c["x"] % 2) * 8 + c["z"] * 2 + c["core"], (c["x"] // 2) * 4 + c["y"])


def moved(c, axis, by):
    out = dict(c)
    out[axis] = (c[axis] + by + 4) % 4
    return out


def place(sel, core=None):
    where = tuple(slice(None) if sel[a] is None else sel[a] for a in "xzy")
    return where if core is None else (core, *where)


def row_parts(rows):
    first = -(-rows // 3 // 16) * 16
    sizes = (first, first, rows - 2 * first)
    return [(sum(sizes[:i]), sizes[i]) for i in range(3)]


class Copies:
    def __init__(self, send_sem, recv_sem):
        self.send_sem, self.recv_sem, self.all = send_sem, recv_sem, []

    def send(self, src, dst, target):
        k = len(self.all)
        copy = pltpu.make_async_remote_copy(
            src_ref=src,
            dst_ref=dst,
            send_sem=self.send_sem.at[k],
            recv_sem=self.recv_sem.at[k],
            device_id=device(target),
            device_id_type=pl.DeviceIdType.MESH,
        )
        copy.start()
        self.all.append(copy)
        return copy

    def drain(self):
        for copy in self.all:
            copy.wait_send()


def meet(me):
    barrier = pltpu.get_barrier_semaphore()
    partner = dict(me, core=1 - me["core"])
    others = [moved(me, a, d) for a in "xyz" for d in (1, -1, 2)] + [partner]
    for other in others:
        pl.semaphore_signal(
            barrier, inc=1, device_id=device(other), device_id_type=pl.DeviceIdType.MESH
        )
    pl.semaphore_wait(barrier, len(others))
    return partner


GATHER_COPIES = 3 * (3 + 3 + 16 + 16)


def gather_kernel(kv_ref, out, send_sem, recv_sem, own_sem, aside=lambda: None):
    me = here()
    core = me["core"]
    own = pltpu.make_async_copy(kv_ref, out.at[place(me, core)], own_sem)
    own.start()
    partner = meet(me)
    net = Copies(send_sem, recv_sem)
    parts = row_parts(kv_ref.shape[0])

    def block(part, sel, cols=FULL):
        return out.at[(*place(sel, core), pl.ds(*parts[part]), cols)]

    def push(part, sel, axis, by, cols=FULL, src=None):
        ref = block(part, sel, cols)
        return net.send(ref if src is None else src, ref, moved(me, axis, by))

    across = []

    def cross(part, sel):
        ref = block(part, sel)
        across.append(net.send(ref, ref, partner))

    def both(part, sel, axis):
        return {d: push(part, sel, axis, d) for d in (1, -1)}

    def relay(part, sel, axis, copies):
        out_copies = {}
        for d in (1, -1):
            copies[d].wait_recv()
            got = dict(sel, **{axis: moved(me, axis, -d)[axis]})
            out_copies[d] = push(part, got, axis, d, HALF[d])
            cross(part, got)
        return out_copies

    def settle(copies):
        for copy in copies.values():
            copy.wait_recv()

    colors = range(3)
    mine = {a: me[a] for a in "xyz"}
    first = [
        {
            d: push(i, mine, ORDERS[i][0], d, src=kv_ref.at[pl.ds(*parts[i]), :])
            for d in (2, 1, -1)
        }
        for i in colors
    ]
    aside()
    own.wait()
    line = [dict(mine, **{ORDERS[i][0]: None}) for i in colors]
    plane = []
    wave = [{} for i in colors]
    last = [{} for i in colors]

    def piece(i, by):
        return dict(line[i], **{ORDERS[i][1]: moved(me, ORDERS[i][1], by)[ORDERS[i][1]]})

    for i in colors:
        settle(first[i])
        plane.append({d: push(i, line[i], ORDERS[i][1], d) for d in (2, 1, -1)})
    for i in colors:
        wave[i][0] = both(i, piece(i, 0), ORDERS[i][2])
    for i in colors:
        cross(i, line[i])
    for by in (1, -1, 2):
        for i in colors:
            plane[i][by if by == 2 else -by].wait_recv()
            wave[i][by] = both(i, piece(i, by), ORDERS[i][2])
            cross(i, piece(i, by))
    for by in (0, 1, -1, 2):
        for i in colors:
            last[i][by] = relay(i, piece(i, by), ORDERS[i][2], wave[i][by])
    for by in (0, 1, -1, 2):
        for i in colors:
            settle(last[i][by])
            a3 = ORDERS[i][2]
            cross(i, dict(piece(i, by), **{a3: moved(me, a3, 2)[a3]}))
    for copy in across:
        copy.wait_recv()
    net.drain()


def gather_keys(keys_values):
    rows = keys_values.shape[0]
    out = pl.pallas_call(
        gather_kernel,
        out_shape=jax.ShapeDtypeStruct((2, 4, 4, 4, rows, COLS), keys_values.dtype),
        in_specs=[pl.BlockSpec(memory_space=pltpu.VMEM)],
        out_specs=pl.BlockSpec(memory_space=pl.ANY),
        scratch_shapes=[
            pltpu.SemaphoreType.DMA((GATHER_COPIES,)),
            pltpu.SemaphoreType.DMA((GATHER_COPIES,)),
            pltpu.SemaphoreType.DMA,
        ],
        compiler_params=pltpu.CompilerParams(collective_id=0, has_side_effects=True),
        name="gather_keys",
    )(keys_values)
    return out.reshape(128 * rows, COLS)


KEYS = (2, 1, -1, 0)
AWAY = (2, 1, -1)


class Scatter:
    def __init__(self, me, net, mine, other, halves, third, second, first, rows):
        self.me, self.net, self.mine, self.other, self.halves = me, net, mine, other, halves
        self.buffers = {3: third, 2: second, 1: first}
        self.parts = row_parts(rows)
        self.spot = {a: me[a] for a in "xyz"}
        self.flight = {}

    def at(self, i, d1, d2, d3):
        sel = dict(self.spot)
        for a, d in zip(ORDERS[i], (d1, d2, d3)):
            sel[a] = None if d is None else moved(self.me, a, d)[a]
        return sel

    def ix(self, i, sel, cols=FULL):
        return (*place(sel), pl.ds(*self.parts[i]), cols)

    def level_sel(self, level, i, key, d):
        return {3: self.at(i, None, key, d), 2: self.at(i, None, d, 0), 1: self.at(i, d, 0, 0)}[level]

    def blocks(self, level, i, key, d):
        sel = self.level_sel(level, i, key, d)
        if level == 1:
            return [((), sel)]
        return [((v,), dict(sel, **{ORDERS[i][0]: v})) for v in range(4)]

    def lead(self, level, i, key, d):
        side = AWAY.index(d) if self.halves is None or level < 3 else (0 if d == 1 else 1)
        return (i, KEYS.index(key), side) if level == 3 else (i, side)

    def slot(self, buf, level, i, key, d):
        lines = () if level == 1 else (slice(None),)
        return buf.at[(*self.lead(level, i, key, d), *lines, pl.ds(0, self.parts[i][1]), slice(None))]

    def row(self, level, i, key, d, v):
        return (*self.lead(level, i, key, d), *v, pl.ds(0, self.parts[i][1]), slice(None))

    def send(self, level, i, key, d):
        src = self.mine.at[self.ix(i, self.level_sel(level, i, key, d))]
        dst = self.slot(self.buffers[level], level, i, key, d)
        to = moved(self.me, ORDERS[i][level - 1], d)
        self.flight[level, i, key, d] = self.net.send(src, dst, to)

    def add_core(self, i, d2, d3):
        for _, sel in self.blocks(3, i, d2, d3):
            ix = self.ix(i, sel)
            self.mine[ix] = self.mine[ix] + self.other[ix]

    def open(self, i, key):
        if self.halves is None:
            for d in AWAY:
                self.send(3, i, key, d)
            return
        self.add_core(i, key, 2)
        sel = self.level_sel(3, i, key, 2)
        for d in (1, -1):
            dst = self.slot(self.halves, 3, i, key, d)
            src = self.mine.at[self.ix(i, sel, HALF[d])]
            to = moved(self.me, ORDERS[i][2], d)
            self.flight["half", i, key, d] = self.net.send(src, dst, to)
        self.add_core(i, key, 1)
        self.add_core(i, key, -1)

    def turn(self, i, key):
        for d in (1, -1):
            self.flight["half", i, key, d].wait_recv()
            for v, sel in self.blocks(3, i, key, d):
                ix = self.ix(i, sel, HALF[d])
                self.mine[ix] = self.mine[ix] + self.halves[self.row(3, i, key, d, v)]
            self.send(3, i, key, d)

    def close(self, level, i, key=0, write=None):
        sides = (1, -1) if level == 3 and self.halves is not None else AWAY
        for d in sides:
            self.flight[level, i, key, d].wait_recv()
        for v, sel in self.blocks(level, i, key, 0):
            ix = self.ix(i, sel)
            total = self.mine[ix].astype(jnp.float32)
            if level == 3 and self.other is not None:
                total = total + self.other[ix].astype(jnp.float32)
            for d in sides:
                total = total + self.buffers[level][self.row(level, i, key, d, v)].astype(jnp.float32)
            if write is None:
                self.mine[ix] = total.astype(self.mine.dtype)
            else:
                write(self.parts[i], total)

    def finish(self, i, key):
        self.close(3, i, key)
        if key != 0:
            self.send(2, i, 0, key)

    def run(self, ready, write, aside):
        colors = range(3)
        lag = 1 if self.halves is None else 2
        for n in range(len(KEYS) + lag):
            if n < len(KEYS):
                for i in colors:
                    ready(i, KEYS[n])
                    self.open(i, KEYS[n])
            if lag == 2 and 1 <= n <= len(KEYS):
                for i in colors:
                    self.turn(i, KEYS[n - 1])
            if n == len(KEYS) - 1:
                aside()
            if n >= lag:
                for i in colors:
                    self.finish(i, KEYS[n - lag])
        for i in colors:
            self.close(2, i)
            for d in AWAY:
                self.send(1, i, 0, d)
        for i in colors:
            self.close(1, i, write=write)


def scatter_scratch(rows, relayed):
    top = row_parts(rows)[0][1]
    plane = pltpu.VMEM((4, 4, 4, rows, COLS), jnp.bfloat16)
    return ([plane, plane, pltpu.VMEM((3, 4, 2, 4, top, HD), jnp.bfloat16)] if relayed else [plane]) + [
        pltpu.VMEM((3, 4, 2 if relayed else 3, 4, top, COLS), jnp.bfloat16),
        pltpu.VMEM((3, 3, 4, top, COLS), jnp.bfloat16),
        pltpu.VMEM((3, 3, top, COLS), jnp.bfloat16),
    ]


SCATTER_COPIES = 3 * (4 * 4 + 3 + 3) + 3 * (4 * 3 + 3 + 3) + 12 + 8 + 1


def scatter_kernel(part_ref, x_ref, kv_out, w_out, *scratch):
    kv_bufs, w_bufs = scratch[:6], scratch[6:10]
    x_theirs, xt, pair, send_sem, recv_sem, load_sem = scratch[10:]
    me = here()
    core = me["core"]
    rows, w_rows = kv_out.shape[0], w_out.shape[0]
    wide = 8 * w_rows
    net = Copies(send_sem, recv_sem)
    job = Scatter(me, net, *kv_bufs, rows)
    w_job = Scatter(me, net, w_bufs[0], None, None, *w_bufs[1:], w_rows)
    loads, swaps = {}, {}
    for n, key in enumerate(KEYS):
        for i in range(3):
            sel = job.at(i, None, key, None)
            src = part_ref.at[(*place(sel, core), pl.ds(*job.parts[i]), FULL)]
            dst = job.mine.at[job.ix(i, sel)]
            loads[i, key] = pltpu.make_async_copy(src, dst, load_sem.at[3 * n + i])
            loads[i, key].start()
    partner = meet(me)
    for key in KEYS:
        for i in range(3):
            sel = job.at(i, None, key, None)
            src = part_ref.at[(*place(sel, 1 - core), pl.ds(*job.parts[i]), FULL)]
            swaps[i, key] = net.send(src, job.other.at[job.ix(i, sel)], partner)

    def columns(j, which):
        first = (j // 4 * 8 + j % 4 * 2 + which) * wide
        return x_ref.at[:, pl.ds(pl.multiple_of(first, 128), wide)]

    x_swaps = [net.send(columns(j, 1 - core), x_theirs.at[j], partner) for j in range(8)]
    for j in range(8):
        xt[j, :, :rows] = columns(j, core)[...].T

    def ready(i, key):
        loads[i, key].wait()
        swaps[i, key].wait_recv()

    def turn_inputs():
        for j in range(8):
            x_swaps[j].wait_recv()
            xt[j, :, rows:] = x_theirs[j].T

    def write(part, total):
        low = total.astype(kv_out.dtype)
        kv_out[pl.ds(*part), :] = low
        pair[pl.ds(*part), :] = low

    job.run(ready, write, turn_inputs)

    swap = net.send(pair.at[pl.ds(0, rows)], pair.at[pl.ds(rows, rows)], partner)
    swap.wait_recv()
    both = pair[...]
    for j in range(8):
        out = jnp.dot(xt[j], both, preferred_element_type=jnp.float32).astype(jnp.bfloat16)
        for xh in range(2):
            for y in range(4):
                first = (xh * 4 + y) * w_rows
                w_job.mine[2 * xh + j // 4, j % 4, y] = out[first : first + w_rows]

    def w_write(part, total):
        w_out[pl.ds(*part), :] = total

    w_job.run(lambda i, key: None, w_write, lambda: None)
    net.drain()


def scatter_grads(kv_part, layer_input):
    tokens, width = kv_part.shape[0], layer_input.shape[1]
    rows, w_rows = tokens // 128, width // 128
    vmem = pl.BlockSpec(memory_space=pltpu.VMEM)
    return pl.pallas_call(
        scatter_kernel,
        out_shape=(
            jax.ShapeDtypeStruct((rows, COLS), jnp.bfloat16),
            jax.ShapeDtypeStruct((w_rows, COLS), jnp.float32),
        ),
        in_specs=[pl.BlockSpec(memory_space=pl.ANY), vmem],
        out_specs=(vmem, vmem),
        scratch_shapes=scatter_scratch(rows, True)
        + scatter_scratch(w_rows, False)
        + [
            pltpu.VMEM((8, rows, 8 * w_rows), jnp.bfloat16),
            pltpu.VMEM((8, 8 * w_rows, 2 * rows), jnp.bfloat16),
            pltpu.VMEM((2 * rows, COLS), jnp.bfloat16),
            pltpu.SemaphoreType.DMA((SCATTER_COPIES,)),
            pltpu.SemaphoreType.DMA((SCATTER_COPIES,)),
            pltpu.SemaphoreType.DMA((12,)),
        ],
        compiler_params=pltpu.CompilerParams(collective_id=1, has_side_effects=True),
        name="scatter_grads",
    )(kv_part.reshape(2, 4, 4, 4, rows, COLS), layer_input)


def per_device(
    layer_input, queries, keys_values, attn_out, out_grad, log_sums, doc_ids, span_order
):
    my_index = lax.axis_index(("inner", "outer"))
    kv_all = gather_keys(keys_values)
    tab, lse2, pos2, start2 = tables(my_index, log_sums, doc_ids, span_order)
    query_grad, kv_part = window_grads(
        tab, queries, out_grad, attn_out, lse2, pos2, start2, kv_all
    )
    kv_total, weight_grad = scatter_grads(kv_part, layer_input)
    return (query_grad, kv_total, weight_grad)


def solution(mesh):
    rows = P(("inner", "outer"), None)
    return jax.shard_map(
        per_device,
        mesh=mesh,
        in_specs=(rows, rows, rows, rows, rows, P(None, ("inner", "outer")), P(), P()),
        out_specs=(rows, rows, rows),
        check_vma=False,
    )
```

```python
import functools

import jax
import jax.numpy as jnp
from jax import lax
from jax.experimental import pallas as pl
from jax.experimental.pallas import tpu as pltpu
from jax.sharding import PartitionSpec as P

CH = 4
SPAN = 64
HD = 128
HEADS = 6
NQ = SPAN * HEADS
MOST_DOC = 2048


def window_kernel(
    tab,
    meta,
    fmeta,
    qs,
    gs,
    qt,
    gt,
    kv_hbm,
    dq_ref,
    dkv_hbm,
    kbuf,
    acc,
    obuf,
    zbuf,
    dqt,
    ksem,
    zsem,
    osem,
    *,
    spans,
):
    scale = HD ** (-0.5)
    zrows = zbuf.shape[0]
    zcount = dkv_hbm.shape[0] // zrows
    p = [tab[0, spans + s] for s in range(2)]
    lo = [tab[0, spans + 2 + s] for s in range(2)]
    nch = [(p[s] - lo[s] + CH) // CH for s in range(2)]
    end = [lo[s] + nch[s] * CH for s in range(2)]

    def key_copy(s, i):
        c = tab[0, jnp.minimum(lo[s] + i, spans - 1)]
        return pltpu.make_async_copy(
            kv_hbm.at[pl.ds(pl.multiple_of(c * SPAN, SPAN), SPAN)],
            kbuf.at[s, pl.ds(pl.multiple_of(i * SPAN, SPAN), SPAN)],
            ksem.at[s, i],
        )

    for s in range(2):

        @pl.loop(0, nch[s] * CH)
        def _(i):
            key_copy(s, i).start()

    zbuf[...] = jnp.zeros_like(zbuf)

    def zero_copy(i):
        return pltpu.make_async_copy(zbuf, dkv_hbm.at[pl.ds(i * zrows, zrows)], zsem.at[i])

    for i in range(zcount):
        zero_copy(i).start()

    lane = lax.broadcasted_iota(jnp.int32, (1, NQ), 1)
    for s in range(2):
        delta = fmeta[pl.ds(s, 1), :]
        lse = fmeta[pl.ds(2 + s, 1), :]
        qpos = p[s] * SPAN + (lane & (SPAN - 1))
        qstart = meta[pl.ds(1 + s, 1), pl.ds(0, NQ)]

        def block(j, dq_acc):
            for i in range(CH):
                key_copy(s, j * CH + i).wait()
            first = pl.multiple_of(j * CH * SPAN, CH * SPAN)
            kc = kbuf[s, pl.ds(first, CH * SPAN), :HD]
            vc = kbuf[s, pl.ds(first, CH * SPAN), HD:]
            st = jnp.dot(kc, qt[s], preferred_element_type=jnp.float32)
            dp = jnp.dot(vc, gt[s], preferred_element_type=jnp.float32)
            kpos = (lo[s] + j * CH) * SPAN + lax.broadcasted_iota(jnp.int32, (CH * SPAN, NQ), 0)
            keep = (kpos >= qstart) & (kpos <= qpos)
            prob = jnp.exp(jnp.where(keep, st * scale - lse, -1e30))
            ds = (scale * prob * (dp - delta)).astype(jnp.bfloat16)
            pb = prob.astype(jnp.bfloat16)
            dk = jnp.dot(ds, qs[s], preferred_element_type=jnp.float32)
            dv = jnp.dot(pb, gs[s], preferred_element_type=jnp.float32)
            row0 = pl.multiple_of((lo[s] + j * CH) * SPAN, SPAN)
            at = pl.ds(row0, CH * SPAN)
            if s == 0:
                acc[at, :HD] = dk
                acc[at, HD:] = dv
            else:
                krow = row0 + lax.broadcasted_iota(jnp.int32, (CH * SPAN, HD), 0)
                seen = (krow >= lo[0] * SPAN) & (krow < end[0] * SPAN)
                acc[at, :HD] = dk + jnp.where(seen, acc[at, :HD], 0.0)
                acc[at, HD:] = dv + jnp.where(seen, acc[at, HD:], 0.0)
            return dq_acc + lax.dot_general(
                kc, ds, (((0,), (0,)), ((), ())), preferred_element_type=jnp.float32
            )

        total = lax.fori_loop(0, nch[s], block, jnp.zeros((HD, NQ), jnp.float32))
        dqt[...] = total.T
        for h in range(HEADS):
            dq_ref[s * SPAN : (s + 1) * SPAN, h * HD : (h + 1) * HD] = dqt[
                h * SPAN : (h + 1) * SPAN, :
            ].astype(dq_ref.dtype)

    for i in range(zcount):
        zero_copy(i).wait()

    def out_copy(s, i):
        c = tab[0, jnp.minimum(lo[s] + i, spans - 1)]
        return pltpu.make_async_copy(
            obuf.at[s, pl.ds(pl.multiple_of(i * SPAN, SPAN), SPAN)],
            dkv_hbm.at[pl.ds(pl.multiple_of(c * SPAN, SPAN), SPAN)],
            osem.at[s, i],
        )

    def mine(s, i):
        k = lo[s] + i
        if s == 1:
            return k < spans
        return (k < spans) & ((k < lo[1]) | (k >= end[1]))

    for s in range(2):

        @pl.loop(0, nch[s] * CH)
        def _(i):
            @pl.when(mine(s, i))
            def _():
                row = pl.multiple_of((lo[s] + i) * SPAN, SPAN)
                obuf[s, pl.ds(pl.multiple_of(i * SPAN, SPAN), SPAN), :] = acc[
                    pl.ds(row, SPAN), :
                ].astype(obuf.dtype)
                out_copy(s, i).start()

    for s in range(2):

        @pl.loop(0, nch[s] * CH)
        def _(i):
            @pl.when(mine(s, i))
            def _():
                out_copy(s, i).wait()


def window_grads(meta, fmeta, qs, gs, qt, gt, kv_all):
    tokens = kv_all.shape[0]
    spans = tokens // SPAN
    wmax = MOST_DOC // SPAN + 1
    wmax = -(-wmax // CH) * CH
    vmem = pl.BlockSpec(memory_space=pltpu.VMEM)
    anyspace = pl.BlockSpec(memory_space=pl.ANY)
    zrows = 1024
    return pl.pallas_call(
        functools.partial(window_kernel, spans=spans),
        out_shape=(
            jax.ShapeDtypeStruct((2 * SPAN, HEADS * HD), jnp.bfloat16),
            jax.ShapeDtypeStruct((tokens, 2 * HD), jnp.bfloat16),
        ),
        in_specs=[pl.BlockSpec(memory_space=pltpu.SMEM)] + [vmem] * 6 + [anyspace],
        out_specs=(vmem, anyspace),
        scratch_shapes=[
            pltpu.VMEM((2, wmax * SPAN, 2 * HD), jnp.bfloat16),
            pltpu.VMEM((tokens + CH * SPAN, 2 * HD), jnp.float32),
            pltpu.VMEM((2, wmax * SPAN, 2 * HD), jnp.bfloat16),
            pltpu.VMEM((zrows, 2 * HD), jnp.bfloat16),
            pltpu.VMEM((NQ, HD), jnp.float32),
            pltpu.SemaphoreType.DMA((2, wmax)),
            pltpu.SemaphoreType.DMA((tokens // zrows,)),
            pltpu.SemaphoreType.DMA((2, wmax)),
        ],
        name="window_grads",
    )(meta, meta, fmeta, qs, gs, qt, gt, kv_all)


def prepare(q_ref, og_ref, ao_ref, lse_ref, doc_ref, order_ref, qs, gs, qt, gt, meta, fmeta, tmp):
    spans = order_ref.shape[0] * order_ref.shape[1]
    order = jnp.concatenate([order_ref[0:1, :], order_ref[1:2, :]], axis=1).astype(jnp.float32)
    stored = jnp.broadcast_to(order, (spans, spans)).T
    lanes = lax.broadcasted_iota(jnp.int32, (spans, spans), 1).astype(jnp.float32)
    c = lax.broadcasted_iota(jnp.int32, (spans, spans), 0)
    kept = (
        ((c >> 4) & 1) * 128
        + (((c >> 3) & 1) * 2 + ((c >> 7) & 1)) * 32
        + ((c >> 5) & 3) * 8
        + ((c >> 1) & 3) * 2
        + (c & 1)
    ).astype(jnp.float32)
    inverse = jnp.sum(jnp.where(stored == lanes, kept, 0.0), axis=0, keepdims=True)
    docs = doc_ref[...]
    counts = [
        jnp.sum(jnp.where(docs < d, 1.0, 0.0), axis=0, keepdims=True) for d in range(16)
    ]
    first = jnp.sum(jnp.concatenate(counts, axis=0), axis=1, keepdims=True)
    mine = 2 * (lax.axis_index("inner") * 8 + lax.axis_index("outer"))
    spot = lax.broadcasted_iota(jnp.int32, (1, spans), 1)
    lane = lax.broadcasted_iota(jnp.int32, (1, NQ), 1)
    tail = jnp.zeros((1, spans), jnp.float32)
    for s in range(2):
        span = jnp.sum(jnp.where(spot == mine + s, order, 0.0), axis=1, keepdims=True)
        pos = span * SPAN + (lane & (SPAN - 1)).astype(jnp.float32)
        start = jnp.max(jnp.where(first <= pos, first, 0.0), axis=0, keepdims=True)
        low = (start[:, :1].astype(jnp.int32) >> 6).astype(jnp.float32)
        tail = jnp.where(spot == s, span, jnp.where(spot == 2 + s, low, tail))
        meta[1 + s : 2 + s, 0:NQ] = start.astype(jnp.int32)
    meta[0:1, 0:spans] = inverse.astype(jnp.int32)
    meta[0:1, spans:] = tail.astype(jnp.int32)
    for s in range(2):
        rows = slice(s * SPAN, (s + 1) * SPAN)
        for h in range(HEADS):
            cols = slice(h * HD, (h + 1) * HD)
            dst = slice(h * SPAN, (h + 1) * SPAN)
            qs[s, dst, :] = q_ref[rows, cols]
            gs[s, dst, :] = og_ref[rows, cols]
            tmp[dst, :] = og_ref[rows, cols].astype(jnp.float32) * ao_ref[rows, cols].astype(
                jnp.float32
            )
        fmeta[s : s + 1, :] = jnp.sum(tmp[...].T, axis=0, keepdims=True)
        fmeta[2 + s : 3 + s, :] = jnp.concatenate(
            [lse_ref[h : h + 1, rows] for h in range(HEADS)], axis=1
        )
        qt[s] = qs[s].T
        gt[s] = gs[s].T


ORDERS = (("x", "y", "z"), ("y", "z", "x"), ("z", "x", "y"))
COLS = 2 * HD
HALF = {1: pl.ds(0, HD), -1: pl.ds(HD, HD)}
FULL = pl.ds(0, COLS)


def here():
    i, o = lax.axis_index("inner"), lax.axis_index("outer")
    return {"x": (o // 4) * 2 + i // 8, "y": o % 4, "z": (i // 2) % 4, "core": i % 2}


def device(c):
    return ((c["x"] % 2) * 8 + c["z"] * 2 + c["core"], (c["x"] // 2) * 4 + c["y"])


def moved(c, axis, by):
    out = dict(c)
    out[axis] = (c[axis] + by + 4) % 4
    return out


def place(sel, core=None):
    where = tuple(slice(None) if sel[a] is None else sel[a] for a in "xzy")
    return where if core is None else (core, *where)


def row_parts(rows):
    first = -(-rows // 3 // 16) * 16
    sizes = (first, first, rows - 2 * first)
    return [(sum(sizes[:i]), sizes[i]) for i in range(3)]


class Copies:
    def __init__(self, send_sem, recv_sem):
        self.send_sem, self.recv_sem, self.all = send_sem, recv_sem, []

    def send(self, src, dst, target):
        k = len(self.all)
        copy = pltpu.make_async_remote_copy(
            src_ref=src,
            dst_ref=dst,
            send_sem=self.send_sem.at[k],
            recv_sem=self.recv_sem.at[k],
            device_id=device(target),
            device_id_type=pl.DeviceIdType.MESH,
        )
        copy.start()
        self.all.append(copy)
        return copy

    def drain(self):
        for copy in self.all:
            copy.wait_send()


def meet(me):
    barrier = pltpu.get_barrier_semaphore()
    partner = dict(me, core=1 - me["core"])
    others = [moved(me, a, d) for a in "xyz" for d in (1, -1, 2)] + [partner]
    for other in others:
        pl.semaphore_signal(
            barrier, inc=1, device_id=device(other), device_id_type=pl.DeviceIdType.MESH
        )
    pl.semaphore_wait(barrier, len(others))
    return partner


GATHER_COPIES = 3 * (3 + 3 + 16 + 16)


def gather_kernel(kv_ref, *refs):
    *small, out, tmp, send_sem, recv_sem, own_sem = refs
    me = here()
    core = me["core"]
    own = pltpu.make_async_copy(kv_ref, out.at[place(me, core)], own_sem)
    own.start()
    partner = meet(me)
    net = Copies(send_sem, recv_sem)
    parts = row_parts(kv_ref.shape[0])

    def block(part, sel, cols=FULL):
        return out.at[(*place(sel, core), pl.ds(*parts[part]), cols)]

    def push(part, sel, axis, by, cols=FULL, src=None):
        ref = block(part, sel, cols)
        return net.send(ref if src is None else src, ref, moved(me, axis, by))

    across = []

    def cross(part, sel):
        ref = block(part, sel)
        across.append(net.send(ref, ref, partner))

    def both(part, sel, axis):
        return {d: push(part, sel, axis, d) for d in (1, -1)}

    def relay(part, sel, axis, copies):
        out_copies = {}
        for d in (1, -1):
            copies[d].wait_recv()
            got = dict(sel, **{axis: moved(me, axis, -d)[axis]})
            out_copies[d] = push(part, got, axis, d, HALF[d])
            cross(part, got)
        return out_copies

    def settle(copies):
        for copy in copies.values():
            copy.wait_recv()

    colors = range(3)
    mine = {a: me[a] for a in "xyz"}
    first = [
        {
            d: push(i, mine, ORDERS[i][0], d, src=kv_ref.at[pl.ds(*parts[i]), :])
            for d in (2, 1, -1)
        }
        for i in colors
    ]
    prepare(*small, tmp)
    own.wait()
    line = [dict(mine, **{ORDERS[i][0]: None}) for i in colors]
    plane = []
    wave = [{} for i in colors]
    last = [{} for i in colors]

    def piece(i, by):
        return dict(line[i], **{ORDERS[i][1]: moved(me, ORDERS[i][1], by)[ORDERS[i][1]]})

    for i in colors:
        settle(first[i])
        plane.append({d: push(i, line[i], ORDERS[i][1], d) for d in (2, 1, -1)})
    for i in colors:
        wave[i][0] = both(i, piece(i, 0), ORDERS[i][2])
    for i in colors:
        cross(i, line[i])
    for by in (1, -1, 2):
        for i in colors:
            plane[i][by if by == 2 else -by].wait_recv()
            wave[i][by] = both(i, piece(i, by), ORDERS[i][2])
            cross(i, piece(i, by))
    for by in (0, 1, -1, 2):
        for i in colors:
            last[i][by] = relay(i, piece(i, by), ORDERS[i][2], wave[i][by])
    for by in (0, 1, -1, 2):
        for i in colors:
            settle(last[i][by])
            a3 = ORDERS[i][2]
            cross(i, dict(piece(i, by), **{a3: moved(me, a3, 2)[a3]}))
    for copy in across:
        copy.wait_recv()
    net.drain()


def gather_keys(keys_values, queries, out_grad, attn_out, log_sums, doc_ids, span_order):
    rows = keys_values.shape[0]
    vmem = pl.BlockSpec(memory_space=pltpu.VMEM)
    *small, out = pl.pallas_call(
        gather_kernel,
        out_shape=(
            jax.ShapeDtypeStruct((2, NQ, HD), jnp.bfloat16),
            jax.ShapeDtypeStruct((2, NQ, HD), jnp.bfloat16),
            jax.ShapeDtypeStruct((2, HD, NQ), jnp.bfloat16),
            jax.ShapeDtypeStruct((2, HD, NQ), jnp.bfloat16),
            jax.ShapeDtypeStruct((8, 2 * span_order.shape[0]), jnp.int32),
            jax.ShapeDtypeStruct((8, NQ), jnp.float32),
            jax.ShapeDtypeStruct((2, 4, 4, 4, rows, COLS), keys_values.dtype),
        ),
        in_specs=[vmem] * 7,
        out_specs=(*[vmem] * 6, pl.BlockSpec(memory_space=pl.ANY)),
        scratch_shapes=[
            pltpu.VMEM((NQ, HD), jnp.float32),
            pltpu.SemaphoreType.DMA((GATHER_COPIES,)),
            pltpu.SemaphoreType.DMA((GATHER_COPIES,)),
            pltpu.SemaphoreType.DMA,
        ],
        compiler_params=pltpu.CompilerParams(collective_id=0, has_side_effects=True),
        name="gather_keys",
    )(
        keys_values,
        queries,
        out_grad,
        attn_out,
        log_sums,
        doc_ids.reshape(-1, 128),
        span_order.reshape(-1, 128),
    )
    qs, gs, qt, gt, meta, fmeta = small
    return meta, fmeta, qs, gs, qt, gt, out.reshape(128 * rows, COLS)


KEYS = (2, 1, -1, 0)
AWAY = (2, 1, -1)


class Scatter:
    def __init__(self, me, net, mine, other, halves, third, second, first, rows):
        self.me, self.net, self.mine, self.other, self.halves = me, net, mine, other, halves
        self.buffers = {3: third, 2: second, 1: first}
        self.parts = row_parts(rows)
        self.spot = {a: me[a] for a in "xyz"}
        self.flight = {}

    def at(self, i, d1, d2, d3):
        sel = dict(self.spot)
        for a, d in zip(ORDERS[i], (d1, d2, d3)):
            sel[a] = None if d is None else moved(self.me, a, d)[a]
        return sel

    def ix(self, i, sel, cols=FULL):
        return (*place(sel), pl.ds(*self.parts[i]), cols)

    def level_sel(self, level, i, key, d):
        return {3: self.at(i, None, key, d), 2: self.at(i, None, d, 0), 1: self.at(i, d, 0, 0)}[level]

    def blocks(self, level, i, key, d):
        sel = self.level_sel(level, i, key, d)
        if level == 1:
            return [((), sel)]
        return [((v,), dict(sel, **{ORDERS[i][0]: v})) for v in range(4)]

    def lead(self, level, i, key, d):
        side = AWAY.index(d) if self.halves is None or level < 3 else (0 if d == 1 else 1)
        return (i, KEYS.index(key), side) if level == 3 else (i, side)

    def slot(self, buf, level, i, key, d):
        lines = () if level == 1 else (slice(None),)
        return buf.at[(*self.lead(level, i, key, d), *lines, pl.ds(0, self.parts[i][1]), slice(None))]

    def row(self, level, i, key, d, v):
        return (*self.lead(level, i, key, d), *v, pl.ds(0, self.parts[i][1]), slice(None))

    def send(self, level, i, key, d):
        src = self.mine.at[self.ix(i, self.level_sel(level, i, key, d))]
        dst = self.slot(self.buffers[level], level, i, key, d)
        to = moved(self.me, ORDERS[i][level - 1], d)
        self.flight[level, i, key, d] = self.net.send(src, dst, to)

    def add_core(self, i, d2, d3):
        for _, sel in self.blocks(3, i, d2, d3):
            ix = self.ix(i, sel)
            self.mine[ix] = self.mine[ix] + self.other[ix]

    def open(self, i, key):
        if self.halves is None:
            for d in AWAY:
                self.send(3, i, key, d)
            return
        self.add_core(i, key, 2)
        sel = self.level_sel(3, i, key, 2)
        for d in (1, -1):
            dst = self.slot(self.halves, 3, i, key, d)
            src = self.mine.at[self.ix(i, sel, HALF[d])]
            to = moved(self.me, ORDERS[i][2], d)
            self.flight["half", i, key, d] = self.net.send(src, dst, to)
        self.add_core(i, key, 1)
        self.add_core(i, key, -1)

    def turn(self, i, key):
        for d in (1, -1):
            self.flight["half", i, key, d].wait_recv()
            for v, sel in self.blocks(3, i, key, d):
                ix = self.ix(i, sel, HALF[d])
                self.mine[ix] = self.mine[ix] + self.halves[self.row(3, i, key, d, v)]
            self.send(3, i, key, d)

    def close(self, level, i, key=0, write=None):
        sides = (1, -1) if level == 3 and self.halves is not None else AWAY
        for d in sides:
            self.flight[level, i, key, d].wait_recv()
        for v, sel in self.blocks(level, i, key, 0):
            ix = self.ix(i, sel)
            total = self.mine[ix].astype(jnp.float32)
            if level == 3 and self.other is not None:
                total = total + self.other[ix].astype(jnp.float32)
            for d in sides:
                total = total + self.buffers[level][self.row(level, i, key, d, v)].astype(jnp.float32)
            if write is None:
                self.mine[ix] = total.astype(self.mine.dtype)
            else:
                write(self.parts[i], total)

    def finish(self, i, key):
        self.close(3, i, key)
        if key != 0:
            self.send(2, i, 0, key)

    def run(self, ready, write, aside):
        colors = range(3)
        lag = 1 if self.halves is None else 2
        for n in range(len(KEYS) + lag):
            if n < len(KEYS):
                for i in colors:
                    ready(i, KEYS[n])
                    self.open(i, KEYS[n])
            if lag == 2 and 1 <= n <= len(KEYS):
                for i in colors:
                    self.turn(i, KEYS[n - 1])
            if n == len(KEYS) - 1:
                aside()
            if n >= lag:
                for i in colors:
                    self.finish(i, KEYS[n - lag])
        for i in colors:
            self.close(2, i)
            for d in AWAY:
                self.send(1, i, 0, d)
        for i in colors:
            self.close(1, i, write=write)


def scatter_scratch(rows, relayed):
    top = row_parts(rows)[0][1]
    plane = pltpu.VMEM((4, 4, 4, rows, COLS), jnp.bfloat16)
    return ([plane, plane, pltpu.VMEM((3, 4, 2, 4, top, HD), jnp.bfloat16)] if relayed else [plane]) + [
        pltpu.VMEM((3, 4, 2 if relayed else 3, 4, top, COLS), jnp.bfloat16),
        pltpu.VMEM((3, 3, 4, top, COLS), jnp.bfloat16),
        pltpu.VMEM((3, 3, top, COLS), jnp.bfloat16),
    ]


SCATTER_COPIES = 3 * (4 * 4 + 3 + 3) + 3 * (4 * 3 + 3 + 3) + 12 + 8 + 1


def scatter_kernel(part_ref, x_ref, kv_out, w_out, *scratch):
    kv_bufs, w_bufs = scratch[:6], scratch[6:10]
    x_theirs, xt, pair, send_sem, recv_sem, load_sem = scratch[10:]
    me = here()
    core = me["core"]
    rows, w_rows = kv_out.shape[0], w_out.shape[0]
    wide = 8 * w_rows
    net = Copies(send_sem, recv_sem)
    job = Scatter(me, net, *kv_bufs, rows)
    w_job = Scatter(me, net, w_bufs[0], None, None, *w_bufs[1:], w_rows)
    loads, swaps = {}, {}
    for n, key in enumerate(KEYS):
        for i in range(3):
            sel = job.at(i, None, key, None)
            src = part_ref.at[(*place(sel, core), pl.ds(*job.parts[i]), FULL)]
            dst = job.mine.at[job.ix(i, sel)]
            loads[i, key] = pltpu.make_async_copy(src, dst, load_sem.at[3 * n + i])
            loads[i, key].start()
    partner = meet(me)
    for key in KEYS:
        for i in range(3):
            sel = job.at(i, None, key, None)
            src = part_ref.at[(*place(sel, 1 - core), pl.ds(*job.parts[i]), FULL)]
            swaps[i, key] = net.send(src, job.other.at[job.ix(i, sel)], partner)

    def columns(j, which):
        first = (j // 4 * 8 + j % 4 * 2 + which) * wide
        return x_ref.at[:, pl.ds(pl.multiple_of(first, 128), wide)]

    x_swaps = [net.send(columns(j, 1 - core), x_theirs.at[j], partner) for j in range(8)]
    for j in range(8):
        xt[j, :, :rows] = columns(j, core)[...].T

    def ready(i, key):
        loads[i, key].wait()
        swaps[i, key].wait_recv()

    def turn_inputs():
        for j in range(8):
            x_swaps[j].wait_recv()
            xt[j, :, rows:] = x_theirs[j].T

    def write(part, total):
        low = total.astype(kv_out.dtype)
        kv_out[pl.ds(*part), :] = low
        pair[pl.ds(*part), :] = low

    job.run(ready, write, turn_inputs)

    swap = net.send(pair.at[pl.ds(0, rows)], pair.at[pl.ds(rows, rows)], partner)
    swap.wait_recv()
    both = pair[...]
    for j in range(8):
        out = jnp.dot(xt[j], both, preferred_element_type=jnp.float32).astype(jnp.bfloat16)
        for xh in range(2):
            for y in range(4):
                first = (xh * 4 + y) * w_rows
                w_job.mine[2 * xh + j // 4, j % 4, y] = out[first : first + w_rows]

    def w_write(part, total):
        w_out[pl.ds(*part), :] = total

    w_job.run(lambda i, key: None, w_write, lambda: None)
    net.drain()


def scatter_grads(kv_part, layer_input):
    tokens, width = kv_part.shape[0], layer_input.shape[1]
    rows, w_rows = tokens // 128, width // 128
    vmem = pl.BlockSpec(memory_space=pltpu.VMEM)
    return pl.pallas_call(
        scatter_kernel,
        out_shape=(
            jax.ShapeDtypeStruct((rows, COLS), jnp.bfloat16),
            jax.ShapeDtypeStruct((w_rows, COLS), jnp.float32),
        ),
        in_specs=[pl.BlockSpec(memory_space=pl.ANY), vmem],
        out_specs=(vmem, vmem),
        scratch_shapes=scatter_scratch(rows, True)
        + scatter_scratch(w_rows, False)
        + [
            pltpu.VMEM((8, rows, 8 * w_rows), jnp.bfloat16),
            pltpu.VMEM((8, 8 * w_rows, 2 * rows), jnp.bfloat16),
            pltpu.VMEM((2 * rows, COLS), jnp.bfloat16),
            pltpu.SemaphoreType.DMA((SCATTER_COPIES,)),
            pltpu.SemaphoreType.DMA((SCATTER_COPIES,)),
            pltpu.SemaphoreType.DMA((12,)),
        ],
        compiler_params=pltpu.CompilerParams(collective_id=1, has_side_effects=True),
        name="scatter_grads",
    )(kv_part.reshape(2, 4, 4, 4, rows, COLS), layer_input)


def per_device(
    layer_input, queries, keys_values, attn_out, out_grad, log_sums, doc_ids, span_order
):
    query_grad, kv_part = window_grads(
        *gather_keys(keys_values, queries, out_grad, attn_out, log_sums, doc_ids, span_order)
    )
    kv_total, weight_grad = scatter_grads(kv_part, layer_input)
    return (query_grad, kv_total, weight_grad)


def solution(mesh):
    rows = P(("inner", "outer"), None)
    return jax.shard_map(
        per_device,
        mesh=mesh,
        in_specs=(rows, rows, rows, rows, rows, P(None, ("inner", "outer")), P(), P()),
        out_specs=(rows, rows, rows),
        check_vma=False,
    )
```

```python
import functools

import jax
import jax.numpy as jnp
from jax import lax
from jax.experimental import pallas as pl
from jax.experimental.pallas import tpu as pltpu
from jax.sharding import PartitionSpec as P

CH = 4
SPAN = 64
HD = 128
HEADS = 6
NQ = SPAN * HEADS
MOST_DOC = 2048


def window_kernel(
    tab,
    meta,
    fmeta,
    qs,
    gs,
    qt,
    gt,
    kv_hbm,
    dq_ref,
    dkv_hbm,
    keys0,
    keys1,
    acc0,
    acc1,
    dq0,
    dq1,
    obuf,
    zbuf,
    dqt,
    ksem,
    zsem,
    osem,
    *,
    spans,
):
    scale = HD ** (-0.5)
    log2e = 1.4426950408889634
    two = range(2)
    kbuf, acc, dqs = (keys0, keys1), (acc0, acc1), (dq0, dq1)
    zrows = zbuf.shape[0]
    zcount = dkv_hbm.shape[0] // zrows
    p = [tab[0, spans + s] for s in two]
    lo = [tab[0, spans + 2 + s] for s in two]
    count = [p[s] - lo[s] + 1 for s in two]
    blocks = (jnp.maximum(count[0], count[1]) + CH - 1) // CH

    def key_copy(s, i):
        c = tab[0, jnp.minimum(lo[s] + i, spans - 1)]
        return pltpu.make_async_copy(
            kv_hbm.at[pl.ds(pl.multiple_of(c * SPAN, SPAN), SPAN)],
            kbuf[s].at[pl.ds(pl.multiple_of(i * SPAN, SPAN), SPAN)],
            ksem.at[s, i],
        )

    @pl.loop(0, blocks * CH)
    def _(i):
        for s in two:
            key_copy(s, i).start()

    zbuf[...] = jnp.zeros_like(zbuf)

    def zero_copy(i):
        return pltpu.make_async_copy(zbuf, dkv_hbm.at[pl.ds(i * zrows, zrows)], zsem.at[i])

    for i in range(zcount):
        zero_copy(i).start()

    lane = lax.broadcasted_iota(jnp.int32, (1, NQ), 1)
    delta = [fmeta[pl.ds(s, 1), :] for s in two]
    lse = [fmeta[pl.ds(2 + s, 1), :] * log2e for s in two]
    qpos = [p[s] * SPAN + (lane & (SPAN - 1)) for s in two]
    qstart = [meta[pl.ds(1 + s, 1), pl.ds(0, NQ)] for s in two]
    for s in two:
        dqs[s][...] = jnp.zeros_like(dqs[s])

    @pl.loop(0, blocks)
    def _(j):
        for i in range(CH):
            for s in two:
                key_copy(s, j * CH + i).wait()
        first = pl.multiple_of(j * CH * SPAN, CH * SPAN)
        at = pl.ds(first, CH * SPAN)
        row = lax.broadcasted_iota(jnp.int32, (CH * SPAN, NQ), 0)
        for s in two:
            kc = kbuf[s][at, :HD]
            vc = kbuf[s][at, HD:]
            st = jnp.dot(kc, qt[s], preferred_element_type=jnp.float32)
            dp = jnp.dot(vc, gt[s], preferred_element_type=jnp.float32)
            base = (lo[s] + j * CH) * SPAN
            keep = (row >= qstart[s] - base) & (row <= qpos[s] - base)
            prob = jnp.exp2(jnp.where(keep, st * (scale * log2e) - lse[s], -1e30))
            ds = (scale * prob * (dp - delta[s])).astype(jnp.bfloat16)
            pb = prob.astype(jnp.bfloat16)
            acc[s][at, :HD] = jnp.dot(ds, qs[s], preferred_element_type=jnp.float32)
            acc[s][at, HD:] = jnp.dot(pb, gs[s], preferred_element_type=jnp.float32)
            dqs[s][...] += lax.dot_general(
                kc, ds, (((0,), (0,)), ((), ())), preferred_element_type=jnp.float32
            )

    for i in range(zcount):
        zero_copy(i).wait()

    def out_copy(s, i):
        c = tab[0, lo[s] + i]
        return pltpu.make_async_copy(
            obuf.at[s, pl.ds(pl.multiple_of(i * SPAN, SPAN), SPAN)],
            dkv_hbm.at[pl.ds(pl.multiple_of(c * SPAN, SPAN), SPAN)],
            osem.at[s, i],
        )

    def shared(s, i):
        other = lo[s] + i - lo[1 - s]
        return other, (other >= 0) & (other < count[1 - s])

    def rows_of(i):
        return pl.ds(pl.multiple_of(i * SPAN, SPAN), SPAN)

    @pl.loop(0, count[0])
    def _(i):
        other, both = shared(0, i)

        @pl.when(both)
        def _():
            obuf[0, rows_of(i), :] = (acc0[rows_of(i), :] + acc1[rows_of(other), :]).astype(obuf.dtype)

        @pl.when(jnp.logical_not(both))
        def _():
            obuf[0, rows_of(i), :] = acc0[rows_of(i), :].astype(obuf.dtype)

        out_copy(0, i).start()

    @pl.loop(0, count[1])
    def _(i):
        @pl.when(jnp.logical_not(shared(1, i)[1]))
        def _():
            obuf[1, rows_of(i), :] = acc1[rows_of(i), :].astype(obuf.dtype)
            out_copy(1, i).start()

    for s in two:
        dqt[...] = dqs[s][...].T
        for h in range(HEADS):
            dq_ref[s * SPAN : (s + 1) * SPAN, h * HD : (h + 1) * HD] = dqt[
                h * SPAN : (h + 1) * SPAN, :
            ].astype(dq_ref.dtype)

    @pl.loop(0, count[0])
    def _(i):
        out_copy(0, i).wait()

    @pl.loop(0, count[1])
    def _(i):
        @pl.when(jnp.logical_not(shared(1, i)[1]))
        def _():
            out_copy(1, i).wait()


def window_grads(meta, fmeta, qs, gs, qt, gt, kv_all):
    tokens = kv_all.shape[0]
    spans = tokens // SPAN
    wmax = MOST_DOC // SPAN + 1
    wmax = -(-wmax // CH) * CH
    vmem = pl.BlockSpec(memory_space=pltpu.VMEM)
    anyspace = pl.BlockSpec(memory_space=pl.ANY)
    zrows = 1024
    return pl.pallas_call(
        functools.partial(window_kernel, spans=spans),
        out_shape=(
            jax.ShapeDtypeStruct((2 * SPAN, HEADS * HD), jnp.bfloat16),
            jax.ShapeDtypeStruct((tokens, 2 * HD), jnp.bfloat16),
        ),
        in_specs=[pl.BlockSpec(memory_space=pltpu.SMEM)] + [vmem] * 6 + [anyspace],
        out_specs=(vmem, anyspace),
        scratch_shapes=[
            pltpu.VMEM((wmax * SPAN, 2 * HD), jnp.bfloat16),
            pltpu.VMEM((wmax * SPAN, 2 * HD), jnp.bfloat16),
            pltpu.VMEM((wmax * SPAN, 2 * HD), jnp.float32),
            pltpu.VMEM((wmax * SPAN, 2 * HD), jnp.float32),
            pltpu.VMEM((HD, NQ), jnp.float32),
            pltpu.VMEM((HD, NQ), jnp.float32),
            pltpu.VMEM((2, wmax * SPAN, 2 * HD), jnp.bfloat16),
            pltpu.VMEM((zrows, 2 * HD), jnp.bfloat16),
            pltpu.VMEM((NQ, HD), jnp.float32),
            pltpu.SemaphoreType.DMA((2, wmax)),
            pltpu.SemaphoreType.DMA((tokens // zrows,)),
            pltpu.SemaphoreType.DMA((2, wmax)),
        ],
        name="window_grads",
    )(meta, meta, fmeta, qs, gs, qt, gt, kv_all)


def prepare(q_ref, og_ref, ao_ref, lse_ref, doc_ref, order_ref, qs, gs, qt, gt, meta, fmeta, tmp):
    spans = order_ref.shape[0] * order_ref.shape[1]
    order = jnp.concatenate([order_ref[0:1, :], order_ref[1:2, :]], axis=1).astype(jnp.float32)
    stored = jnp.broadcast_to(order, (spans, spans)).T
    lanes = lax.broadcasted_iota(jnp.int32, (spans, spans), 1).astype(jnp.float32)
    c = lax.broadcasted_iota(jnp.int32, (spans, spans), 0)
    kept = (
        ((c >> 4) & 1) * 128
        + (((c >> 3) & 1) * 2 + ((c >> 7) & 1)) * 32
        + ((c >> 5) & 3) * 8
        + ((c >> 1) & 3) * 2
        + (c & 1)
    ).astype(jnp.float32)
    inverse = jnp.sum(jnp.where(stored == lanes, kept, 0.0), axis=0, keepdims=True)
    docs = doc_ref[...]
    counts = [
        jnp.sum(jnp.where(docs < d, 1.0, 0.0), axis=0, keepdims=True) for d in range(16)
    ]
    first = jnp.sum(jnp.concatenate(counts, axis=0), axis=1, keepdims=True)
    mine = 2 * (lax.axis_index("inner") * 8 + lax.axis_index("outer"))
    spot = lax.broadcasted_iota(jnp.int32, (1, spans), 1)
    lane = lax.broadcasted_iota(jnp.int32, (1, NQ), 1)
    tail = jnp.zeros((1, spans), jnp.float32)
    for s in range(2):
        span = jnp.sum(jnp.where(spot == mine + s, order, 0.0), axis=1, keepdims=True)
        pos = span * SPAN + (lane & (SPAN - 1)).astype(jnp.float32)
        start = jnp.max(jnp.where(first <= pos, first, 0.0), axis=0, keepdims=True)
        low = (start[:, :1].astype(jnp.int32) >> 6).astype(jnp.float32)
        tail = jnp.where(spot == s, span, jnp.where(spot == 2 + s, low, tail))
        meta[1 + s : 2 + s, 0:NQ] = start.astype(jnp.int32)
    meta[0:1, 0:spans] = inverse.astype(jnp.int32)
    meta[0:1, spans:] = tail.astype(jnp.int32)
    for s in range(2):
        rows = slice(s * SPAN, (s + 1) * SPAN)
        for h in range(HEADS):
            cols = slice(h * HD, (h + 1) * HD)
            dst = slice(h * SPAN, (h + 1) * SPAN)
            qs[s, dst, :] = q_ref[rows, cols]
            gs[s, dst, :] = og_ref[rows, cols]
            tmp[dst, :] = og_ref[rows, cols].astype(jnp.float32) * ao_ref[rows, cols].astype(
                jnp.float32
            )
        fmeta[s : s + 1, :] = jnp.sum(tmp[...].T, axis=0, keepdims=True)
        fmeta[2 + s : 3 + s, :] = jnp.concatenate(
            [lse_ref[h : h + 1, rows] for h in range(HEADS)], axis=1
        )
        qt[s] = qs[s].T
        gt[s] = gs[s].T


ORDERS = (("x", "y", "z"), ("y", "z", "x"), ("z", "x", "y"))
COLS = 2 * HD
HALF = {1: pl.ds(0, HD), -1: pl.ds(HD, HD)}
FULL = pl.ds(0, COLS)


def here():
    i, o = lax.axis_index("inner"), lax.axis_index("outer")
    return {"x": (o // 4) * 2 + i // 8, "y": o % 4, "z": (i // 2) % 4, "core": i % 2}


def device(c):
    return ((c["x"] % 2) * 8 + c["z"] * 2 + c["core"], (c["x"] // 2) * 4 + c["y"])


def moved(c, axis, by):
    out = dict(c)
    out[axis] = (c[axis] + by + 4) % 4
    return out


def place(sel, core=None):
    where = tuple(slice(None) if sel[a] is None else sel[a] for a in "xzy")
    return where if core is None else (core, *where)


def row_parts(rows):
    first = -(-rows // 3 // 16) * 16
    sizes = (first, first, rows - 2 * first)
    return [(sum(sizes[:i]), sizes[i]) for i in range(3)]


class Copies:
    def __init__(self, send_sem, recv_sem):
        self.send_sem, self.recv_sem, self.all = send_sem, recv_sem, []

    def send(self, src, dst, target):
        k = len(self.all)
        copy = pltpu.make_async_remote_copy(
            src_ref=src,
            dst_ref=dst,
            send_sem=self.send_sem.at[k],
            recv_sem=self.recv_sem.at[k],
            device_id=device(target),
            device_id_type=pl.DeviceIdType.MESH,
        )
        copy.start()
        self.all.append(copy)
        return copy

    def drain(self):
        for copy in self.all:
            copy.wait_send()


def meet(me):
    barrier = pltpu.get_barrier_semaphore()
    partner = dict(me, core=1 - me["core"])
    others = [moved(me, a, d) for a in "xyz" for d in (1, -1, 2)] + [partner]
    for other in others:
        pl.semaphore_signal(
            barrier, inc=1, device_id=device(other), device_id_type=pl.DeviceIdType.MESH
        )
    pl.semaphore_wait(barrier, len(others))
    return partner


GATHER_COPIES = 3 * (3 + 3 + 16 + 16)


def gather_kernel(kv_ref, *refs):
    sources, targets, out = refs[:6], refs[6:12], refs[12]
    held, made = refs[13:19], refs[19:25]
    tmp, send_sem, recv_sem, own_sem, small_sem = refs[25:]
    taken = [
        pltpu.make_async_copy(sources[k], held[k], small_sem.at[k]) for k in range(6)
    ]
    given = [
        pltpu.make_async_copy(made[k], targets[k], small_sem.at[6 + k]) for k in range(6)
    ]
    for copy in taken:
        copy.start()
    me = here()
    core = me["core"]
    own = pltpu.make_async_copy(kv_ref, out.at[place(me, core)], own_sem)
    own.start()
    partner = meet(me)
    net = Copies(send_sem, recv_sem)
    parts = row_parts(kv_ref.shape[0])

    def block(part, sel, cols=FULL):
        return out.at[(*place(sel, core), pl.ds(*parts[part]), cols)]

    def push(part, sel, axis, by, cols=FULL, src=None):
        ref = block(part, sel, cols)
        return net.send(ref if src is None else src, ref, moved(me, axis, by))

    across = []

    def cross(part, sel):
        ref = block(part, sel)
        across.append(net.send(ref, ref, partner))

    def both(part, sel, axis):
        return {d: push(part, sel, axis, d) for d in (1, -1)}

    def relay(part, sel, axis, copies):
        out_copies = {}
        for d in (1, -1):
            copies[d].wait_recv()
            got = dict(sel, **{axis: moved(me, axis, -d)[axis]})
            out_copies[d] = push(part, got, axis, d, HALF[d])
            cross(part, got)
        return out_copies

    def settle(copies):
        for copy in copies.values():
            copy.wait_recv()

    colors = range(3)
    mine = {a: me[a] for a in "xyz"}
    first = [
        {
            d: push(i, mine, ORDERS[i][0], d, src=kv_ref.at[pl.ds(*parts[i]), :])
            for d in (2, 1, -1)
        }
        for i in colors
    ]
    for copy in taken:
        copy.wait()
    prepare(*held, *made, tmp)
    for copy in given:
        copy.start()
    own.wait()
    line = [dict(mine, **{ORDERS[i][0]: None}) for i in colors]
    plane = []
    wave = [{} for i in colors]
    last = [{} for i in colors]

    def piece(i, by):
        return dict(line[i], **{ORDERS[i][1]: moved(me, ORDERS[i][1], by)[ORDERS[i][1]]})

    for i in colors:
        settle(first[i])
        plane.append({d: push(i, line[i], ORDERS[i][1], d) for d in (2, 1, -1)})
    for i in colors:
        wave[i][0] = both(i, piece(i, 0), ORDERS[i][2])
    for i in colors:
        cross(i, line[i])
    for by in (1, -1, 2):
        for i in colors:
            plane[i][by if by == 2 else -by].wait_recv()
            wave[i][by] = both(i, piece(i, by), ORDERS[i][2])
            cross(i, piece(i, by))
    for by in (0, 1, -1, 2):
        for i in colors:
            last[i][by] = relay(i, piece(i, by), ORDERS[i][2], wave[i][by])
    for by in (0, 1, -1, 2):
        for i in colors:
            settle(last[i][by])
            a3 = ORDERS[i][2]
            cross(i, dict(piece(i, by), **{a3: moved(me, a3, 2)[a3]}))
    for copy in across:
        copy.wait_recv()
    for copy in given:
        copy.wait()
    net.drain()


def gather_keys(keys_values, queries, out_grad, attn_out, log_sums, doc_ids, span_order):
    rows = keys_values.shape[0]
    vmem = pl.BlockSpec(memory_space=pltpu.VMEM)
    anyspace = pl.BlockSpec(memory_space=pl.ANY)
    sources = (
        queries,
        out_grad,
        attn_out,
        log_sums,
        doc_ids.reshape(-1, 128),
        span_order.reshape(-1, 128),
    )
    made = [
        ((2, NQ, HD), jnp.bfloat16),
        ((2, NQ, HD), jnp.bfloat16),
        ((2, HD, NQ), jnp.bfloat16),
        ((2, HD, NQ), jnp.bfloat16),
        ((8, 2 * span_order.shape[0]), jnp.int32),
        ((8, NQ), jnp.float32),
    ]
    *small, out = pl.pallas_call(
        gather_kernel,
        out_shape=(
            *[jax.ShapeDtypeStruct(*m) for m in made],
            jax.ShapeDtypeStruct((2, 4, 4, 4, rows, COLS), keys_values.dtype),
        ),
        in_specs=[vmem] + [anyspace] * 6,
        out_specs=[anyspace] * 7,
        scratch_shapes=[pltpu.VMEM(v.shape, v.dtype) for v in sources]
        + [pltpu.VMEM(*m) for m in made]
        + [
            pltpu.VMEM((NQ, HD), jnp.float32),
            pltpu.SemaphoreType.DMA((GATHER_COPIES,)),
            pltpu.SemaphoreType.DMA((GATHER_COPIES,)),
            pltpu.SemaphoreType.DMA,
            pltpu.SemaphoreType.DMA((12,)),
        ],
        compiler_params=pltpu.CompilerParams(collective_id=0, has_side_effects=True),
        name="gather_keys",
    )(keys_values, *sources)
    qs, gs, qt, gt, meta, fmeta = small
    return meta, fmeta, qs, gs, qt, gt, out.reshape(128 * rows, COLS)


KEYS = (2, 1, -1, 0)
AWAY = (2, 1, -1)


class Scatter:
    def __init__(self, me, net, mine, other, halves, third, second, first, rows):
        self.me, self.net, self.mine, self.other, self.halves = me, net, mine, other, halves
        self.buffers = {3: third, 2: second, 1: first}
        self.parts = row_parts(rows)
        self.spot = {a: me[a] for a in "xyz"}
        self.flight = {}

    def at(self, i, d1, d2, d3):
        sel = dict(self.spot)
        for a, d in zip(ORDERS[i], (d1, d2, d3)):
            sel[a] = None if d is None else moved(self.me, a, d)[a]
        return sel

    def ix(self, i, sel, cols=FULL):
        return (*place(sel), pl.ds(*self.parts[i]), cols)

    def level_sel(self, level, i, key, d):
        return {3: self.at(i, None, key, d), 2: self.at(i, None, d, 0), 1: self.at(i, d, 0, 0)}[level]

    def blocks(self, level, i, key, d):
        sel = self.level_sel(level, i, key, d)
        if level == 1:
            return [((), sel)]
        return [((v,), dict(sel, **{ORDERS[i][0]: v})) for v in range(4)]

    def lead(self, level, i, key, d):
        side = AWAY.index(d) if self.halves is None or level < 3 else (0 if d == 1 else 1)
        return (i, KEYS.index(key), side) if level == 3 else (i, side)

    def slot(self, buf, level, i, key, d):
        lines = () if level == 1 else (slice(None),)
        return buf.at[(*self.lead(level, i, key, d), *lines, pl.ds(0, self.parts[i][1]), slice(None))]

    def row(self, level, i, key, d, v):
        return (*self.lead(level, i, key, d), *v, pl.ds(0, self.parts[i][1]), slice(None))

    def send(self, level, i, key, d):
        src = self.mine.at[self.ix(i, self.level_sel(level, i, key, d))]
        dst = self.slot(self.buffers[level], level, i, key, d)
        to = moved(self.me, ORDERS[i][level - 1], d)
        self.flight[level, i, key, d] = self.net.send(src, dst, to)

    def add_core(self, i, d2, d3):
        for _, sel in self.blocks(3, i, d2, d3):
            ix = self.ix(i, sel)
            self.mine[ix] = self.mine[ix] + self.other[ix]

    def open(self, i, key):
        if self.halves is None:
            for d in AWAY:
                self.send(3, i, key, d)
            return
        self.add_core(i, key, 2)
        sel = self.level_sel(3, i, key, 2)
        for d in (1, -1):
            dst = self.slot(self.halves, 3, i, key, d)
            src = self.mine.at[self.ix(i, sel, HALF[d])]
            to = moved(self.me, ORDERS[i][2], d)
            self.flight["half", i, key, d] = self.net.send(src, dst, to)
        self.add_core(i, key, 1)
        self.add_core(i, key, -1)

    def turn(self, i, key):
        for d in (1, -1):
            self.flight["half", i, key, d].wait_recv()
            for v, sel in self.blocks(3, i, key, d):
                ix = self.ix(i, sel, HALF[d])
                self.mine[ix] = self.mine[ix] + self.halves[self.row(3, i, key, d, v)]
            self.send(3, i, key, d)

    def close(self, level, i, key=0, write=None):
        sides = (1, -1) if level == 3 and self.halves is not None else AWAY
        for d in sides:
            self.flight[level, i, key, d].wait_recv()
        for v, sel in self.blocks(level, i, key, 0):
            ix = self.ix(i, sel)
            total = self.mine[ix].astype(jnp.float32)
            if level == 3 and self.other is not None:
                total = total + self.other[ix].astype(jnp.float32)
            for d in sides:
                total = total + self.buffers[level][self.row(level, i, key, d, v)].astype(jnp.float32)
            if write is None:
                self.mine[ix] = total.astype(self.mine.dtype)
            else:
                write(self.parts[i], total)

    def finish(self, i, key):
        self.close(3, i, key)
        if key != 0:
            self.send(2, i, 0, key)

    def run(self, ready, write, aside):
        colors = range(3)
        lag = 1 if self.halves is None else 2
        for n in range(len(KEYS) + lag):
            if n < len(KEYS):
                for i in colors:
                    ready(i, KEYS[n])
                    self.open(i, KEYS[n])
            if lag == 2 and 1 <= n <= len(KEYS):
                for i in colors:
                    self.turn(i, KEYS[n - 1])
            if n == len(KEYS) - 1:
                aside()
            if n >= lag:
                for i in colors:
                    self.finish(i, KEYS[n - lag])
        for i in colors:
            self.close(2, i)
            for d in AWAY:
                self.send(1, i, 0, d)
        for i in colors:
            self.close(1, i, write=write)


def scatter_scratch(rows, relayed):
    top = row_parts(rows)[0][1]
    plane = pltpu.VMEM((4, 4, 4, rows, COLS), jnp.bfloat16)
    return ([plane, plane, pltpu.VMEM((3, 4, 2, 4, top, HD), jnp.bfloat16)] if relayed else [plane]) + [
        pltpu.VMEM((3, 4, 2 if relayed else 3, 4, top, COLS), jnp.bfloat16),
        pltpu.VMEM((3, 3, 4, top, COLS), jnp.bfloat16),
        pltpu.VMEM((3, 3, top, COLS), jnp.bfloat16),
    ]


SCATTER_COPIES = 3 * (4 * 4 + 3 + 3) + 3 * (4 * 3 + 3 + 3) + 12 + 8 + 1


def scatter_kernel(part_ref, x_ref, kv_out, w_out, *scratch):
    kv_bufs, w_bufs = scratch[:6], scratch[6:10]
    x_buf, x_theirs, xt, pair, send_sem, recv_sem, load_sem = scratch[10:]
    x_load = pltpu.make_async_copy(x_ref, x_buf, load_sem.at[12])
    me = here()
    core = me["core"]
    rows, w_rows = kv_out.shape[0], w_out.shape[0]
    wide = 8 * w_rows
    net = Copies(send_sem, recv_sem)
    job = Scatter(me, net, *kv_bufs, rows)
    w_job = Scatter(me, net, w_bufs[0], None, None, *w_bufs[1:], w_rows)
    loads, swaps = {}, {}
    for n, key in enumerate(KEYS):
        for i in range(3):
            sel = job.at(i, None, key, None)
            src = part_ref.at[(*place(sel, core), pl.ds(*job.parts[i]), FULL)]
            dst = job.mine.at[job.ix(i, sel)]
            loads[i, key] = pltpu.make_async_copy(src, dst, load_sem.at[3 * n + i])
            loads[i, key].start()
    x_load.start()
    partner = meet(me)
    for key in KEYS:
        for i in range(3):
            sel = job.at(i, None, key, None)
            src = part_ref.at[(*place(sel, 1 - core), pl.ds(*job.parts[i]), FULL)]
            swaps[i, key] = net.send(src, job.other.at[job.ix(i, sel)], partner)

    def columns(j, which):
        first = (j // 4 * 8 + j % 4 * 2 + which) * wide
        return x_buf.at[:, pl.ds(pl.multiple_of(first, 128), wide)]

    x_load.wait()
    x_swaps = [net.send(columns(j, 1 - core), x_theirs.at[j], partner) for j in range(8)]
    for j in range(8):
        xt[j, :, :rows] = columns(j, core)[...].T

    def ready(i, key):
        loads[i, key].wait()
        swaps[i, key].wait_recv()

    def turn_inputs():
        for j in range(8):
            x_swaps[j].wait_recv()
            xt[j, :, rows:] = x_theirs[j].T

    def write(part, total):
        low = total.astype(kv_out.dtype)
        kv_out[pl.ds(*part), :] = low
        pair[pl.ds(*part), :] = low

    job.run(ready, write, turn_inputs)

    swap = net.send(pair.at[pl.ds(0, rows)], pair.at[pl.ds(rows, rows)], partner)
    swap.wait_recv()
    both = pair[...]
    for j in range(8):
        out = jnp.dot(xt[j], both, preferred_element_type=jnp.float32).astype(jnp.bfloat16)
        for xh in range(2):
            for y in range(4):
                first = (xh * 4 + y) * w_rows
                w_job.mine[2 * xh + j // 4, j % 4, y] = out[first : first + w_rows]

    def w_write(part, total):
        w_out[pl.ds(*part), :] = total

    w_job.run(lambda i, key: None, w_write, lambda: None)
    net.drain()


def scatter_grads(kv_part, layer_input):
    tokens, width = kv_part.shape[0], layer_input.shape[1]
    rows, w_rows = tokens // 128, width // 128
    vmem = pl.BlockSpec(memory_space=pltpu.VMEM)
    return pl.pallas_call(
        scatter_kernel,
        out_shape=(
            jax.ShapeDtypeStruct((rows, COLS), jnp.bfloat16),
            jax.ShapeDtypeStruct((w_rows, COLS), jnp.float32),
        ),
        in_specs=[pl.BlockSpec(memory_space=pl.ANY)] * 2,
        out_specs=(vmem, vmem),
        scratch_shapes=scatter_scratch(rows, True)
        + scatter_scratch(w_rows, False)
        + [
            pltpu.VMEM((rows, width), jnp.bfloat16),
            pltpu.VMEM((8, rows, 8 * w_rows), jnp.bfloat16),
            pltpu.VMEM((8, 8 * w_rows, 2 * rows), jnp.bfloat16),
            pltpu.VMEM((2 * rows, COLS), jnp.bfloat16),
            pltpu.SemaphoreType.DMA((SCATTER_COPIES,)),
            pltpu.SemaphoreType.DMA((SCATTER_COPIES,)),
            pltpu.SemaphoreType.DMA((13,)),
        ],
        compiler_params=pltpu.CompilerParams(collective_id=1, has_side_effects=True),
        name="scatter_grads",
    )(kv_part.reshape(2, 4, 4, 4, rows, COLS), layer_input)


def per_device(
    layer_input, queries, keys_values, attn_out, out_grad, log_sums, doc_ids, span_order
):
    query_grad, kv_part = window_grads(
        *gather_keys(keys_values, queries, out_grad, attn_out, log_sums, doc_ids, span_order)
    )
    kv_total, weight_grad = scatter_grads(kv_part, layer_input)
    return (query_grad, kv_total, weight_grad)


def solution(mesh):
    rows = P(("inner", "outer"), None)
    return jax.shard_map(
        per_device,
        mesh=mesh,
        in_specs=(rows, rows, rows, rows, rows, P(None, ("inner", "outer")), P(), P()),
        out_specs=(rows, rows, rows),
        check_vma=False,
    )
```

```python
import functools

import jax
import jax.numpy as jnp
from jax import lax
from jax.experimental import pallas as pl
from jax.experimental.pallas import tpu as pltpu
from jax.sharding import PartitionSpec as P

CH = 4
SPAN = 64
HD = 128
HEADS = 6
NQ = SPAN * HEADS
MOST_DOC = 2048


def window_kernel(
    tab,
    meta,
    fmeta,
    qs,
    gs,
    qt,
    gt,
    kv_hbm,
    dq_ref,
    dkv_hbm,
    keys0,
    keys1,
    acc0,
    acc1,
    dq0,
    dq1,
    sc0,
    sc1,
    dp0,
    dp1,
    ds0,
    ds1,
    pb0,
    pb1,
    obuf,
    zbuf,
    dqt,
    ksem,
    zsem,
    osem,
    *,
    spans,
):
    scale = HD ** (-0.5)
    log2e = 1.4426950408889634
    two = range(2)
    kbuf, acc, dqs = (keys0, keys1), (acc0, acc1), (dq0, dq1)
    sc, dp, ds, pb = (sc0, sc1), (dp0, dp1), (ds0, ds1), (pb0, pb1)
    zrows = zbuf.shape[0]
    zcount = dkv_hbm.shape[0] // zrows
    p = [tab[0, spans + s] for s in two]
    lo = [tab[0, spans + 2 + s] for s in two]
    count = [p[s] - lo[s] + 1 for s in two]
    blocks = (jnp.maximum(count[0], count[1]) + CH - 1) // CH

    def key_copy(s, i):
        c = tab[0, jnp.minimum(lo[s] + i, spans - 1)]
        return pltpu.make_async_copy(
            kv_hbm.at[pl.ds(pl.multiple_of(c * SPAN, SPAN), SPAN)],
            kbuf[s].at[pl.ds(pl.multiple_of(i * SPAN, SPAN), SPAN)],
            ksem.at[s, i],
        )

    @pl.loop(0, blocks * CH)
    def _(i):
        for s in two:
            key_copy(s, i).start()

    zbuf[...] = jnp.zeros_like(zbuf)

    def zero_copy(i):
        return pltpu.make_async_copy(zbuf, dkv_hbm.at[pl.ds(i * zrows, zrows)], zsem.at[i])

    for i in range(zcount):
        zero_copy(i).start()

    lane = lax.broadcasted_iota(jnp.int32, (1, NQ), 1)
    delta = [fmeta[pl.ds(s, 1), :] for s in two]
    lse = [fmeta[pl.ds(2 + s, 1), :] * log2e for s in two]
    qpos = [p[s] * SPAN + (lane & (SPAN - 1)) for s in two]
    qstart = [meta[pl.ds(1 + s, 1), pl.ds(0, NQ)] for s in two]
    for s in two:
        dqs[s][...] = jnp.zeros_like(dqs[s])

    def arrive(j):
        for i in range(CH):
            for s in two:
                key_copy(s, j * CH + i).wait()

    def block_rows(j):
        return pl.ds(pl.multiple_of(j * CH * SPAN, CH * SPAN), CH * SPAN)

    def products_in(j, two=two):
        at = block_rows(j)
        for s in two:
            sc[s][...] = jnp.dot(kbuf[s][at, :HD], qt[s], preferred_element_type=jnp.float32)
            dp[s][...] = jnp.dot(kbuf[s][at, HD:], gt[s], preferred_element_type=jnp.float32)

    def weigh(j, two=two):
        part = 16
        row = lax.broadcasted_iota(jnp.int32, (part, NQ), 0)
        for n in range(CH * SPAN // part):
            some = slice(n * part, (n + 1) * part)
            for s in two:
                base = (lo[s] + j * CH) * SPAN + n * part
                keep = (row >= qstart[s] - base) & (row <= qpos[s] - base)
                score = sc[s][some, :] * (scale * log2e) - lse[s]
                prob = jnp.exp2(jnp.where(keep, score, -1e30))
                grad = scale * prob * (dp[s][some, :] - delta[s])
                ds[s][some, :] = grad.astype(jnp.bfloat16)
                pb[s][some, :] = prob.astype(jnp.bfloat16)

    def products_out(j, two=two):
        at = block_rows(j)
        for s in two:
            acc[s][at, :HD] = jnp.dot(ds[s][...], qs[s], preferred_element_type=jnp.float32)
            acc[s][at, HD:] = jnp.dot(pb[s][...], gs[s], preferred_element_type=jnp.float32)
            dqs[s][...] += lax.dot_general(
                kbuf[s][at, :HD],
                ds[s][...],
                (((0,), (0,)), ((), ())),
                preferred_element_type=jnp.float32,
            )

    for s in two:
        ds[s][...] = jnp.zeros_like(ds[s])
        pb[s][...] = jnp.zeros_like(pb[s])
    arrive(0)
    products_in(0)

    @pl.loop(0, blocks)
    def _(j):
        @pl.when(j + 1 < blocks)
        def _():
            arrive(j + 1)

        for s in two:
            products_out(jnp.maximum(j - 1, 0), (s,))
            weigh(j, (s,))
            products_in(jnp.minimum(j + 1, blocks - 1), (s,))

    products_out(blocks - 1)

    for i in range(zcount):
        zero_copy(i).wait()

    def out_copy(s, i):
        c = tab[0, lo[s] + i]
        return pltpu.make_async_copy(
            obuf.at[s, pl.ds(pl.multiple_of(i * SPAN, SPAN), SPAN)],
            dkv_hbm.at[pl.ds(pl.multiple_of(c * SPAN, SPAN), SPAN)],
            osem.at[s, i],
        )

    def shared(s, i):
        other = lo[s] + i - lo[1 - s]
        return other, (other >= 0) & (other < count[1 - s])

    def rows_of(i):
        return pl.ds(pl.multiple_of(i * SPAN, SPAN), SPAN)

    @pl.loop(0, count[0])
    def _(i):
        other, both = shared(0, i)

        @pl.when(both)
        def _():
            obuf[0, rows_of(i), :] = (acc0[rows_of(i), :] + acc1[rows_of(other), :]).astype(obuf.dtype)

        @pl.when(jnp.logical_not(both))
        def _():
            obuf[0, rows_of(i), :] = acc0[rows_of(i), :].astype(obuf.dtype)

        out_copy(0, i).start()

    @pl.loop(0, count[1])
    def _(i):
        @pl.when(jnp.logical_not(shared(1, i)[1]))
        def _():
            obuf[1, rows_of(i), :] = acc1[rows_of(i), :].astype(obuf.dtype)
            out_copy(1, i).start()

    for s in two:
        dqt[...] = dqs[s][...].T
        for h in range(HEADS):
            dq_ref[s * SPAN : (s + 1) * SPAN, h * HD : (h + 1) * HD] = dqt[
                h * SPAN : (h + 1) * SPAN, :
            ].astype(dq_ref.dtype)

    @pl.loop(0, count[0])
    def _(i):
        out_copy(0, i).wait()

    @pl.loop(0, count[1])
    def _(i):
        @pl.when(jnp.logical_not(shared(1, i)[1]))
        def _():
            out_copy(1, i).wait()


def window_grads(meta, fmeta, qs, gs, qt, gt, kv_all):
    tokens = kv_all.shape[0]
    spans = tokens // SPAN
    wmax = MOST_DOC // SPAN + 1
    wmax = -(-wmax // CH) * CH
    vmem = pl.BlockSpec(memory_space=pltpu.VMEM)
    anyspace = pl.BlockSpec(memory_space=pl.ANY)
    zrows = 1024
    return pl.pallas_call(
        functools.partial(window_kernel, spans=spans),
        out_shape=(
            jax.ShapeDtypeStruct((2 * SPAN, HEADS * HD), jnp.bfloat16),
            jax.ShapeDtypeStruct((tokens, 2 * HD), jnp.bfloat16),
        ),
        in_specs=[pl.BlockSpec(memory_space=pltpu.SMEM)] + [vmem] * 6 + [anyspace],
        out_specs=(vmem, anyspace),
        scratch_shapes=[
            pltpu.VMEM((wmax * SPAN, 2 * HD), jnp.bfloat16),
            pltpu.VMEM((wmax * SPAN, 2 * HD), jnp.bfloat16),
            pltpu.VMEM((wmax * SPAN, 2 * HD), jnp.float32),
            pltpu.VMEM((wmax * SPAN, 2 * HD), jnp.float32),
            pltpu.VMEM((HD, NQ), jnp.float32),
            pltpu.VMEM((HD, NQ), jnp.float32),
            *[pltpu.VMEM((CH * SPAN, NQ), jnp.float32)] * 4,
            *[pltpu.VMEM((CH * SPAN, NQ), jnp.bfloat16)] * 4,
            pltpu.VMEM((2, wmax * SPAN, 2 * HD), jnp.bfloat16),
            pltpu.VMEM((zrows, 2 * HD), jnp.bfloat16),
            pltpu.VMEM((NQ, HD), jnp.float32),
            pltpu.SemaphoreType.DMA((2, wmax)),
            pltpu.SemaphoreType.DMA((tokens // zrows,)),
            pltpu.SemaphoreType.DMA((2, wmax)),
        ],
        name="window_grads",
    )(meta, meta, fmeta, qs, gs, qt, gt, kv_all)


def prepare(q_ref, og_ref, ao_ref, lse_ref, doc_ref, order_ref, qs, gs, qt, gt, meta, fmeta, tmp):
    spans = order_ref.shape[0] * order_ref.shape[1]
    order = jnp.concatenate([order_ref[0:1, :], order_ref[1:2, :]], axis=1).astype(jnp.float32)
    stored = jnp.broadcast_to(order, (spans, spans)).T
    lanes = lax.broadcasted_iota(jnp.int32, (spans, spans), 1).astype(jnp.float32)
    c = lax.broadcasted_iota(jnp.int32, (spans, spans), 0)
    kept = (
        ((c >> 4) & 1) * 128
        + (((c >> 3) & 1) * 2 + ((c >> 7) & 1)) * 32
        + ((c >> 5) & 3) * 8
        + ((c >> 1) & 3) * 2
        + (c & 1)
    ).astype(jnp.float32)
    inverse = jnp.sum(jnp.where(stored == lanes, kept, 0.0), axis=0, keepdims=True)
    docs = doc_ref[...]
    counts = [
        jnp.sum(jnp.where(docs < d, 1.0, 0.0), axis=0, keepdims=True) for d in range(16)
    ]
    first = jnp.sum(jnp.concatenate(counts, axis=0), axis=1, keepdims=True)
    mine = 2 * (lax.axis_index("inner") * 8 + lax.axis_index("outer"))
    spot = lax.broadcasted_iota(jnp.int32, (1, spans), 1)
    lane = lax.broadcasted_iota(jnp.int32, (1, NQ), 1)
    tail = jnp.zeros((1, spans), jnp.float32)
    for s in range(2):
        span = jnp.sum(jnp.where(spot == mine + s, order, 0.0), axis=1, keepdims=True)
        pos = span * SPAN + (lane & (SPAN - 1)).astype(jnp.float32)
        start = jnp.max(jnp.where(first <= pos, first, 0.0), axis=0, keepdims=True)
        low = (start[:, :1].astype(jnp.int32) >> 6).astype(jnp.float32)
        tail = jnp.where(spot == s, span, jnp.where(spot == 2 + s, low, tail))
        meta[1 + s : 2 + s, 0:NQ] = start.astype(jnp.int32)
    meta[0:1, 0:spans] = inverse.astype(jnp.int32)
    meta[0:1, spans:] = tail.astype(jnp.int32)
    for s in range(2):
        rows = slice(s * SPAN, (s + 1) * SPAN)
        for h in range(HEADS):
            cols = slice(h * HD, (h + 1) * HD)
            dst = slice(h * SPAN, (h + 1) * SPAN)
            qs[s, dst, :] = q_ref[rows, cols]
            gs[s, dst, :] = og_ref[rows, cols]
            tmp[dst, :] = og_ref[rows, cols].astype(jnp.float32) * ao_ref[rows, cols].astype(
                jnp.float32
            )
        fmeta[s : s + 1, :] = jnp.sum(tmp[...].T, axis=0, keepdims=True)
        fmeta[2 + s : 3 + s, :] = jnp.concatenate(
            [lse_ref[h : h + 1, rows] for h in range(HEADS)], axis=1
        )
        qt[s] = qs[s].T
        gt[s] = gs[s].T


ORDERS = (("x", "y", "z"), ("y", "z", "x"), ("z", "x", "y"))
COLS = 2 * HD
HALF = {1: pl.ds(0, HD), -1: pl.ds(HD, HD)}
FULL = pl.ds(0, COLS)


def here():
    i, o = lax.axis_index("inner"), lax.axis_index("outer")
    return {"x": (o // 4) * 2 + i // 8, "y": o % 4, "z": (i // 2) % 4, "core": i % 2}


def device(c):
    return ((c["x"] % 2) * 8 + c["z"] * 2 + c["core"], (c["x"] // 2) * 4 + c["y"])


def moved(c, axis, by):
    out = dict(c)
    out[axis] = (c[axis] + by + 4) % 4
    return out


def place(sel, core=None):
    where = tuple(slice(None) if sel[a] is None else sel[a] for a in "xzy")
    return where if core is None else (core, *where)


def row_parts(rows):
    first = -(-rows // 3 // 16) * 16
    sizes = (first, first, rows - 2 * first)
    return [(sum(sizes[:i]), sizes[i]) for i in range(3)]


class Copies:
    def __init__(self, send_sem, recv_sem):
        self.send_sem, self.recv_sem, self.all = send_sem, recv_sem, []

    def send(self, src, dst, target):
        k = len(self.all)
        copy = pltpu.make_async_remote_copy(
            src_ref=src,
            dst_ref=dst,
            send_sem=self.send_sem.at[k],
            recv_sem=self.recv_sem.at[k],
            device_id=device(target),
            device_id_type=pl.DeviceIdType.MESH,
        )
        copy.start()
        self.all.append(copy)
        return copy

    def drain(self):
        for copy in self.all:
            copy.wait_send()


def meet(me):
    barrier = pltpu.get_barrier_semaphore()
    partner = dict(me, core=1 - me["core"])
    others = [moved(me, a, d) for a in "xyz" for d in (1, -1, 2)] + [partner]
    for other in others:
        pl.semaphore_signal(
            barrier, inc=1, device_id=device(other), device_id_type=pl.DeviceIdType.MESH
        )
    pl.semaphore_wait(barrier, len(others))
    return partner


GATHER_COPIES = 3 * (3 + 3 + 16 + 16)


def gather_kernel(kv_ref, *refs):
    sources, targets, out = refs[:6], refs[6:12], refs[12]
    held, made = refs[13:19], refs[19:25]
    tmp, send_sem, recv_sem, own_sem, small_sem = refs[25:]
    taken = [
        pltpu.make_async_copy(sources[k], held[k], small_sem.at[k]) for k in range(6)
    ]
    given = [
        pltpu.make_async_copy(made[k], targets[k], small_sem.at[6 + k]) for k in range(6)
    ]
    for copy in taken:
        copy.start()
    me = here()
    core = me["core"]
    own = pltpu.make_async_copy(kv_ref, out.at[place(me, core)], own_sem)
    own.start()
    partner = meet(me)
    net = Copies(send_sem, recv_sem)
    parts = row_parts(kv_ref.shape[0])

    def block(part, sel, cols=FULL):
        return out.at[(*place(sel, core), pl.ds(*parts[part]), cols)]

    def push(part, sel, axis, by, cols=FULL, src=None):
        ref = block(part, sel, cols)
        return net.send(ref if src is None else src, ref, moved(me, axis, by))

    across = []

    def cross(part, sel):
        ref = block(part, sel)
        across.append(net.send(ref, ref, partner))

    def both(part, sel, axis):
        return {d: push(part, sel, axis, d) for d in (1, -1)}

    def relay(part, sel, axis, copies):
        out_copies = {}
        for d in (1, -1):
            copies[d].wait_recv()
            got = dict(sel, **{axis: moved(me, axis, -d)[axis]})
            out_copies[d] = push(part, got, axis, d, HALF[d])
            cross(part, got)
        return out_copies

    def settle(copies):
        for copy in copies.values():
            copy.wait_recv()

    colors = range(3)
    mine = {a: me[a] for a in "xyz"}
    first = [
        {
            d: push(i, mine, ORDERS[i][0], d, src=kv_ref.at[pl.ds(*parts[i]), :])
            for d in (2, 1, -1)
        }
        for i in colors
    ]
    for copy in taken:
        copy.wait()
    prepare(*held, *made, tmp)
    for copy in given:
        copy.start()
    own.wait()
    line = [dict(mine, **{ORDERS[i][0]: None}) for i in colors]
    plane = []
    wave = [{} for i in colors]
    last = [{} for i in colors]

    def piece(i, by):
        return dict(line[i], **{ORDERS[i][1]: moved(me, ORDERS[i][1], by)[ORDERS[i][1]]})

    for i in colors:
        settle(first[i])
        plane.append({d: push(i, line[i], ORDERS[i][1], d) for d in (2, 1, -1)})
    for i in colors:
        wave[i][0] = both(i, piece(i, 0), ORDERS[i][2])
    for i in colors:
        cross(i, line[i])
    for by in (1, -1, 2):
        for i in colors:
            plane[i][by if by == 2 else -by].wait_recv()
            wave[i][by] = both(i, piece(i, by), ORDERS[i][2])
            cross(i, piece(i, by))
    for by in (0, 1, -1, 2):
        for i in colors:
            last[i][by] = relay(i, piece(i, by), ORDERS[i][2], wave[i][by])
    for by in (0, 1, -1, 2):
        for i in colors:
            settle(last[i][by])
            a3 = ORDERS[i][2]
            cross(i, dict(piece(i, by), **{a3: moved(me, a3, 2)[a3]}))
    for copy in across:
        copy.wait_recv()
    for copy in given:
        copy.wait()
    net.drain()


def gather_keys(keys_values, queries, out_grad, attn_out, log_sums, doc_ids, span_order):
    rows = keys_values.shape[0]
    vmem = pl.BlockSpec(memory_space=pltpu.VMEM)
    anyspace = pl.BlockSpec(memory_space=pl.ANY)
    sources = (
        queries,
        out_grad,
        attn_out,
        log_sums,
        doc_ids.reshape(-1, 128),
        span_order.reshape(-1, 128),
    )
    made = [
        ((2, NQ, HD), jnp.bfloat16),
        ((2, NQ, HD), jnp.bfloat16),
        ((2, HD, NQ), jnp.bfloat16),
        ((2, HD, NQ), jnp.bfloat16),
        ((8, 2 * span_order.shape[0]), jnp.int32),
        ((8, NQ), jnp.float32),
    ]
    *small, out = pl.pallas_call(
        gather_kernel,
        out_shape=(
            *[jax.ShapeDtypeStruct(*m) for m in made],
            jax.ShapeDtypeStruct((2, 4, 4, 4, rows, COLS), keys_values.dtype),
        ),
        in_specs=[vmem] + [anyspace] * 6,
        out_specs=[anyspace] * 7,
        scratch_shapes=[pltpu.VMEM(v.shape, v.dtype) for v in sources]
        + [pltpu.VMEM(*m) for m in made]
        + [
            pltpu.VMEM((NQ, HD), jnp.float32),
            pltpu.SemaphoreType.DMA((GATHER_COPIES,)),
            pltpu.SemaphoreType.DMA((GATHER_COPIES,)),
            pltpu.SemaphoreType.DMA,
            pltpu.SemaphoreType.DMA((12,)),
        ],
        compiler_params=pltpu.CompilerParams(collective_id=0, has_side_effects=True),
        name="gather_keys",
    )(keys_values, *sources)
    qs, gs, qt, gt, meta, fmeta = small
    return meta, fmeta, qs, gs, qt, gt, out.reshape(128 * rows, COLS)


KEYS = (2, 1, -1, 0)
AWAY = (2, 1, -1)


class Scatter:
    def __init__(self, me, net, mine, other, halves, third, second, first, rows):
        self.me, self.net, self.mine, self.other, self.halves = me, net, mine, other, halves
        self.buffers = {3: third, 2: second, 1: first}
        self.parts = row_parts(rows)
        self.spot = {a: me[a] for a in "xyz"}
        self.flight = {}

    def at(self, i, d1, d2, d3):
        sel = dict(self.spot)
        for a, d in zip(ORDERS[i], (d1, d2, d3)):
            sel[a] = None if d is None else moved(self.me, a, d)[a]
        return sel

    def ix(self, i, sel, cols=FULL):
        return (*place(sel), pl.ds(*self.parts[i]), cols)

    def level_sel(self, level, i, key, d):
        return {3: self.at(i, None, key, d), 2: self.at(i, None, d, 0), 1: self.at(i, d, 0, 0)}[level]

    def blocks(self, level, i, key, d):
        sel = self.level_sel(level, i, key, d)
        if level == 1:
            return [((), sel)]
        return [((v,), dict(sel, **{ORDERS[i][0]: v})) for v in range(4)]

    def lead(self, level, i, key, d):
        side = AWAY.index(d) if self.halves is None or level < 3 else (0 if d == 1 else 1)
        return (i, KEYS.index(key), side) if level == 3 else (i, side)

    def slot(self, buf, level, i, key, d):
        lines = () if level == 1 else (slice(None),)
        return buf.at[(*self.lead(level, i, key, d), *lines, pl.ds(0, self.parts[i][1]), slice(None))]

    def row(self, level, i, key, d, v):
        return (*self.lead(level, i, key, d), *v, pl.ds(0, self.parts[i][1]), slice(None))

    def send(self, level, i, key, d):
        src = self.mine.at[self.ix(i, self.level_sel(level, i, key, d))]
        dst = self.slot(self.buffers[level], level, i, key, d)
        to = moved(self.me, ORDERS[i][level - 1], d)
        self.flight[level, i, key, d] = self.net.send(src, dst, to)

    def add_core(self, i, d2, d3):
        for _, sel in self.blocks(3, i, d2, d3):
            ix = self.ix(i, sel)
            self.mine[ix] = self.mine[ix] + self.other[ix]

    def open(self, i, key):
        if self.halves is None:
            for d in AWAY:
                self.send(3, i, key, d)
            return
        self.add_core(i, key, 2)
        sel = self.level_sel(3, i, key, 2)
        for d in (1, -1):
            dst = self.slot(self.halves, 3, i, key, d)
            src = self.mine.at[self.ix(i, sel, HALF[d])]
            to = moved(self.me, ORDERS[i][2], d)
            self.flight["half", i, key, d] = self.net.send(src, dst, to)
        self.add_core(i, key, 1)
        self.add_core(i, key, -1)

    def turn(self, i, key):
        for d in (1, -1):
            self.flight["half", i, key, d].wait_recv()
            for v, sel in self.blocks(3, i, key, d):
                ix = self.ix(i, sel, HALF[d])
                self.mine[ix] = self.mine[ix] + self.halves[self.row(3, i, key, d, v)]
            self.send(3, i, key, d)

    def close(self, level, i, key=0, write=None):
        sides = (1, -1) if level == 3 and self.halves is not None else AWAY
        for d in sides:
            self.flight[level, i, key, d].wait_recv()
        for v, sel in self.blocks(level, i, key, 0):
            ix = self.ix(i, sel)
            total = self.mine[ix].astype(jnp.float32)
            if level == 3 and self.other is not None:
                total = total + self.other[ix].astype(jnp.float32)
            for d in sides:
                total = total + self.buffers[level][self.row(level, i, key, d, v)].astype(jnp.float32)
            if write is None:
                self.mine[ix] = total.astype(self.mine.dtype)
            else:
                write(self.parts[i], total)

    def finish(self, i, key):
        self.close(3, i, key)
        if key != 0:
            self.send(2, i, 0, key)

    def run(self, ready, write, aside):
        colors = range(3)
        lag = 1 if self.halves is None else 2
        for n in range(len(KEYS) + lag):
            if n < len(KEYS):
                for i in colors:
                    ready(i, KEYS[n])
                    self.open(i, KEYS[n])
            if lag == 2 and 1 <= n <= len(KEYS):
                for i in colors:
                    self.turn(i, KEYS[n - 1])
            if n == len(KEYS) - 1:
                aside()
            if n >= lag:
                for i in colors:
                    self.finish(i, KEYS[n - lag])
        for i in colors:
            self.close(2, i)
            for d in AWAY:
                self.send(1, i, 0, d)
        for i in colors:
            self.close(1, i, write=write)


def scatter_scratch(rows, relayed):
    top = row_parts(rows)[0][1]
    plane = pltpu.VMEM((4, 4, 4, rows, COLS), jnp.bfloat16)
    return ([plane, plane, pltpu.VMEM((3, 4, 2, 4, top, HD), jnp.bfloat16)] if relayed else [plane]) + [
        pltpu.VMEM((3, 4, 2 if relayed else 3, 4, top, COLS), jnp.bfloat16),
        pltpu.VMEM((3, 3, 4, top, COLS), jnp.bfloat16),
        pltpu.VMEM((3, 3, top, COLS), jnp.bfloat16),
    ]


SCATTER_COPIES = 3 * (4 * 4 + 3 + 3) + 3 * (4 * 3 + 3 + 3) + 12 + 8 + 1


def scatter_kernel(part_ref, x_ref, kv_out, w_out, *scratch):
    kv_bufs, w_bufs = scratch[:6], scratch[6:10]
    x_buf, x_theirs, xt, pair, send_sem, recv_sem, load_sem = scratch[10:]
    x_load = pltpu.make_async_copy(x_ref, x_buf, load_sem.at[12])
    me = here()
    core = me["core"]
    rows, w_rows = kv_out.shape[0], w_out.shape[0]
    wide = 8 * w_rows
    net = Copies(send_sem, recv_sem)
    job = Scatter(me, net, *kv_bufs, rows)
    w_job = Scatter(me, net, w_bufs[0], None, None, *w_bufs[1:], w_rows)
    loads, swaps = {}, {}
    for n, key in enumerate(KEYS):
        for i in range(3):
            sel = job.at(i, None, key, None)
            src = part_ref.at[(*place(sel, core), pl.ds(*job.parts[i]), FULL)]
            dst = job.mine.at[job.ix(i, sel)]
            loads[i, key] = pltpu.make_async_copy(src, dst, load_sem.at[3 * n + i])
            loads[i, key].start()
    x_load.start()
    partner = meet(me)
    for key in KEYS:
        for i in range(3):
            sel = job.at(i, None, key, None)
            src = part_ref.at[(*place(sel, 1 - core), pl.ds(*job.parts[i]), FULL)]
            swaps[i, key] = net.send(src, job.other.at[job.ix(i, sel)], partner)

    def columns(j, which):
        first = (j // 4 * 8 + j % 4 * 2 + which) * wide
        return x_buf.at[:, pl.ds(pl.multiple_of(first, 128), wide)]

    x_load.wait()
    x_swaps = [net.send(columns(j, 1 - core), x_theirs.at[j], partner) for j in range(8)]
    for j in range(8):
        xt[j, :, :rows] = columns(j, core)[...].T

    def ready(i, key):
        loads[i, key].wait()
        swaps[i, key].wait_recv()

    def turn_inputs():
        for j in range(8):
            x_swaps[j].wait_recv()
            xt[j, :, rows:] = x_theirs[j].T

    def write(part, total):
        low = total.astype(kv_out.dtype)
        kv_out[pl.ds(*part), :] = low
        pair[pl.ds(*part), :] = low

    job.run(ready, write, turn_inputs)

    swap = net.send(pair.at[pl.ds(0, rows)], pair.at[pl.ds(rows, rows)], partner)
    swap.wait_recv()
    both = pair[...]
    for j in range(8):
        out = jnp.dot(xt[j], both, preferred_element_type=jnp.float32).astype(jnp.bfloat16)
        for xh in range(2):
            for y in range(4):
                first = (xh * 4 + y) * w_rows
                w_job.mine[2 * xh + j // 4, j % 4, y] = out[first : first + w_rows]

    def w_write(part, total):
        w_out[pl.ds(*part), :] = total

    w_job.run(lambda i, key: None, w_write, lambda: None)
    net.drain()


def scatter_grads(kv_part, layer_input):
    tokens, width = kv_part.shape[0], layer_input.shape[1]
    rows, w_rows = tokens // 128, width // 128
    vmem = pl.BlockSpec(memory_space=pltpu.VMEM)
    return pl.pallas_call(
        scatter_kernel,
        out_shape=(
            jax.ShapeDtypeStruct((rows, COLS), jnp.bfloat16),
            jax.ShapeDtypeStruct((w_rows, COLS), jnp.float32),
        ),
        in_specs=[pl.BlockSpec(memory_space=pl.ANY)] * 2,
        out_specs=(vmem, vmem),
        scratch_shapes=scatter_scratch(rows, True)
        + scatter_scratch(w_rows, False)
        + [
            pltpu.VMEM((rows, width), jnp.bfloat16),
            pltpu.VMEM((8, rows, 8 * w_rows), jnp.bfloat16),
            pltpu.VMEM((8, 8 * w_rows, 2 * rows), jnp.bfloat16),
            pltpu.VMEM((2 * rows, COLS), jnp.bfloat16),
            pltpu.SemaphoreType.DMA((SCATTER_COPIES,)),
            pltpu.SemaphoreType.DMA((SCATTER_COPIES,)),
            pltpu.SemaphoreType.DMA((13,)),
        ],
        compiler_params=pltpu.CompilerParams(collective_id=1, has_side_effects=True),
        name="scatter_grads",
    )(kv_part.reshape(2, 4, 4, 4, rows, COLS), layer_input)


def copy_kernel(a, b, a_out, b_out):
    a_out[...] = a[...]
    b_out[...] = b[...]


def handed_on(a, b):
    vmem = pl.BlockSpec(memory_space=pltpu.VMEM)
    return pl.pallas_call(
        copy_kernel,
        out_shape=[jax.ShapeDtypeStruct(v.shape, v.dtype) for v in (a, b)],
        in_specs=[vmem] * 2,
        out_specs=[vmem] * 2,
        name="handed_on",
    )(a, b)


def per_device(
    layer_input, queries, keys_values, attn_out, out_grad, log_sums, doc_ids, span_order
):
    query_grad, kv_part = window_grads(
        *gather_keys(keys_values, queries, out_grad, attn_out, log_sums, doc_ids, span_order)
    )
    return (query_grad, *handed_on(*scatter_grads(kv_part, layer_input)))


def solution(mesh):
    rows = P(("inner", "outer"), None)
    return jax.shard_map(
        per_device,
        mesh=mesh,
        in_specs=(rows, rows, rows, rows, rows, P(None, ("inner", "outer")), P(), P()),
        out_specs=(rows, rows, rows),
        check_vma=False,
    )
```

```python
import functools

import jax
import jax.numpy as jnp
from jax import lax
from jax.experimental import pallas as pl
from jax.experimental.pallas import tpu as pltpu
from jax.sharding import PartitionSpec as P

CH = 4
SPAN = 64
HD = 128
HEADS = 6
NQ = SPAN * HEADS
MOST_DOC = 2048


def window_kernel(
    tab,
    meta_hbm,
    fmeta_hbm,
    qs_hbm,
    gs_hbm,
    qt_hbm,
    gt_hbm,
    kv_hbm,
    dq_hbm,
    dkv_hbm,
    meta,
    fmeta,
    qs,
    gs,
    qt,
    gt,
    dq_ref,
    keys0,
    keys1,
    acc0,
    acc1,
    dq0,
    dq1,
    sc0,
    sc1,
    dp0,
    dp1,
    ds0,
    ds1,
    pb0,
    pb1,
    zbuf,
    dqt,
    ksem,
    zsem,
    osem,
    isem,
    *,
    spans,
):
    scale = HD ** (-0.5)
    log2e = 1.4426950408889634
    two = range(2)
    kbuf, acc, dqs = (keys0, keys1), (acc0, acc1), (dq0, dq1)
    sc, dp, ds, pb = (sc0, sc1), (dp0, dp1), (ds0, ds1), (pb0, pb1)
    zrows = zbuf.shape[0]
    zcount = dkv_hbm.shape[0] // zrows
    p = [tab[0, spans + s] for s in two]
    lo = [tab[0, spans + 2 + s] for s in two]
    count = [p[s] - lo[s] + 1 for s in two]
    blocks = (jnp.maximum(count[0], count[1]) + CH - 1) // CH

    def key_copy(s, i):
        c = tab[0, jnp.minimum(lo[s] + i, spans - 1)]
        return pltpu.make_async_copy(
            kv_hbm.at[pl.ds(pl.multiple_of(c * SPAN, SPAN), SPAN)],
            kbuf[s].at[pl.ds(pl.multiple_of(i * SPAN, SPAN), SPAN)],
            ksem.at[s, i],
        )

    @pl.loop(0, blocks * CH)
    def _(i):
        for s in two:
            key_copy(s, i).start()

    sources = (meta_hbm, fmeta_hbm, qs_hbm, gs_hbm, qt_hbm, gt_hbm)
    taken = [
        pltpu.make_async_copy(src, dst, isem.at[k])
        for k, (src, dst) in enumerate(zip(sources, (meta, fmeta, qs, gs, qt, gt)))
    ]
    for copy in taken:
        copy.start()
    zbuf[...] = jnp.zeros_like(zbuf)

    def zero_copy(i):
        return pltpu.make_async_copy(zbuf, dkv_hbm.at[pl.ds(i * zrows, zrows)], zsem.at[i])

    for i in range(zcount):
        zero_copy(i).start()

    for copy in taken:
        copy.wait()
    lane = lax.broadcasted_iota(jnp.int32, (1, NQ), 1)
    delta = [fmeta[pl.ds(s, 1), :] for s in two]
    lse = [fmeta[pl.ds(2 + s, 1), :] * log2e for s in two]
    qpos = [p[s] * SPAN + (lane & (SPAN - 1)) for s in two]
    qstart = [meta[pl.ds(1 + s, 1), pl.ds(0, NQ)] for s in two]
    for s in two:
        dqs[s][...] = jnp.zeros_like(dqs[s])

    def arrive(j):
        for i in range(CH):
            for s in two:
                key_copy(s, j * CH + i).wait()

    def block_rows(j):
        return pl.ds(pl.multiple_of(j * CH * SPAN, CH * SPAN), CH * SPAN)

    def products_in(j, two=two):
        at = block_rows(j)
        for s in two:
            sc[s][...] = jnp.dot(kbuf[s][at, :HD], qt[s], preferred_element_type=jnp.float32)
            dp[s][...] = jnp.dot(kbuf[s][at, HD:], gt[s], preferred_element_type=jnp.float32)

    def weigh(j, two=two):
        part = 16
        row = lax.broadcasted_iota(jnp.int32, (part, NQ), 0)
        for n in range(CH * SPAN // part):
            some = slice(n * part, (n + 1) * part)
            for s in two:
                base = (lo[s] + j * CH) * SPAN + n * part
                keep = (row >= qstart[s] - base) & (row <= qpos[s] - base)
                score = sc[s][some, :] * (scale * log2e) - lse[s]
                prob = jnp.exp2(jnp.where(keep, score, -1e30))
                grad = scale * prob * (dp[s][some, :] - delta[s])
                ds[s][some, :] = grad.astype(jnp.bfloat16)
                pb[s][some, :] = prob.astype(jnp.bfloat16)

    def products_out(j, two=two):
        at = block_rows(j)
        for s in two:
            dk = jnp.dot(ds[s][...], qs[s], preferred_element_type=jnp.float32)
            dv = jnp.dot(pb[s][...], gs[s], preferred_element_type=jnp.float32)
            acc[s][at, :HD] = dk.astype(jnp.bfloat16)
            acc[s][at, HD:] = dv.astype(jnp.bfloat16)
            dqs[s][...] += lax.dot_general(
                kbuf[s][at, :HD],
                ds[s][...],
                (((0,), (0,)), ((), ())),
                preferred_element_type=jnp.float32,
            )

    for s in two:
        ds[s][...] = jnp.zeros_like(ds[s])
        pb[s][...] = jnp.zeros_like(pb[s])
    arrive(0)
    products_in(0)

    @pl.loop(0, blocks)
    def _(j):
        @pl.when(j + 1 < blocks)
        def _():
            arrive(j + 1)

        for s in two:
            products_out(jnp.maximum(j - 1, 0), (s,))
            weigh(j, (s,))
            products_in(jnp.minimum(j + 1, blocks - 1), (s,))

    products_out(blocks - 1)

    def out_copy(s, i):
        c = tab[0, lo[s] + i]
        return pltpu.make_async_copy(
            acc[s].at[rows_of(i)],
            dkv_hbm.at[pl.ds(pl.multiple_of(c * SPAN, SPAN), SPAN)],
            osem.at[s, i],
        )

    def rows_of(i):
        return pl.ds(pl.multiple_of(i * SPAN, SPAN), SPAN)

    def shared(s, i):
        other = lo[s] + i - lo[1 - s]
        return other, (other >= 0) & (other < count[1 - s])

    for i in range(zcount):
        zero_copy(i).wait()

    @pl.loop(0, count[0])
    def _(i):
        other, both = shared(0, i)

        @pl.when(both)
        def _():
            term = acc0[rows_of(i), :].astype(jnp.float32) + acc1[rows_of(other), :].astype(jnp.float32)
            acc0[rows_of(i), :] = term.astype(jnp.bfloat16)

        out_copy(0, i).start()

    @pl.loop(0, count[1])
    def _(i):
        @pl.when(jnp.logical_not(shared(1, i)[1]))
        def _():
            out_copy(1, i).start()

    for s in two:
        dqt[...] = dqs[s][...].T
        for h in range(HEADS):
            dq_ref[s * SPAN : (s + 1) * SPAN, h * HD : (h + 1) * HD] = dqt[
                h * SPAN : (h + 1) * SPAN, :
            ].astype(dq_ref.dtype)
    dq_out = pltpu.make_async_copy(dq_ref, dq_hbm, isem.at[6])
    dq_out.start()

    @pl.loop(0, count[0])
    def _(i):
        out_copy(0, i).wait()

    @pl.loop(0, count[1])
    def _(i):
        @pl.when(jnp.logical_not(shared(1, i)[1]))
        def _():
            out_copy(1, i).wait()

    dq_out.wait()


def window_grads(meta, fmeta, qs, gs, qt, gt, kv_all):
    tokens = kv_all.shape[0]
    spans = tokens // SPAN
    wmax = MOST_DOC // SPAN + 1
    wmax = -(-wmax // CH) * CH
    anyspace = pl.BlockSpec(memory_space=pl.ANY)
    zrows = 1024
    return pl.pallas_call(
        functools.partial(window_kernel, spans=spans),
        out_shape=(
            jax.ShapeDtypeStruct((2 * SPAN, HEADS * HD), jnp.bfloat16),
            jax.ShapeDtypeStruct((tokens, 2 * HD), jnp.bfloat16),
        ),
        in_specs=[pl.BlockSpec(memory_space=pltpu.SMEM)] + [anyspace] * 7,
        out_specs=(anyspace, anyspace),
        scratch_shapes=[pltpu.VMEM(v.shape, v.dtype) for v in (meta, fmeta, qs, gs, qt, gt)]
        + [
            pltpu.VMEM((2 * SPAN, HEADS * HD), jnp.bfloat16),
            *[pltpu.VMEM((wmax * SPAN, 2 * HD), jnp.bfloat16)] * 4,
            pltpu.VMEM((HD, NQ), jnp.float32),
            pltpu.VMEM((HD, NQ), jnp.float32),
            *[pltpu.VMEM((CH * SPAN, NQ), jnp.float32)] * 4,
            *[pltpu.VMEM((CH * SPAN, NQ), jnp.bfloat16)] * 4,
            pltpu.VMEM((zrows, 2 * HD), jnp.bfloat16),
            pltpu.VMEM((NQ, HD), jnp.float32),
            pltpu.SemaphoreType.DMA((2, wmax)),
            pltpu.SemaphoreType.DMA((tokens // zrows,)),
            pltpu.SemaphoreType.DMA((2, wmax)),
            pltpu.SemaphoreType.DMA((7,)),
        ],
        name="window_grads",
    )(meta, meta, fmeta, qs, gs, qt, gt, kv_all)


def prepare(q_ref, og_ref, ao_ref, lse_ref, doc_ref, order_ref, qs, gs, qt, gt, meta, fmeta, tmp):
    spans = order_ref.shape[0] * order_ref.shape[1]
    order = jnp.concatenate([order_ref[0:1, :], order_ref[1:2, :]], axis=1).astype(jnp.float32)
    stored = jnp.broadcast_to(order, (spans, spans)).T
    lanes = lax.broadcasted_iota(jnp.int32, (spans, spans), 1).astype(jnp.float32)
    c = lax.broadcasted_iota(jnp.int32, (spans, spans), 0)
    kept = (
        ((c >> 4) & 1) * 128
        + (((c >> 3) & 1) * 2 + ((c >> 7) & 1)) * 32
        + ((c >> 5) & 3) * 8
        + ((c >> 1) & 3) * 2
        + (c & 1)
    ).astype(jnp.float32)
    inverse = jnp.sum(jnp.where(stored == lanes, kept, 0.0), axis=0, keepdims=True)
    docs = doc_ref[...]
    counts = [
        jnp.sum(jnp.where(docs < d, 1.0, 0.0), axis=0, keepdims=True) for d in range(16)
    ]
    first = jnp.sum(jnp.concatenate(counts, axis=0), axis=1, keepdims=True)
    mine = 2 * (lax.axis_index("inner") * 8 + lax.axis_index("outer"))
    spot = lax.broadcasted_iota(jnp.int32, (1, spans), 1)
    lane = lax.broadcasted_iota(jnp.int32, (1, NQ), 1)
    tail = jnp.zeros((1, spans), jnp.float32)
    for s in range(2):
        span = jnp.sum(jnp.where(spot == mine + s, order, 0.0), axis=1, keepdims=True)
        pos = span * SPAN + (lane & (SPAN - 1)).astype(jnp.float32)
        start = jnp.max(jnp.where(first <= pos, first, 0.0), axis=0, keepdims=True)
        low = (start[:, :1].astype(jnp.int32) >> 6).astype(jnp.float32)
        tail = jnp.where(spot == s, span, jnp.where(spot == 2 + s, low, tail))
        meta[1 + s : 2 + s, 0:NQ] = start.astype(jnp.int32)
    meta[0:1, 0:spans] = inverse.astype(jnp.int32)
    meta[0:1, spans:] = tail.astype(jnp.int32)
    for s in range(2):
        rows = slice(s * SPAN, (s + 1) * SPAN)
        for h in range(HEADS):
            cols = slice(h * HD, (h + 1) * HD)
            dst = slice(h * SPAN, (h + 1) * SPAN)
            qs[s, dst, :] = q_ref[rows, cols]
            gs[s, dst, :] = og_ref[rows, cols]
            tmp[dst, :] = og_ref[rows, cols].astype(jnp.float32) * ao_ref[rows, cols].astype(
                jnp.float32
            )
        fmeta[s : s + 1, :] = jnp.sum(tmp[...].T, axis=0, keepdims=True)
        fmeta[2 + s : 3 + s, :] = jnp.concatenate(
            [lse_ref[h : h + 1, rows] for h in range(HEADS)], axis=1
        )
        qt[s] = qs[s].T
        gt[s] = gs[s].T


ORDERS = (("x", "y", "z"), ("y", "z", "x"), ("z", "x", "y"))
COLS = 2 * HD
HALF = {1: pl.ds(0, HD), -1: pl.ds(HD, HD)}
FULL = pl.ds(0, COLS)


def here():
    i, o = lax.axis_index("inner"), lax.axis_index("outer")
    return {"x": (o // 4) * 2 + i // 8, "y": o % 4, "z": (i // 2) % 4, "core": i % 2}


def device(c):
    return ((c["x"] % 2) * 8 + c["z"] * 2 + c["core"], (c["x"] // 2) * 4 + c["y"])


def moved(c, axis, by):
    out = dict(c)
    out[axis] = (c[axis] + by + 4) % 4
    return out


def place(sel, core=None):
    where = tuple(slice(None) if sel[a] is None else sel[a] for a in "xzy")
    return where if core is None else (core, *where)


def row_parts(rows):
    first = -(-rows // 3 // 16) * 16
    sizes = (first, first, rows - 2 * first)
    return [(sum(sizes[:i]), sizes[i]) for i in range(3)]


class Copies:
    def __init__(self, send_sem, recv_sem):
        self.send_sem, self.recv_sem, self.all = send_sem, recv_sem, []

    def send(self, src, dst, target):
        k = len(self.all)
        copy = pltpu.make_async_remote_copy(
            src_ref=src,
            dst_ref=dst,
            send_sem=self.send_sem.at[k],
            recv_sem=self.recv_sem.at[k],
            device_id=device(target),
            device_id_type=pl.DeviceIdType.MESH,
        )
        copy.start()
        self.all.append(copy)
        return copy

    def drain(self):
        for copy in self.all:
            copy.wait_send()


def meet(me):
    barrier = pltpu.get_barrier_semaphore()
    partner = dict(me, core=1 - me["core"])
    others = [moved(me, a, d) for a in "xyz" for d in (1, -1, 2)] + [partner]
    for other in others:
        pl.semaphore_signal(
            barrier, inc=1, device_id=device(other), device_id_type=pl.DeviceIdType.MESH
        )
    pl.semaphore_wait(barrier, len(others))
    return partner


GATHER_COPIES = 3 * (3 + 3 + 16 + 16)


def gather_kernel(kv_ref, *refs):
    sources, targets, out = refs[:6], refs[6:12], refs[12]
    held, made = refs[13:19], refs[19:25]
    tmp, send_sem, recv_sem, own_sem, small_sem = refs[25:]
    taken = [
        pltpu.make_async_copy(sources[k], held[k], small_sem.at[k]) for k in range(6)
    ]
    given = [
        pltpu.make_async_copy(made[k], targets[k], small_sem.at[6 + k]) for k in range(6)
    ]
    for copy in taken:
        copy.start()
    me = here()
    core = me["core"]
    own = pltpu.make_async_copy(kv_ref, out.at[place(me, core)], own_sem)
    own.start()
    partner = meet(me)
    net = Copies(send_sem, recv_sem)
    parts = row_parts(kv_ref.shape[0])

    def block(part, sel, cols=FULL):
        return out.at[(*place(sel, core), pl.ds(*parts[part]), cols)]

    def push(part, sel, axis, by, cols=FULL, src=None):
        ref = block(part, sel, cols)
        return net.send(ref if src is None else src, ref, moved(me, axis, by))

    across = []

    def cross(part, sel):
        ref = block(part, sel)
        across.append(net.send(ref, ref, partner))

    def both(part, sel, axis):
        return {d: push(part, sel, axis, d) for d in (1, -1)}

    def relay(part, sel, axis, copies):
        out_copies = {}
        for d in (1, -1):
            copies[d].wait_recv()
            got = dict(sel, **{axis: moved(me, axis, -d)[axis]})
            out_copies[d] = push(part, got, axis, d, HALF[d])
            cross(part, got)
        return out_copies

    def settle(copies):
        for copy in copies.values():
            copy.wait_recv()

    colors = range(3)
    mine = {a: me[a] for a in "xyz"}
    first = [
        {
            d: push(i, mine, ORDERS[i][0], d, src=kv_ref.at[pl.ds(*parts[i]), :])
            for d in (2, 1, -1)
        }
        for i in colors
    ]
    for copy in taken:
        copy.wait()
    prepare(*held, *made, tmp)
    for copy in given:
        copy.start()
    own.wait()
    line = [dict(mine, **{ORDERS[i][0]: None}) for i in colors]
    plane = []
    wave = [{} for i in colors]
    last = [{} for i in colors]

    def piece(i, by):
        return dict(line[i], **{ORDERS[i][1]: moved(me, ORDERS[i][1], by)[ORDERS[i][1]]})

    for i in colors:
        settle(first[i])
        plane.append({d: push(i, line[i], ORDERS[i][1], d) for d in (2, 1, -1)})
    for i in colors:
        wave[i][0] = both(i, piece(i, 0), ORDERS[i][2])
    for i in colors:
        cross(i, line[i])
    for by in (1, -1, 2):
        for i in colors:
            plane[i][by if by == 2 else -by].wait_recv()
            wave[i][by] = both(i, piece(i, by), ORDERS[i][2])
            cross(i, piece(i, by))
    for by in (0, 1, -1, 2):
        for i in colors:
            last[i][by] = relay(i, piece(i, by), ORDERS[i][2], wave[i][by])
    for by in (0, 1, -1, 2):
        for i in colors:
            settle(last[i][by])
            a3 = ORDERS[i][2]
            cross(i, dict(piece(i, by), **{a3: moved(me, a3, 2)[a3]}))
    for copy in across:
        copy.wait_recv()
    for copy in given:
        copy.wait()
    net.drain()


def gather_keys(keys_values, queries, out_grad, attn_out, log_sums, doc_ids, span_order):
    rows = keys_values.shape[0]
    vmem = pl.BlockSpec(memory_space=pltpu.VMEM)
    anyspace = pl.BlockSpec(memory_space=pl.ANY)
    sources = (
        queries,
        out_grad,
        attn_out,
        log_sums,
        doc_ids.reshape(-1, 128),
        span_order.reshape(-1, 128),
    )
    made = [
        ((2, NQ, HD), jnp.bfloat16),
        ((2, NQ, HD), jnp.bfloat16),
        ((2, HD, NQ), jnp.bfloat16),
        ((2, HD, NQ), jnp.bfloat16),
        ((8, 2 * span_order.shape[0]), jnp.int32),
        ((8, NQ), jnp.float32),
    ]
    *small, out = pl.pallas_call(
        gather_kernel,
        out_shape=(
            *[jax.ShapeDtypeStruct(*m) for m in made],
            jax.ShapeDtypeStruct((2, 4, 4, 4, rows, COLS), keys_values.dtype),
        ),
        in_specs=[vmem] + [anyspace] * 6,
        out_specs=[anyspace] * 7,
        scratch_shapes=[pltpu.VMEM(v.shape, v.dtype) for v in sources]
        + [pltpu.VMEM(*m) for m in made]
        + [
            pltpu.VMEM((NQ, HD), jnp.float32),
            pltpu.SemaphoreType.DMA((GATHER_COPIES,)),
            pltpu.SemaphoreType.DMA((GATHER_COPIES,)),
            pltpu.SemaphoreType.DMA,
            pltpu.SemaphoreType.DMA((12,)),
        ],
        compiler_params=pltpu.CompilerParams(collective_id=0, has_side_effects=True),
        name="gather_keys",
    )(keys_values, *sources)
    qs, gs, qt, gt, meta, fmeta = small
    return meta, fmeta, qs, gs, qt, gt, out.reshape(128 * rows, COLS)


KEYS = (2, 1, -1, 0)
AWAY = (2, 1, -1)


class Scatter:
    def __init__(self, me, net, mine, other, halves, third, second, first, rows):
        self.me, self.net, self.mine, self.other, self.halves = me, net, mine, other, halves
        self.buffers = {3: third, 2: second, 1: first}
        self.parts = row_parts(rows)
        self.spot = {a: me[a] for a in "xyz"}
        self.flight = {}

    def at(self, i, d1, d2, d3):
        sel = dict(self.spot)
        for a, d in zip(ORDERS[i], (d1, d2, d3)):
            sel[a] = None if d is None else moved(self.me, a, d)[a]
        return sel

    def ix(self, i, sel, cols=FULL):
        return (*place(sel), pl.ds(*self.parts[i]), cols)

    def level_sel(self, level, i, key, d):
        return {3: self.at(i, None, key, d), 2: self.at(i, None, d, 0), 1: self.at(i, d, 0, 0)}[level]

    def blocks(self, level, i, key, d):
        sel = self.level_sel(level, i, key, d)
        if level == 1:
            return [((), sel)]
        return [((v,), dict(sel, **{ORDERS[i][0]: v})) for v in range(4)]

    def lead(self, level, i, key, d):
        side = AWAY.index(d) if self.halves is None or level < 3 else (0 if d == 1 else 1)
        return (i, KEYS.index(key), side) if level == 3 else (i, side)

    def slot(self, buf, level, i, key, d):
        lines = () if level == 1 else (slice(None),)
        return buf.at[(*self.lead(level, i, key, d), *lines, pl.ds(0, self.parts[i][1]), slice(None))]

    def row(self, level, i, key, d, v):
        return (*self.lead(level, i, key, d), *v, pl.ds(0, self.parts[i][1]), slice(None))

    def send(self, level, i, key, d):
        src = self.mine.at[self.ix(i, self.level_sel(level, i, key, d))]
        dst = self.slot(self.buffers[level], level, i, key, d)
        to = moved(self.me, ORDERS[i][level - 1], d)
        self.flight[level, i, key, d] = self.net.send(src, dst, to)

    def add_core(self, i, d2, d3):
        self.arrived(i, d2, d3)
        for _, sel in self.blocks(3, i, d2, d3):
            ix = self.ix(i, sel)
            self.mine[ix] = self.mine[ix] + self.other[ix]

    def open(self, i, key):
        if self.halves is None:
            for d in AWAY:
                self.send(3, i, key, d)
            return
        self.add_core(i, key, 2)
        sel = self.level_sel(3, i, key, 2)
        for d in (1, -1):
            dst = self.slot(self.halves, 3, i, key, d)
            src = self.mine.at[self.ix(i, sel, HALF[d])]
            to = moved(self.me, ORDERS[i][2], d)
            self.flight["half", i, key, d] = self.net.send(src, dst, to)
        self.add_core(i, key, 1)
        self.add_core(i, key, -1)

    def turn(self, i, key):
        for d in (1, -1):
            self.flight["half", i, key, d].wait_recv()
            for v, sel in self.blocks(3, i, key, d):
                ix = self.ix(i, sel, HALF[d])
                self.mine[ix] = self.mine[ix] + self.halves[self.row(3, i, key, d, v)]
            self.send(3, i, key, d)

    def close(self, level, i, key=0, write=None):
        sides = (1, -1) if level == 3 and self.halves is not None else AWAY
        if level == 3 and self.other is not None:
            self.arrived(i, key, 0)
        for d in sides:
            self.flight[level, i, key, d].wait_recv()
        for v, sel in self.blocks(level, i, key, 0):
            ix = self.ix(i, sel)
            total = self.mine[ix].astype(jnp.float32)
            if level == 3 and self.other is not None:
                total = total + self.other[ix].astype(jnp.float32)
            for d in sides:
                total = total + self.buffers[level][self.row(level, i, key, d, v)].astype(jnp.float32)
            if write is None:
                self.mine[ix] = total.astype(self.mine.dtype)
            else:
                write(self.parts[i], total)

    def finish(self, i, key):
        self.close(3, i, key)
        if key != 0:
            self.send(2, i, 0, key)

    def run(self, ready, write, aside):
        colors = range(3)
        lag = 1 if self.halves is None else 2
        for n in range(len(KEYS) + lag):
            if n < len(KEYS):
                for i in colors:
                    ready(i, KEYS[n])
                    self.open(i, KEYS[n])
            if lag == 2 and 1 <= n <= len(KEYS):
                for i in colors:
                    self.turn(i, KEYS[n - 1])
            if n == len(KEYS) - 1:
                aside()
            if n >= lag:
                for i in colors:
                    self.finish(i, KEYS[n - lag])
        for i in colors:
            self.close(2, i)
            for d in AWAY:
                self.send(1, i, 0, d)
        for i in colors:
            self.close(1, i, write=write)


def scatter_scratch(rows, relayed):
    top = row_parts(rows)[0][1]
    plane = pltpu.VMEM((4, 4, 4, rows, COLS), jnp.bfloat16)
    return ([plane, plane, pltpu.VMEM((3, 4, 2, 4, top, HD), jnp.bfloat16)] if relayed else [plane]) + [
        pltpu.VMEM((3, 4, 2 if relayed else 3, 4, top, COLS), jnp.bfloat16),
        pltpu.VMEM((3, 3, 4, top, COLS), jnp.bfloat16),
        pltpu.VMEM((3, 3, top, COLS), jnp.bfloat16),
    ]


SCATTER_COPIES = 3 * (4 * 4 + 3 + 3) + 3 * (4 * 3 + 3 + 3) + 21 + 8 + 1


def scatter_kernel(part_ref, x_ref, kv_out, w_out, *scratch):
    kv_bufs, w_bufs = scratch[:6], scratch[6:10]
    x_buf, x_theirs, xt, pair, send_sem, recv_sem, load_sem = scratch[10:]
    x_load = pltpu.make_async_copy(x_ref, x_buf, load_sem.at[12])
    me = here()
    core = me["core"]
    rows, w_rows = kv_out.shape[0], w_out.shape[0]
    wide = 8 * w_rows
    net = Copies(send_sem, recv_sem)
    job = Scatter(me, net, *kv_bufs, rows)
    w_job = Scatter(me, net, w_bufs[0], None, None, *w_bufs[1:], w_rows)
    loads, swaps = {}, {}
    for n, key in enumerate(KEYS):
        for i in range(3):
            sel = job.at(i, None, key, None)
            src = part_ref.at[(*place(sel, core), pl.ds(*job.parts[i]), FULL)]
            dst = job.mine.at[job.ix(i, sel)]
            loads[i, key] = pltpu.make_async_copy(src, dst, load_sem.at[3 * n + i])
            loads[i, key].start()
    x_load.start()
    partner = meet(me)
    for key in KEYS:
        for d in KEYS if key == KEYS[0] else (None,):
            for i in range(3):
                sel = job.at(i, None, key, d)
                src = part_ref.at[(*place(sel, 1 - core), pl.ds(*job.parts[i]), FULL)]
                swaps[i, key, d] = net.send(src, job.other.at[job.ix(i, sel)], partner)

    def arrived(i, key, d):
        copy = swaps.pop((i, key, d if key == KEYS[0] else None), None)
        if copy is not None:
            copy.wait_recv()

    job.arrived = arrived

    def columns(j, which):
        first = (j // 4 * 8 + j % 4 * 2 + which) * wide
        return x_buf.at[:, pl.ds(pl.multiple_of(first, 128), wide)]

    x_load.wait()
    x_swaps = [net.send(columns(j, 1 - core), x_theirs.at[j], partner) for j in range(8)]
    for j in range(8):
        xt[j, :, :rows] = columns(j, core)[...].T

    def ready(i, key):
        loads[i, key].wait()

    def turn_inputs():
        for j in range(8):
            x_swaps[j].wait_recv()
            xt[j, :, rows:] = x_theirs[j].T

    def write(part, total):
        low = total.astype(kv_out.dtype)
        kv_out[pl.ds(*part), :] = low
        pair[pl.ds(*part), :] = low

    job.run(ready, write, turn_inputs)

    swap = net.send(pair.at[pl.ds(0, rows)], pair.at[pl.ds(rows, rows)], partner)
    swap.wait_recv()
    both = pair[...]
    for j in range(8):
        out = jnp.dot(xt[j], both, preferred_element_type=jnp.float32).astype(jnp.bfloat16)
        for xh in range(2):
            for y in range(4):
                first = (xh * 4 + y) * w_rows
                w_job.mine[2 * xh + j // 4, j % 4, y] = out[first : first + w_rows]

    def w_write(part, total):
        w_out[pl.ds(*part), :] = total

    w_job.run(lambda i, key: None, w_write, lambda: None)
    net.drain()


def scatter_grads(kv_part, layer_input):
    tokens, width = kv_part.shape[0], layer_input.shape[1]
    rows, w_rows = tokens // 128, width // 128
    vmem = pl.BlockSpec(memory_space=pltpu.VMEM)
    return pl.pallas_call(
        scatter_kernel,
        out_shape=(
            jax.ShapeDtypeStruct((rows, COLS), jnp.bfloat16),
            jax.ShapeDtypeStruct((w_rows, COLS), jnp.float32),
        ),
        in_specs=[pl.BlockSpec(memory_space=pl.ANY)] * 2,
        out_specs=(vmem, vmem),
        scratch_shapes=scatter_scratch(rows, True)
        + scatter_scratch(w_rows, False)
        + [
            pltpu.VMEM((rows, width), jnp.bfloat16),
            pltpu.VMEM((8, rows, 8 * w_rows), jnp.bfloat16),
            pltpu.VMEM((8, 8 * w_rows, 2 * rows), jnp.bfloat16),
            pltpu.VMEM((2 * rows, COLS), jnp.bfloat16),
            pltpu.SemaphoreType.DMA((SCATTER_COPIES,)),
            pltpu.SemaphoreType.DMA((SCATTER_COPIES,)),
            pltpu.SemaphoreType.DMA((13,)),
        ],
        compiler_params=pltpu.CompilerParams(collective_id=1, has_side_effects=True),
        name="scatter_grads",
    )(kv_part.reshape(2, 4, 4, 4, rows, COLS), layer_input)


def copy_kernel(a, b, a_out, b_out):
    a_out[...] = a[...]
    b_out[...] = b[...]


def handed_on(a, b):
    vmem = pl.BlockSpec(memory_space=pltpu.VMEM)
    return pl.pallas_call(
        copy_kernel,
        out_shape=[jax.ShapeDtypeStruct(v.shape, v.dtype) for v in (a, b)],
        in_specs=[vmem] * 2,
        out_specs=[vmem] * 2,
        name="handed_on",
    )(a, b)


def per_device(
    layer_input, queries, keys_values, attn_out, out_grad, log_sums, doc_ids, span_order
):
    query_grad, kv_part = window_grads(
        *gather_keys(keys_values, queries, out_grad, attn_out, log_sums, doc_ids, span_order)
    )
    return (query_grad, *handed_on(*scatter_grads(kv_part, layer_input)))


def solution(mesh):
    rows = P(("inner", "outer"), None)
    return jax.shard_map(
        per_device,
        mesh=mesh,
        in_specs=(rows, rows, rows, rows, rows, P(None, ("inner", "outer")), P(), P()),
        out_specs=(rows, rows, rows),
        check_vma=False,
    )
```

```python
import functools

import jax
import jax.numpy as jnp
from jax import lax
from jax.experimental import pallas as pl
from jax.experimental.pallas import tpu as pltpu
from jax.sharding import PartitionSpec as P

CH = 4
SPAN = 64
HD = 128
HEADS = 6
NQ = SPAN * HEADS
MOST_DOC = 2048


def window_kernel(
    tab,
    meta_hbm,
    fmeta_hbm,
    qs_hbm,
    gs_hbm,
    qt_hbm,
    gt_hbm,
    kv_hbm,
    blank,
    dq_hbm,
    dkv_hbm,
    meta,
    fmeta,
    qs,
    gs,
    qt,
    gt,
    dq_ref,
    keys0,
    keys1,
    acc0,
    acc1,
    dq0,
    dq1,
    sc0,
    sc1,
    dp0,
    dp1,
    ds0,
    ds1,
    pb0,
    pb1,
    dqt,
    ksem,
    osem,
    isem,
    *,
    spans,
):
    scale = HD ** (-0.5)
    log2e = 1.4426950408889634
    two = range(2)
    kbuf, acc, dqs = (keys0, keys1), (acc0, acc1), (dq0, dq1)
    sc, dp, ds, pb = (sc0, sc1), (dp0, dp1), (ds0, ds1), (pb0, pb1)
    p = [tab[0, spans + s] for s in two]
    lo = [tab[0, spans + 2 + s] for s in two]
    count = [p[s] - lo[s] + 1 for s in two]
    blocks = (jnp.maximum(count[0], count[1]) + CH - 1) // CH

    def key_copy(s, i):
        c = tab[0, jnp.minimum(lo[s] + i, spans - 1)]
        return pltpu.make_async_copy(
            kv_hbm.at[pl.ds(pl.multiple_of(c * SPAN, SPAN), SPAN)],
            kbuf[s].at[pl.ds(pl.multiple_of(i * SPAN, SPAN), SPAN)],
            ksem.at[s, i],
        )

    @pl.loop(0, blocks * CH)
    def _(i):
        for s in two:
            key_copy(s, i).start()

    sources = (meta_hbm, fmeta_hbm, qs_hbm, gs_hbm, qt_hbm, gt_hbm)
    taken = [
        pltpu.make_async_copy(src, dst, isem.at[k])
        for k, (src, dst) in enumerate(zip(sources, (meta, fmeta, qs, gs, qt, gt)))
    ]
    for copy in taken:
        copy.start()
    for copy in taken:
        copy.wait()
    lane = lax.broadcasted_iota(jnp.int32, (1, NQ), 1)
    delta = [fmeta[pl.ds(s, 1), :] for s in two]
    lse = [fmeta[pl.ds(2 + s, 1), :] * log2e for s in two]
    qpos = [p[s] * SPAN + (lane & (SPAN - 1)) for s in two]
    qstart = [meta[pl.ds(1 + s, 1), pl.ds(0, NQ)] for s in two]
    for s in two:
        dqs[s][...] = jnp.zeros_like(dqs[s])

    def arrive(j):
        for i in range(CH):
            for s in two:
                key_copy(s, j * CH + i).wait()

    def block_rows(j):
        return pl.ds(pl.multiple_of(j * CH * SPAN, CH * SPAN), CH * SPAN)

    def products_in(j, two=two):
        at = block_rows(j)
        for s in two:
            sc[s][...] = jnp.dot(kbuf[s][at, :HD], qt[s], preferred_element_type=jnp.float32)
            dp[s][...] = jnp.dot(kbuf[s][at, HD:], gt[s], preferred_element_type=jnp.float32)

    def weigh(j, two=two):
        part = 16
        row = lax.broadcasted_iota(jnp.int32, (part, NQ), 0)
        for n in range(CH * SPAN // part):
            some = slice(n * part, (n + 1) * part)
            for s in two:
                base = (lo[s] + j * CH) * SPAN + n * part
                keep = (row >= qstart[s] - base) & (row <= qpos[s] - base)
                score = sc[s][some, :] * (scale * log2e) - lse[s]
                prob = jnp.exp2(jnp.where(keep, score, -1e30))
                grad = scale * prob * (dp[s][some, :] - delta[s])
                ds[s][some, :] = grad.astype(jnp.bfloat16)
                pb[s][some, :] = prob.astype(jnp.bfloat16)

    def products_out(j, two=two):
        at = block_rows(j)
        for s in two:
            dk = jnp.dot(ds[s][...], qs[s], preferred_element_type=jnp.float32)
            dv = jnp.dot(pb[s][...], gs[s], preferred_element_type=jnp.float32)
            acc[s][at, :HD] = dk.astype(jnp.bfloat16)
            acc[s][at, HD:] = dv.astype(jnp.bfloat16)
            dqs[s][...] += lax.dot_general(
                kbuf[s][at, :HD],
                ds[s][...],
                (((0,), (0,)), ((), ())),
                preferred_element_type=jnp.float32,
            )

    for s in two:
        ds[s][...] = jnp.zeros_like(ds[s])
        pb[s][...] = jnp.zeros_like(pb[s])
    arrive(0)
    products_in(0)

    @pl.loop(0, blocks)
    def _(j):
        @pl.when(j + 1 < blocks)
        def _():
            arrive(j + 1)

        for s in two:
            products_out(jnp.maximum(j - 1, 0), (s,))
            weigh(j, (s,))
            products_in(jnp.minimum(j + 1, blocks - 1), (s,))

    products_out(blocks - 1)

    def out_copy(s, i):
        c = tab[0, lo[s] + i]
        return pltpu.make_async_copy(
            acc[s].at[rows_of(i)],
            dkv_hbm.at[pl.ds(pl.multiple_of(c * SPAN, SPAN), SPAN)],
            osem.at[s, i],
        )

    def rows_of(i):
        return pl.ds(pl.multiple_of(i * SPAN, SPAN), SPAN)

    def shared(s, i):
        other = lo[s] + i - lo[1 - s]
        return other, (other >= 0) & (other < count[1 - s])

    @pl.loop(0, count[0])
    def _(i):
        other, both = shared(0, i)

        @pl.when(both)
        def _():
            term = acc0[rows_of(i), :].astype(jnp.float32) + acc1[rows_of(other), :].astype(jnp.float32)
            acc0[rows_of(i), :] = term.astype(jnp.bfloat16)

        out_copy(0, i).start()

    @pl.loop(0, count[1])
    def _(i):
        @pl.when(jnp.logical_not(shared(1, i)[1]))
        def _():
            out_copy(1, i).start()

    for s in two:
        dqt[...] = dqs[s][...].T
        for h in range(HEADS):
            dq_ref[s * SPAN : (s + 1) * SPAN, h * HD : (h + 1) * HD] = dqt[
                h * SPAN : (h + 1) * SPAN, :
            ].astype(dq_ref.dtype)
    dq_out = pltpu.make_async_copy(dq_ref, dq_hbm, isem.at[6])
    dq_out.start()

    @pl.loop(0, count[0])
    def _(i):
        out_copy(0, i).wait()

    @pl.loop(0, count[1])
    def _(i):
        @pl.when(jnp.logical_not(shared(1, i)[1]))
        def _():
            out_copy(1, i).wait()

    dq_out.wait()


def window_grads(meta, fmeta, qs, gs, qt, gt, kv_all, blank):
    tokens = kv_all.shape[0]
    spans = tokens // SPAN
    wmax = MOST_DOC // SPAN + 1
    wmax = -(-wmax // CH) * CH
    anyspace = pl.BlockSpec(memory_space=pl.ANY)
    return pl.pallas_call(
        functools.partial(window_kernel, spans=spans),
        out_shape=(
            jax.ShapeDtypeStruct((2 * SPAN, HEADS * HD), jnp.bfloat16),
            jax.ShapeDtypeStruct((tokens, 2 * HD), jnp.bfloat16),
        ),
        in_specs=[pl.BlockSpec(memory_space=pltpu.SMEM)] + [anyspace] * 8,
        input_output_aliases={8: 1},
        out_specs=(anyspace, anyspace),
        scratch_shapes=[pltpu.VMEM(v.shape, v.dtype) for v in (meta, fmeta, qs, gs, qt, gt)]
        + [
            pltpu.VMEM((2 * SPAN, HEADS * HD), jnp.bfloat16),
            *[pltpu.VMEM((wmax * SPAN, 2 * HD), jnp.bfloat16)] * 4,
            pltpu.VMEM((HD, NQ), jnp.float32),
            pltpu.VMEM((HD, NQ), jnp.float32),
            *[pltpu.VMEM((CH * SPAN, NQ), jnp.float32)] * 4,
            *[pltpu.VMEM((CH * SPAN, NQ), jnp.bfloat16)] * 4,
            pltpu.VMEM((NQ, HD), jnp.float32),
            pltpu.SemaphoreType.DMA((2, wmax)),
            pltpu.SemaphoreType.DMA((2, wmax)),
            pltpu.SemaphoreType.DMA((7,)),
        ],
        name="window_grads",
    )(meta, meta, fmeta, qs, gs, qt, gt, kv_all, blank)


def prepare(q_ref, og_ref, ao_ref, lse_ref, doc_ref, order_ref, qs, gs, qt, gt, meta, fmeta, tmp):
    spans = order_ref.shape[0] * order_ref.shape[1]
    order = jnp.concatenate([order_ref[0:1, :], order_ref[1:2, :]], axis=1).astype(jnp.float32)
    stored = jnp.broadcast_to(order, (spans, spans)).T
    lanes = lax.broadcasted_iota(jnp.int32, (spans, spans), 1).astype(jnp.float32)
    c = lax.broadcasted_iota(jnp.int32, (spans, spans), 0)
    kept = (
        ((c >> 4) & 1) * 128
        + (((c >> 3) & 1) * 2 + ((c >> 7) & 1)) * 32
        + ((c >> 5) & 3) * 8
        + ((c >> 1) & 3) * 2
        + (c & 1)
    ).astype(jnp.float32)
    inverse = jnp.sum(jnp.where(stored == lanes, kept, 0.0), axis=0, keepdims=True)
    docs = doc_ref[...]
    counts = [
        jnp.sum(jnp.where(docs < d, 1.0, 0.0), axis=0, keepdims=True) for d in range(16)
    ]
    first = jnp.sum(jnp.concatenate(counts, axis=0), axis=1, keepdims=True)
    mine = 2 * (lax.axis_index("inner") * 8 + lax.axis_index("outer"))
    spot = lax.broadcasted_iota(jnp.int32, (1, spans), 1)
    lane = lax.broadcasted_iota(jnp.int32, (1, NQ), 1)
    tail = jnp.zeros((1, spans), jnp.float32)
    for s in range(2):
        span = jnp.sum(jnp.where(spot == mine + s, order, 0.0), axis=1, keepdims=True)
        pos = span * SPAN + (lane & (SPAN - 1)).astype(jnp.float32)
        start = jnp.max(jnp.where(first <= pos, first, 0.0), axis=0, keepdims=True)
        low = (start[:, :1].astype(jnp.int32) >> 6).astype(jnp.float32)
        tail = jnp.where(spot == s, span, jnp.where(spot == 2 + s, low, tail))
        meta[1 + s : 2 + s, 0:NQ] = start.astype(jnp.int32)
    meta[0:1, 0:spans] = inverse.astype(jnp.int32)
    meta[0:1, spans:] = tail.astype(jnp.int32)
    for s in range(2):
        rows = slice(s * SPAN, (s + 1) * SPAN)
        for h in range(HEADS):
            cols = slice(h * HD, (h + 1) * HD)
            dst = slice(h * SPAN, (h + 1) * SPAN)
            qs[s, dst, :] = q_ref[rows, cols]
            gs[s, dst, :] = og_ref[rows, cols]
            tmp[dst, :] = og_ref[rows, cols].astype(jnp.float32) * ao_ref[rows, cols].astype(
                jnp.float32
            )
        fmeta[s : s + 1, :] = jnp.sum(tmp[...].T, axis=0, keepdims=True)
        fmeta[2 + s : 3 + s, :] = jnp.concatenate(
            [lse_ref[h : h + 1, rows] for h in range(HEADS)], axis=1
        )
        qt[s] = qs[s].T
        gt[s] = gs[s].T


ORDERS = (("x", "y", "z"), ("y", "z", "x"), ("z", "x", "y"))
COLS = 2 * HD
HALF = {1: pl.ds(0, HD), -1: pl.ds(HD, HD)}
FULL = pl.ds(0, COLS)


def here():
    i, o = lax.axis_index("inner"), lax.axis_index("outer")
    return {"x": (o // 4) * 2 + i // 8, "y": o % 4, "z": (i // 2) % 4, "core": i % 2}


def device(c):
    return ((c["x"] % 2) * 8 + c["z"] * 2 + c["core"], (c["x"] // 2) * 4 + c["y"])


def moved(c, axis, by):
    out = dict(c)
    out[axis] = (c[axis] + by + 4) % 4
    return out


def place(sel, core=None):
    where = tuple(slice(None) if sel[a] is None else sel[a] for a in "xzy")
    return where if core is None else (core, *where)


def row_parts(rows):
    first = -(-rows // 3 // 16) * 16
    sizes = (first, first, rows - 2 * first)
    return [(sum(sizes[:i]), sizes[i]) for i in range(3)]


class Copies:
    def __init__(self, send_sem, recv_sem):
        self.send_sem, self.recv_sem, self.all = send_sem, recv_sem, []

    def send(self, src, dst, target):
        k = len(self.all)
        copy = pltpu.make_async_remote_copy(
            src_ref=src,
            dst_ref=dst,
            send_sem=self.send_sem.at[k],
            recv_sem=self.recv_sem.at[k],
            device_id=device(target),
            device_id_type=pl.DeviceIdType.MESH,
        )
        copy.start()
        self.all.append(copy)
        return copy

    def drain(self):
        for copy in self.all:
            copy.wait_send()


def meet(me):
    barrier = pltpu.get_barrier_semaphore()
    partner = dict(me, core=1 - me["core"])
    others = [moved(me, a, d) for a in "xyz" for d in (1, -1, 2)] + [partner]
    for other in others:
        pl.semaphore_signal(
            barrier, inc=1, device_id=device(other), device_id_type=pl.DeviceIdType.MESH
        )
    pl.semaphore_wait(barrier, len(others))
    return partner


GATHER_COPIES = 3 * (3 + 4 + 16 + 16)


def gather_kernel(kv_ref, *refs):
    sources, targets, out, blank = refs[:6], refs[6:12], refs[12], refs[13]
    held, made = refs[14:20], refs[20:26]
    tmp, zeros, send_sem, recv_sem, own_sem, small_sem, zero_sem = refs[26:]
    zrows = zeros.shape[0]
    wiped = [
        pltpu.make_async_copy(zeros, blank.at[pl.ds(k * zrows, zrows)], zero_sem.at[k])
        for k in range(blank.shape[0] // zrows)
    ]
    taken = [
        pltpu.make_async_copy(sources[k], held[k], small_sem.at[k]) for k in range(6)
    ]
    given = [
        pltpu.make_async_copy(made[k], targets[k], small_sem.at[6 + k]) for k in range(6)
    ]
    for copy in taken:
        copy.start()
    me = here()
    core = me["core"]
    own = pltpu.make_async_copy(kv_ref, out.at[place(me, core)], own_sem)
    own.start()
    partner = meet(me)
    net = Copies(send_sem, recv_sem)
    parts = row_parts(kv_ref.shape[0])

    def block(part, sel, cols=FULL):
        return out.at[(*place(sel, core), pl.ds(*parts[part]), cols)]

    def push(part, sel, axis, by, cols=FULL, src=None):
        ref = block(part, sel, cols)
        return net.send(ref if src is None else src, ref, moved(me, axis, by))

    across = []

    def cross(part, sel):
        ref = block(part, sel)
        across.append(net.send(ref, ref, partner))

    def both(part, sel, axis):
        return {d: push(part, sel, axis, d) for d in (1, -1)}

    def relay(part, sel, axis, copies):
        out_copies = {}
        for d in (1, -1):
            copies[d].wait_recv()
            got = dict(sel, **{axis: moved(me, axis, -d)[axis]})
            out_copies[d] = push(part, got, axis, d, HALF[d])
            cross(part, got)
        return out_copies

    def settle(copies):
        for copy in copies.values():
            copy.wait_recv()

    colors = range(3)
    mine = {a: me[a] for a in "xyz"}
    first = [
        {
            d: push(i, mine, ORDERS[i][0], d, src=kv_ref.at[pl.ds(*parts[i]), :])
            for d in (2, 1, -1)
        }
        for i in colors
    ]
    for copy in taken:
        copy.wait()
    prepare(*held, *made, tmp)
    for copy in given:
        copy.start()
    zeros[...] = jnp.zeros_like(zeros)
    for copy in wiped:
        copy.start()
    own.wait()
    line = [dict(mine, **{ORDERS[i][0]: None}) for i in colors]
    plane = []
    wave = [{} for i in colors]
    last = [{} for i in colors]

    def piece(i, by):
        return dict(line[i], **{ORDERS[i][1]: moved(me, ORDERS[i][1], by)[ORDERS[i][1]]})

    for i in colors:
        settle(first[i])
        plane.append(both(i, line[i], ORDERS[i][1]))
    for i in colors:
        wave[i][0] = both(i, piece(i, 0), ORDERS[i][2])
    for i in colors:
        cross(i, line[i])
    turn = [{} for i in colors]
    for by in (1, -1):
        for i in colors:
            a2 = ORDERS[i][1]
            plane[i][-by].wait_recv()
            turn[i][-by] = push(i, piece(i, by), a2, -by, HALF[-by])
    for by in (1, -1):
        for i in colors:
            wave[i][by] = both(i, piece(i, by), ORDERS[i][2])
            cross(i, piece(i, by))
    last0 = [relay(i, piece(i, 0), ORDERS[i][2], wave[i][0]) for i in colors]
    for i in colors:
        last[i][0] = last0[i]
        settle(turn[i])
        wave[i][2] = both(i, piece(i, 2), ORDERS[i][2])
        cross(i, piece(i, 2))
    for by in (1, -1, 2):
        for i in colors:
            last[i][by] = relay(i, piece(i, by), ORDERS[i][2], wave[i][by])
    for by in (0, 1, -1, 2):
        for i in colors:
            settle(last[i][by])
            a3 = ORDERS[i][2]
            cross(i, dict(piece(i, by), **{a3: moved(me, a3, 2)[a3]}))
    for copy in across:
        copy.wait_recv()
    for copy in given + wiped:
        copy.wait()
    net.drain()


def gather_keys(keys_values, queries, out_grad, attn_out, log_sums, doc_ids, span_order):
    rows = keys_values.shape[0]
    vmem = pl.BlockSpec(memory_space=pltpu.VMEM)
    anyspace = pl.BlockSpec(memory_space=pl.ANY)
    sources = (
        queries,
        out_grad,
        attn_out,
        log_sums,
        doc_ids.reshape(-1, 128),
        span_order.reshape(-1, 128),
    )
    made = [
        ((2, NQ, HD), jnp.bfloat16),
        ((2, NQ, HD), jnp.bfloat16),
        ((2, HD, NQ), jnp.bfloat16),
        ((2, HD, NQ), jnp.bfloat16),
        ((8, 2 * span_order.shape[0]), jnp.int32),
        ((8, NQ), jnp.float32),
    ]
    *small, out, blank = pl.pallas_call(
        gather_kernel,
        out_shape=(
            *[jax.ShapeDtypeStruct(*m) for m in made],
            jax.ShapeDtypeStruct((2, 4, 4, 4, rows, COLS), keys_values.dtype),
            jax.ShapeDtypeStruct((128 * rows, COLS), jnp.bfloat16),
        ),
        in_specs=[vmem] + [anyspace] * 6,
        out_specs=[anyspace] * 8,
        scratch_shapes=[pltpu.VMEM(v.shape, v.dtype) for v in sources]
        + [pltpu.VMEM(*m) for m in made]
        + [
            pltpu.VMEM((NQ, HD), jnp.float32),
            pltpu.VMEM((1024, COLS), jnp.bfloat16),
            pltpu.SemaphoreType.DMA((GATHER_COPIES,)),
            pltpu.SemaphoreType.DMA((GATHER_COPIES,)),
            pltpu.SemaphoreType.DMA,
            pltpu.SemaphoreType.DMA((12,)),
            pltpu.SemaphoreType.DMA((128 * rows // 1024,)),
        ],
        compiler_params=pltpu.CompilerParams(collective_id=0, has_side_effects=True),
        name="gather_keys",
    )(keys_values, *sources)
    qs, gs, qt, gt, meta, fmeta = small
    return meta, fmeta, qs, gs, qt, gt, out.reshape(128 * rows, COLS), blank


KEYS = (2, 1, -1, 0)
AWAY = (2, 1, -1)


class Scatter:
    def __init__(self, me, net, mine, other, third, second, first, halves, rows):
        self.me, self.net, self.mine, self.other, self.halves = me, net, mine, other, halves
        self.buffers = {3: third, 2: second, 1: first}
        self.parts = row_parts(rows)
        self.spot = {a: me[a] for a in "xyz"}
        self.flight = {}

    def at(self, i, d1, d2, d3):
        sel = dict(self.spot)
        for a, d in zip(ORDERS[i], (d1, d2, d3)):
            sel[a] = None if d is None else moved(self.me, a, d)[a]
        return sel

    def ix(self, i, sel, cols=FULL):
        return (*place(sel), pl.ds(*self.parts[i]), cols)

    def level_sel(self, level, i, key, d):
        return {3: self.at(i, None, key, d), 2: self.at(i, None, d, 0), 1: self.at(i, d, 0, 0)}[level]

    def blocks(self, level, i, key, d):
        sel = self.level_sel(level, i, key, d)
        if level == 1:
            return [((), sel)]
        return [((v,), dict(sel, **{ORDERS[i][0]: v})) for v in range(4)]

    def lead(self, level, i, key, d):
        side = AWAY.index(d)
        return (i, KEYS.index(key), side) if level == 3 else (i, side)

    def slot(self, buf, level, i, key, d):
        lines = () if level == 1 else (slice(None),)
        return buf.at[(*self.lead(level, i, key, d), *lines, pl.ds(0, self.parts[i][1]), slice(None))]

    def row(self, level, i, key, d, v):
        return (*self.lead(level, i, key, d), *v, pl.ds(0, self.parts[i][1]), slice(None))

    def send(self, level, i, key, d):
        src = self.mine.at[self.ix(i, self.level_sel(level, i, key, d))]
        dst = self.slot(self.buffers[level], level, i, key, d)
        to = moved(self.me, ORDERS[i][level - 1], d)
        self.flight[level, i, key, d] = self.net.send(src, dst, to)

    def add_core(self, i, d2, d3):
        self.arrived(i, d2, d3)
        for _, sel in self.blocks(3, i, d2, d3):
            ix = self.ix(i, sel)
            self.mine[ix] = self.mine[ix] + self.other[ix]

    def part_ways(self, level, i, key):
        sel = self.level_sel(level, i, key, 2)
        for d in (1, -1):
            dst = self.slot(self.halves[level], level, i, key, d)
            src = self.mine.at[self.ix(i, sel, HALF[d])]
            to = moved(self.me, ORDERS[i][level - 1], d)
            self.flight["half", level, i, key, d] = self.net.send(src, dst, to)

    def join(self, level, i, key, d):
        self.flight["half", level, i, key, d].wait_recv()
        for v, sel in self.blocks(level, i, key, d):
            ix = self.ix(i, sel, HALF[d])
            self.mine[ix] = self.mine[ix] + self.halves[level][self.row(level, i, key, d, v)]
        self.send(level, i, key, d)

    def open(self, i, key):
        if 3 not in self.halves:
            for d in AWAY:
                self.send(3, i, key, d)
            return
        if self.other is not None:
            self.add_core(i, key, 2)
        self.part_ways(3, i, key)
        if self.other is not None:
            self.add_core(i, key, 1)
            self.add_core(i, key, -1)

    def close(self, level, i, key=0, write=None):
        sides = (1, -1) if level in self.halves else AWAY
        if level == 3 and self.other is not None:
            self.arrived(i, key, 0)
        for d in sides:
            self.flight[level, i, key, d].wait_recv()
        for v, sel in self.blocks(level, i, key, 0):
            ix = self.ix(i, sel)
            total = self.mine[ix].astype(jnp.float32)
            if level == 3 and self.other is not None:
                total = total + self.other[ix].astype(jnp.float32)
            for d in sides:
                total = total + self.buffers[level][self.row(level, i, key, d, v)].astype(jnp.float32)
            if write is None:
                self.mine[ix] = total.astype(self.mine.dtype)
            else:
                write(self.parts[i], total)

    def finish(self, i, key):
        self.close(3, i, key)
        if key == 0:
            return
        if 2 not in self.halves:
            self.send(2, i, 0, key)
        elif key == 2:
            self.part_ways(2, i, 0)
        else:
            self.join(2, i, 0, key)

    def run(self, ready, write, aside):
        colors = range(3)
        lag = 2 if 3 in self.halves else 1
        for n in range(len(KEYS) + lag):
            if n < len(KEYS):
                for i in colors:
                    ready(i, KEYS[n])
                    self.open(i, KEYS[n])
            if lag == 2 and 1 <= n <= len(KEYS):
                for i in colors:
                    for d in (1, -1):
                        self.join(3, i, KEYS[n - 1], d)
            if n == len(KEYS) - 1:
                aside()
            if n >= lag:
                for i in colors:
                    self.finish(i, KEYS[n - lag])
        for i in colors:
            self.close(2, i)
            for d in AWAY:
                self.send(1, i, 0, d)
        for i in colors:
            self.close(1, i, write=write)


def scatter_scratch(rows, planes, relayed):
    top = row_parts(rows)[0][1]
    return (
        [pltpu.VMEM((4, 4, 4, rows, COLS), jnp.bfloat16)] * planes
        + [
            pltpu.VMEM((3, 4, 3, 4, top, COLS), jnp.bfloat16),
            pltpu.VMEM((3, 3, 4, top, COLS), jnp.bfloat16),
            pltpu.VMEM((3, 3, top, COLS), jnp.bfloat16),
        ]
        + [
            pltpu.VMEM((3, 4, 3, 4, top, HD) if level == 3 else (3, 3, 4, top, HD), jnp.bfloat16)
            for level in relayed
        ]
    )


KV_RELAYED = (3, 2)
W_RELAYED = ()
SCATTER_COPIES = 2 * 3 * (4 * 4 + 4 + 3) + 21 + 8 + 1


def scatter_kernel(part_ref, x_ref, kv_out, w_out, *scratch):
    kv_end = 5 + len(KV_RELAYED)
    w_end = kv_end + 4 + len(W_RELAYED)
    kv_bufs, w_bufs = scratch[:kv_end], scratch[kv_end:w_end]
    x_buf, x_theirs, xt, pair, send_sem, recv_sem, load_sem = scratch[w_end:]
    x_load = pltpu.make_async_copy(x_ref, x_buf, load_sem.at[12])
    me = here()
    core = me["core"]
    rows, w_rows = kv_out.shape[0], w_out.shape[0]
    wide = 8 * w_rows
    net = Copies(send_sem, recv_sem)
    job = Scatter(me, net, *kv_bufs[:5], dict(zip(KV_RELAYED, kv_bufs[5:])), rows)
    w_job = Scatter(me, net, w_bufs[0], None, *w_bufs[1:4], dict(zip(W_RELAYED, w_bufs[4:])), w_rows)
    loads, swaps = {}, {}
    for n, key in enumerate(KEYS):
        for i in range(3):
            sel = job.at(i, None, key, None)
            src = part_ref.at[(*place(sel, core), pl.ds(*job.parts[i]), FULL)]
            dst = job.mine.at[job.ix(i, sel)]
            loads[i, key] = pltpu.make_async_copy(src, dst, load_sem.at[3 * n + i])
            loads[i, key].start()
    x_load.start()
    partner = meet(me)
    for key in KEYS:
        for d in KEYS if key == KEYS[0] else (None,):
            for i in range(3):
                sel = job.at(i, None, key, d)
                src = part_ref.at[(*place(sel, 1 - core), pl.ds(*job.parts[i]), FULL)]
                swaps[i, key, d] = net.send(src, job.other.at[job.ix(i, sel)], partner)

    def arrived(i, key, d):
        copy = swaps.pop((i, key, d if key == KEYS[0] else None), None)
        if copy is not None:
            copy.wait_recv()

    job.arrived = arrived

    def columns(j, which):
        first = (j // 4 * 8 + j % 4 * 2 + which) * wide
        return x_buf.at[:, pl.ds(pl.multiple_of(first, 128), wide)]

    x_load.wait()
    x_swaps = [net.send(columns(j, 1 - core), x_theirs.at[j], partner) for j in range(8)]
    for j in range(8):
        xt[j, :, :rows] = columns(j, core)[...].T

    def ready(i, key):
        loads[i, key].wait()

    def turn_inputs():
        for j in range(8):
            x_swaps[j].wait_recv()
            xt[j, :, rows:] = x_theirs[j].T

    def write(part, total):
        low = total.astype(kv_out.dtype)
        kv_out[pl.ds(*part), :] = low
        pair[pl.ds(*part), :] = low

    job.run(ready, write, turn_inputs)

    swap = net.send(pair.at[pl.ds(0, rows)], pair.at[pl.ds(rows, rows)], partner)
    swap.wait_recv()
    both = pair[...]
    for j in range(8):
        out = jnp.dot(xt[j], both, preferred_element_type=jnp.float32).astype(jnp.bfloat16)
        for xh in range(2):
            for y in range(4):
                first = (xh * 4 + y) * w_rows
                w_job.mine[2 * xh + j // 4, j % 4, y] = out[first : first + w_rows]

    def w_write(part, total):
        w_out[pl.ds(*part), :] = total

    w_job.run(lambda i, key: None, w_write, lambda: None)
    net.drain()


def scatter_grads(kv_part, layer_input):
    tokens, width = kv_part.shape[0], layer_input.shape[1]
    rows, w_rows = tokens // 128, width // 128
    vmem = pl.BlockSpec(memory_space=pltpu.VMEM)
    return pl.pallas_call(
        scatter_kernel,
        out_shape=(
            jax.ShapeDtypeStruct((rows, COLS), jnp.bfloat16),
            jax.ShapeDtypeStruct((w_rows, COLS), jnp.float32),
        ),
        in_specs=[pl.BlockSpec(memory_space=pl.ANY)] * 2,
        out_specs=(vmem, vmem),
        scratch_shapes=scatter_scratch(rows, 2, KV_RELAYED)
        + scatter_scratch(w_rows, 1, W_RELAYED)
        + [
            pltpu.VMEM((rows, width), jnp.bfloat16),
            pltpu.VMEM((8, rows, 8 * w_rows), jnp.bfloat16),
            pltpu.VMEM((8, 8 * w_rows, 2 * rows), jnp.bfloat16),
            pltpu.VMEM((2 * rows, COLS), jnp.bfloat16),
            pltpu.SemaphoreType.DMA((SCATTER_COPIES,)),
            pltpu.SemaphoreType.DMA((SCATTER_COPIES,)),
            pltpu.SemaphoreType.DMA((13,)),
        ],
        compiler_params=pltpu.CompilerParams(collective_id=1, has_side_effects=True),
        name="scatter_grads",
    )(kv_part.reshape(2, 4, 4, 4, rows, COLS), layer_input)


def copy_kernel(a, b, a_out, b_out):
    a_out[...] = a[...]
    b_out[...] = b[...]


def handed_on(a, b):
    vmem = pl.BlockSpec(memory_space=pltpu.VMEM)
    return pl.pallas_call(
        copy_kernel,
        out_shape=[jax.ShapeDtypeStruct(v.shape, v.dtype) for v in (a, b)],
        in_specs=[vmem] * 2,
        out_specs=[vmem] * 2,
        name="handed_on",
    )(a, b)


def per_device(
    layer_input, queries, keys_values, attn_out, out_grad, log_sums, doc_ids, span_order
):
    query_grad, kv_part = window_grads(
        *gather_keys(keys_values, queries, out_grad, attn_out, log_sums, doc_ids, span_order)
    )
    return (query_grad, *handed_on(*scatter_grads(kv_part, layer_input)))


def solution(mesh):
    rows = P(("inner", "outer"), None)
    return jax.shard_map(
        per_device,
        mesh=mesh,
        in_specs=(rows, rows, rows, rows, rows, P(None, ("inner", "outer")), P(), P()),
        out_specs=(rows, rows, rows),
        check_vma=False,
    )
```

```python
import functools

import jax
import jax.numpy as jnp
from jax import lax
from jax.experimental import pallas as pl
from jax.experimental.pallas import tpu as pltpu
from jax.sharding import PartitionSpec as P

CH = 4
SPAN = 64
HD = 128
HEADS = 6
NQ = SPAN * HEADS
MOST_DOC = 2048


def window_kernel(
    tab,
    meta_hbm,
    fmeta_hbm,
    qs_hbm,
    gs_hbm,
    qt_hbm,
    gt_hbm,
    kv_hbm,
    blank,
    dq_hbm,
    dkv_hbm,
    meta,
    fmeta,
    qs,
    gs,
    qt,
    gt,
    dq_ref,
    keys0,
    keys1,
    acc0,
    acc1,
    dq0,
    dq1,
    sc0,
    sc1,
    dp0,
    dp1,
    ds0,
    ds1,
    pb0,
    pb1,
    dqt,
    ksem,
    osem,
    isem,
    *,
    spans,
):
    scale = HD ** (-0.5)
    log2e = 1.4426950408889634
    two = range(2)
    kbuf, acc, dqs = (keys0, keys1), (acc0, acc1), (dq0, dq1)
    sc, dp, ds, pb = (sc0, sc1), (dp0, dp1), (ds0, ds1), (pb0, pb1)
    p = [tab[0, spans + s] for s in two]
    lo = [tab[0, spans + 2 + s] for s in two]
    count = [p[s] - lo[s] + 1 for s in two]
    blocks = (jnp.maximum(count[0], count[1]) + CH - 1) // CH

    def key_copy(s, i):
        c = tab[0, jnp.minimum(lo[s] + i, spans - 1)]
        return pltpu.make_async_copy(
            kv_hbm.at[pl.ds(pl.multiple_of(c * SPAN, SPAN), SPAN)],
            kbuf[s].at[pl.ds(pl.multiple_of(i * SPAN, SPAN), SPAN)],
            ksem.at[s, i],
        )

    @pl.loop(0, blocks * CH)
    def _(i):
        for s in two:
            key_copy(s, i).start()

    sources = (meta_hbm, fmeta_hbm, qs_hbm, gs_hbm, qt_hbm, gt_hbm)
    taken = [
        pltpu.make_async_copy(src, dst, isem.at[k])
        for k, (src, dst) in enumerate(zip(sources, (meta, fmeta, qs, gs, qt, gt)))
    ]
    for copy in taken:
        copy.start()
    for copy in taken:
        copy.wait()
    lane = lax.broadcasted_iota(jnp.int32, (1, NQ), 1)
    delta = [fmeta[pl.ds(s, 1), :] for s in two]
    lse = [fmeta[pl.ds(2 + s, 1), :] * log2e for s in two]
    qpos = [p[s] * SPAN + (lane & (SPAN - 1)) for s in two]
    qstart = [meta[pl.ds(1 + s, 1), pl.ds(0, NQ)] for s in two]
    for s in two:
        dqs[s][...] = jnp.zeros_like(dqs[s])

    def arrive(j):
        for i in range(CH):
            for s in two:
                key_copy(s, j * CH + i).wait()

    def block_rows(j):
        return pl.ds(pl.multiple_of(j * CH * SPAN, CH * SPAN), CH * SPAN)

    def products_in(j, two=two):
        at = block_rows(j)
        for s in two:
            sc[s][...] = jnp.dot(kbuf[s][at, :HD], qt[s], preferred_element_type=jnp.float32)
            dp[s][...] = jnp.dot(kbuf[s][at, HD:], gt[s], preferred_element_type=jnp.float32)

    def weigh(j, two=two):
        part = 32
        row = lax.broadcasted_iota(jnp.int32, (part, NQ), 0)
        for n in range(CH * SPAN // part):
            some = slice(n * part, (n + 1) * part)
            for s in two:
                base = (lo[s] + j * CH) * SPAN + n * part
                keep = (row >= qstart[s] - base) & (row <= qpos[s] - base)
                score = sc[s][some, :] * (scale * log2e) - lse[s]
                prob = jnp.exp2(jnp.where(keep, score, -1e30))
                grad = scale * prob * (dp[s][some, :] - delta[s])
                ds[s][some, :] = grad.astype(jnp.bfloat16)
                pb[s][some, :] = prob.astype(jnp.bfloat16)

    def products_out(j, two=two):
        at = block_rows(j)
        for s in two:
            dk = jnp.dot(ds[s][...], qs[s], preferred_element_type=jnp.float32)
            dv = jnp.dot(pb[s][...], gs[s], preferred_element_type=jnp.float32)
            acc[s][at, :HD] = dk.astype(jnp.bfloat16)
            acc[s][at, HD:] = dv.astype(jnp.bfloat16)
            dqs[s][...] += lax.dot_general(
                kbuf[s][at, :HD],
                ds[s][...],
                (((0,), (0,)), ((), ())),
                preferred_element_type=jnp.float32,
            )

    for s in two:
        ds[s][...] = jnp.zeros_like(ds[s])
        pb[s][...] = jnp.zeros_like(pb[s])
    arrive(0)
    products_in(0)

    @pl.loop(0, blocks)
    def _(j):
        @pl.when(j + 1 < blocks)
        def _():
            arrive(j + 1)

        for s in two:
            products_out(jnp.maximum(j - 1, 0), (s,))
            weigh(j, (s,))
            products_in(jnp.minimum(j + 1, blocks - 1), (s,))

    products_out(blocks - 1)

    def out_copy(s, i):
        c = tab[0, lo[s] + i]
        return pltpu.make_async_copy(
            acc[s].at[rows_of(i)],
            dkv_hbm.at[pl.ds(pl.multiple_of(c * SPAN, SPAN), SPAN)],
            osem.at[s, i],
        )

    def rows_of(i):
        return pl.ds(pl.multiple_of(i * SPAN, SPAN), SPAN)

    def shared(s, i):
        other = lo[s] + i - lo[1 - s]
        return other, (other >= 0) & (other < count[1 - s])

    @pl.loop(0, count[0])
    def _(i):
        other, both = shared(0, i)

        @pl.when(both)
        def _():
            term = acc0[rows_of(i), :].astype(jnp.float32) + acc1[rows_of(other), :].astype(jnp.float32)
            acc0[rows_of(i), :] = term.astype(jnp.bfloat16)

        out_copy(0, i).start()

    @pl.loop(0, count[1])
    def _(i):
        @pl.when(jnp.logical_not(shared(1, i)[1]))
        def _():
            out_copy(1, i).start()

    for s in two:
        dqt[...] = dqs[s][...].T
        for h in range(HEADS):
            dq_ref[s * SPAN : (s + 1) * SPAN, h * HD : (h + 1) * HD] = dqt[
                h * SPAN : (h + 1) * SPAN, :
            ].astype(dq_ref.dtype)
    dq_out = pltpu.make_async_copy(dq_ref, dq_hbm, isem.at[6])
    dq_out.start()

    @pl.loop(0, count[0])
    def _(i):
        out_copy(0, i).wait()

    @pl.loop(0, count[1])
    def _(i):
        @pl.when(jnp.logical_not(shared(1, i)[1]))
        def _():
            out_copy(1, i).wait()

    dq_out.wait()


def window_grads(meta, fmeta, qs, gs, qt, gt, kv_all, blank):
    tokens = kv_all.shape[0]
    spans = tokens // SPAN
    wmax = MOST_DOC // SPAN + 1
    wmax = -(-wmax // CH) * CH
    anyspace = pl.BlockSpec(memory_space=pl.ANY)
    return pl.pallas_call(
        functools.partial(window_kernel, spans=spans),
        out_shape=(
            jax.ShapeDtypeStruct((2 * SPAN, HEADS * HD), jnp.bfloat16),
            jax.ShapeDtypeStruct((tokens, 2 * HD), jnp.bfloat16),
        ),
        in_specs=[pl.BlockSpec(memory_space=pltpu.SMEM)] + [anyspace] * 8,
        input_output_aliases={8: 1},
        out_specs=(anyspace, anyspace),
        scratch_shapes=[pltpu.VMEM(v.shape, v.dtype) for v in (meta, fmeta, qs, gs, qt, gt)]
        + [
            pltpu.VMEM((2 * SPAN, HEADS * HD), jnp.bfloat16),
            *[pltpu.VMEM((wmax * SPAN, 2 * HD), jnp.bfloat16)] * 4,
            pltpu.VMEM((HD, NQ), jnp.float32),
            pltpu.VMEM((HD, NQ), jnp.float32),
            *[pltpu.VMEM((CH * SPAN, NQ), jnp.float32)] * 4,
            *[pltpu.VMEM((CH * SPAN, NQ), jnp.bfloat16)] * 4,
            pltpu.VMEM((NQ, HD), jnp.float32),
            pltpu.SemaphoreType.DMA((2, wmax)),
            pltpu.SemaphoreType.DMA((2, wmax)),
            pltpu.SemaphoreType.DMA((7,)),
        ],
        name="window_grads",
    )(meta, meta, fmeta, qs, gs, qt, gt, kv_all, blank)


def prepare(q_ref, og_ref, ao_ref, lse_ref, doc_ref, order_ref, qs, gs, qt, gt, meta, fmeta, tmp):
    spans = order_ref.shape[0] * order_ref.shape[1]
    order = jnp.concatenate([order_ref[0:1, :], order_ref[1:2, :]], axis=1).astype(jnp.float32)
    stored = jnp.broadcast_to(order, (spans, spans)).T
    lanes = lax.broadcasted_iota(jnp.int32, (spans, spans), 1).astype(jnp.float32)
    c = lax.broadcasted_iota(jnp.int32, (spans, spans), 0)
    kept = (
        ((c >> 4) & 1) * 128
        + (((c >> 3) & 1) * 2 + ((c >> 7) & 1)) * 32
        + ((c >> 5) & 3) * 8
        + ((c >> 1) & 3) * 2
        + (c & 1)
    ).astype(jnp.float32)
    inverse = jnp.sum(jnp.where(stored == lanes, kept, 0.0), axis=0, keepdims=True)
    docs = doc_ref[...]
    counts = [
        jnp.sum(jnp.where(docs < d, 1.0, 0.0), axis=0, keepdims=True) for d in range(16)
    ]
    first = jnp.sum(jnp.concatenate(counts, axis=0), axis=1, keepdims=True)
    mine = 2 * (lax.axis_index("inner") * 8 + lax.axis_index("outer"))
    spot = lax.broadcasted_iota(jnp.int32, (1, spans), 1)
    lane = lax.broadcasted_iota(jnp.int32, (1, NQ), 1)
    tail = jnp.zeros((1, spans), jnp.float32)
    for s in range(2):
        span = jnp.sum(jnp.where(spot == mine + s, order, 0.0), axis=1, keepdims=True)
        pos = span * SPAN + (lane & (SPAN - 1)).astype(jnp.float32)
        start = jnp.max(jnp.where(first <= pos, first, 0.0), axis=0, keepdims=True)
        low = (start[:, :1].astype(jnp.int32) >> 6).astype(jnp.float32)
        tail = jnp.where(spot == s, span, jnp.where(spot == 2 + s, low, tail))
        meta[1 + s : 2 + s, 0:NQ] = start.astype(jnp.int32)
    meta[0:1, 0:spans] = inverse.astype(jnp.int32)
    meta[0:1, spans:] = tail.astype(jnp.int32)
    for s in range(2):
        rows = slice(s * SPAN, (s + 1) * SPAN)
        for h in range(HEADS):
            cols = slice(h * HD, (h + 1) * HD)
            dst = slice(h * SPAN, (h + 1) * SPAN)
            qs[s, dst, :] = q_ref[rows, cols]
            gs[s, dst, :] = og_ref[rows, cols]
            tmp[dst, :] = og_ref[rows, cols].astype(jnp.float32) * ao_ref[rows, cols].astype(
                jnp.float32
            )
        fmeta[s : s + 1, :] = jnp.sum(tmp[...].T, axis=0, keepdims=True)
        fmeta[2 + s : 3 + s, :] = jnp.concatenate(
            [lse_ref[h : h + 1, rows] for h in range(HEADS)], axis=1
        )
        qt[s] = qs[s].T
        gt[s] = gs[s].T


ORDERS = (("x", "y", "z"), ("y", "z", "x"), ("z", "x", "y"))
COLS = 2 * HD
HALF = {1: pl.ds(0, HD), -1: pl.ds(HD, HD)}
FULL = pl.ds(0, COLS)


def here():
    i, o = lax.axis_index("inner"), lax.axis_index("outer")
    return {"x": (o // 4) * 2 + i // 8, "y": o % 4, "z": (i // 2) % 4, "core": i % 2}


def device(c):
    return ((c["x"] % 2) * 8 + c["z"] * 2 + c["core"], (c["x"] // 2) * 4 + c["y"])


def moved(c, axis, by):
    out = dict(c)
    out[axis] = (c[axis] + by + 4) % 4
    return out


def place(sel, core=None):
    where = tuple(slice(None) if sel[a] is None else sel[a] for a in "xzy")
    return where if core is None else (core, *where)


def row_parts(rows):
    first = -(-rows // 3 // 16) * 16
    sizes = (first, first, rows - 2 * first)
    return [(sum(sizes[:i]), sizes[i]) for i in range(3)]


class Copies:
    def __init__(self, send_sem, recv_sem):
        self.send_sem, self.recv_sem, self.all = send_sem, recv_sem, []

    def send(self, src, dst, target):
        k = len(self.all)
        copy = pltpu.make_async_remote_copy(
            src_ref=src,
            dst_ref=dst,
            send_sem=self.send_sem.at[k],
            recv_sem=self.recv_sem.at[k],
            device_id=device(target),
            device_id_type=pl.DeviceIdType.MESH,
        )
        copy.start()
        self.all.append(copy)
        return copy

    def drain(self):
        for copy in self.all:
            copy.wait_send()


def meet(me):
    barrier = pltpu.get_barrier_semaphore()
    partner = dict(me, core=1 - me["core"])
    others = [moved(me, a, d) for a in "xyz" for d in (1, -1, 2)] + [partner]
    for other in others:
        pl.semaphore_signal(
            barrier, inc=1, device_id=device(other), device_id_type=pl.DeviceIdType.MESH
        )
    pl.semaphore_wait(barrier, len(others))
    return partner


GATHER_COPIES = 3 * (3 + 4 + 16 + 16)


def gather_kernel(kv_ref, *refs):
    sources, targets, out, blank = refs[:6], refs[6:12], refs[12], refs[13]
    held, made = refs[14:20], refs[20:26]
    tmp, zeros, send_sem, recv_sem, own_sem, small_sem, zero_sem = refs[26:]
    zrows = zeros.shape[0]
    wiped = [
        pltpu.make_async_copy(zeros, blank.at[pl.ds(k * zrows, zrows)], zero_sem.at[k])
        for k in range(blank.shape[0] // zrows)
    ]
    taken = [
        pltpu.make_async_copy(sources[k], held[k], small_sem.at[k]) for k in range(6)
    ]
    given = [
        pltpu.make_async_copy(made[k], targets[k], small_sem.at[6 + k]) for k in range(6)
    ]
    for copy in taken:
        copy.start()
    me = here()
    core = me["core"]
    own = pltpu.make_async_copy(kv_ref, out.at[place(me, core)], own_sem)
    own.start()
    partner = meet(me)
    net = Copies(send_sem, recv_sem)
    parts = row_parts(kv_ref.shape[0])

    def block(part, sel, cols=FULL):
        return out.at[(*place(sel, core), pl.ds(*parts[part]), cols)]

    def push(part, sel, axis, by, cols=FULL, src=None):
        ref = block(part, sel, cols)
        return net.send(ref if src is None else src, ref, moved(me, axis, by))

    across = []

    def cross(part, sel):
        ref = block(part, sel)
        across.append(net.send(ref, ref, partner))

    def both(part, sel, axis):
        return {d: push(part, sel, axis, d) for d in (1, -1)}

    def relay(part, sel, axis, copies):
        out_copies = {}
        for d in (1, -1):
            copies[d].wait_recv()
            got = dict(sel, **{axis: moved(me, axis, -d)[axis]})
            out_copies[d] = push(part, got, axis, d, HALF[d])
            cross(part, got)
        return out_copies

    def settle(copies):
        for copy in copies.values():
            copy.wait_recv()

    colors = range(3)
    mine = {a: me[a] for a in "xyz"}
    first = [
        {
            d: push(i, mine, ORDERS[i][0], d, src=kv_ref.at[pl.ds(*parts[i]), :])
            for d in (2, 1, -1)
        }
        for i in colors
    ]
    for copy in taken:
        copy.wait()
    prepare(*held, *made, tmp)
    for copy in given:
        copy.start()
    zeros[...] = jnp.zeros_like(zeros)
    for copy in wiped:
        copy.start()
    own.wait()
    line = [dict(mine, **{ORDERS[i][0]: None}) for i in colors]
    plane = []
    wave = [{} for i in colors]
    last = [{} for i in colors]

    def piece(i, by):
        return dict(line[i], **{ORDERS[i][1]: moved(me, ORDERS[i][1], by)[ORDERS[i][1]]})

    for i in colors:
        settle(first[i])
        plane.append(both(i, line[i], ORDERS[i][1]))
    for i in colors:
        wave[i][0] = both(i, piece(i, 0), ORDERS[i][2])
    for i in colors:
        cross(i, line[i])
    turn = [{} for i in colors]
    for by in (1, -1):
        for i in colors:
            a2 = ORDERS[i][1]
            plane[i][-by].wait_recv()
            turn[i][-by] = push(i, piece(i, by), a2, -by, HALF[-by])
    for by in (1, -1):
        for i in colors:
            wave[i][by] = both(i, piece(i, by), ORDERS[i][2])
            cross(i, piece(i, by))
    last0 = [relay(i, piece(i, 0), ORDERS[i][2], wave[i][0]) for i in colors]
    for i in colors:
        last[i][0] = last0[i]
        settle(turn[i])
        wave[i][2] = both(i, piece(i, 2), ORDERS[i][2])
        cross(i, piece(i, 2))
    for by in (1, -1, 2):
        for i in colors:
            last[i][by] = relay(i, piece(i, by), ORDERS[i][2], wave[i][by])
    for by in (0, 1, -1, 2):
        for i in colors:
            settle(last[i][by])
            a3 = ORDERS[i][2]
            cross(i, dict(piece(i, by), **{a3: moved(me, a3, 2)[a3]}))
    for copy in across:
        copy.wait_recv()
    for copy in given + wiped:
        copy.wait()
    net.drain()


def gather_keys(keys_values, queries, out_grad, attn_out, log_sums, doc_ids, span_order):
    rows = keys_values.shape[0]
    vmem = pl.BlockSpec(memory_space=pltpu.VMEM)
    anyspace = pl.BlockSpec(memory_space=pl.ANY)
    sources = (
        queries,
        out_grad,
        attn_out,
        log_sums,
        doc_ids.reshape(-1, 128),
        span_order.reshape(-1, 128),
    )
    made = [
        ((2, NQ, HD), jnp.bfloat16),
        ((2, NQ, HD), jnp.bfloat16),
        ((2, HD, NQ), jnp.bfloat16),
        ((2, HD, NQ), jnp.bfloat16),
        ((8, 2 * span_order.shape[0]), jnp.int32),
        ((8, NQ), jnp.float32),
    ]
    *small, out, blank = pl.pallas_call(
        gather_kernel,
        out_shape=(
            *[jax.ShapeDtypeStruct(*m) for m in made],
            jax.ShapeDtypeStruct((2, 4, 4, 4, rows, COLS), keys_values.dtype),
            jax.ShapeDtypeStruct((128 * rows, COLS), jnp.bfloat16),
        ),
        in_specs=[vmem] + [anyspace] * 6,
        out_specs=[anyspace] * 8,
        scratch_shapes=[pltpu.VMEM(v.shape, v.dtype) for v in sources]
        + [pltpu.VMEM(*m) for m in made]
        + [
            pltpu.VMEM((NQ, HD), jnp.float32),
            pltpu.VMEM((1024, COLS), jnp.bfloat16),
            pltpu.SemaphoreType.DMA((GATHER_COPIES,)),
            pltpu.SemaphoreType.DMA((GATHER_COPIES,)),
            pltpu.SemaphoreType.DMA,
            pltpu.SemaphoreType.DMA((12,)),
            pltpu.SemaphoreType.DMA((128 * rows // 1024,)),
        ],
        compiler_params=pltpu.CompilerParams(collective_id=0, has_side_effects=True),
        name="gather_keys",
    )(keys_values, *sources)
    qs, gs, qt, gt, meta, fmeta = small
    return meta, fmeta, qs, gs, qt, gt, out.reshape(128 * rows, COLS), blank


KEYS = (2, 1, -1, 0)
AWAY = (1, -1, 2)


class Scatter:
    def __init__(self, me, net, mine, other, third, second, first, halves, rows):
        self.me, self.net, self.mine, self.other, self.halves = me, net, mine, other, halves
        self.buffers = {3: third, 2: second, 1: first}
        self.parts = row_parts(rows)
        self.spot = {a: me[a] for a in "xyz"}
        self.flight = {}

    def at(self, i, d1, d2, d3):
        sel = dict(self.spot)
        for a, d in zip(ORDERS[i], (d1, d2, d3)):
            sel[a] = None if d is None else moved(self.me, a, d)[a]
        return sel

    def ix(self, i, sel, cols=FULL):
        return (*place(sel), pl.ds(*self.parts[i]), cols)

    def level_sel(self, level, i, key, d):
        return {3: self.at(i, None, key, d), 2: self.at(i, None, d, 0), 1: self.at(i, d, 0, 0)}[level]

    def blocks(self, level, i, key, d):
        sel = self.level_sel(level, i, key, d)
        if level == 1:
            return [((), sel)]
        return [((v,), dict(sel, **{ORDERS[i][0]: v})) for v in range(4)]

    def lead(self, level, i, key, d):
        side = AWAY.index(d)
        return (i, KEYS.index(key), side) if level == 3 else (i, side)

    def slot(self, buf, level, i, key, d):
        lines = () if level == 1 else (slice(None),)
        return buf.at[(*self.lead(level, i, key, d), *lines, pl.ds(0, self.parts[i][1]), slice(None))]

    def row(self, level, i, key, d, v):
        return (*self.lead(level, i, key, d), *v, pl.ds(0, self.parts[i][1]), slice(None))

    def send(self, level, i, key, d):
        src = self.mine.at[self.ix(i, self.level_sel(level, i, key, d))]
        dst = self.slot(self.buffers[level], level, i, key, d)
        to = moved(self.me, ORDERS[i][level - 1], d)
        self.flight[level, i, key, d] = self.net.send(src, dst, to)

    def add_core(self, i, d2, d3):
        self.arrived(i, d2, d3)
        for _, sel in self.blocks(3, i, d2, d3):
            ix = self.ix(i, sel)
            self.mine[ix] = self.mine[ix] + self.other[ix]

    def part_ways(self, level, i, key):
        sel = self.level_sel(level, i, key, 2)
        for d in (1, -1):
            dst = self.slot(self.halves[level], level, i, key, d)
            src = self.mine.at[self.ix(i, sel, HALF[d])]
            to = moved(self.me, ORDERS[i][level - 1], d)
            self.flight["half", level, i, key, d] = self.net.send(src, dst, to)

    def join(self, level, i, key, d):
        self.flight["half", level, i, key, d].wait_recv()
        for v, sel in self.blocks(level, i, key, d):
            ix = self.ix(i, sel, HALF[d])
            self.mine[ix] = self.mine[ix] + self.halves[level][self.row(level, i, key, d, v)]
        self.send(level, i, key, d)

    def open(self, i, key):
        if 3 not in self.halves:
            for d in AWAY:
                self.send(3, i, key, d)
            return
        if self.other is not None:
            self.add_core(i, key, 2)
        self.part_ways(3, i, key)
        if self.other is not None:
            self.add_core(i, key, 1)
            self.add_core(i, key, -1)

    def close(self, level, i, key=0, write=None):
        sides = (1, -1) if level in self.halves else AWAY
        if level == 3 and self.other is not None:
            self.arrived(i, key, 0)
        for d in sides:
            self.flight[level, i, key, d].wait_recv()
        for v, sel in self.blocks(level, i, key, 0):
            ix = self.ix(i, sel)
            total = self.mine[ix].astype(jnp.float32)
            if level == 3 and self.other is not None:
                total = total + self.other[ix].astype(jnp.float32)
            for d in sides:
                total = total + self.buffers[level][self.row(level, i, key, d, v)].astype(jnp.float32)
            if write is None:
                self.mine[ix] = total.astype(self.mine.dtype)
            else:
                write(self.parts[i], total)

    def finish(self, i, key):
        self.close(3, i, key)
        if key == 0:
            return
        if 2 not in self.halves:
            self.send(2, i, 0, key)
        elif key == 2:
            self.part_ways(2, i, 0)
        else:
            self.join(2, i, 0, key)

    def run(self, ready, write, aside):
        colors = range(3)
        lag = 2 if 3 in self.halves else 1
        for n in range(len(KEYS) + lag):
            if n < len(KEYS):
                for i in colors:
                    ready(i, KEYS[n])
                    self.open(i, KEYS[n])
            if lag == 2 and 1 <= n <= len(KEYS):
                for i in colors:
                    for d in (1, -1):
                        self.join(3, i, KEYS[n - 1], d)
            if n == len(KEYS) - 1:
                aside()
            if n >= lag:
                for i in colors:
                    self.finish(i, KEYS[n - lag])
        for i in colors:
            self.close(2, i)
            for d in AWAY:
                self.send(1, i, 0, d)
        for i in colors:
            self.close(1, i, write=write)


def scatter_scratch(rows, planes, relayed):
    top = row_parts(rows)[0][1]
    return (
        [pltpu.VMEM((4, 4, 4, rows, COLS), jnp.bfloat16)] * planes
        + [
            pltpu.VMEM((3, 4, 3, 4, top, COLS), jnp.bfloat16),
            pltpu.VMEM((3, 3, 4, top, COLS), jnp.bfloat16),
            pltpu.VMEM((3, 3, top, COLS), jnp.bfloat16),
        ]
        + [
            pltpu.VMEM((3, 4, 3, 4, top, HD) if level == 3 else (3, 3, 4, top, HD), jnp.bfloat16)
            for level in relayed
        ]
    )


KV_RELAYED = (3, 2)
W_RELAYED = ()
SCATTER_COPIES = 2 * 3 * (4 * 4 + 4 + 3) + 21 + 8 + 1


def scatter_kernel(part_ref, x_ref, kv_out, w_out, *scratch):
    kv_end = 5 + len(KV_RELAYED)
    w_end = kv_end + 4 + len(W_RELAYED)
    kv_bufs, w_bufs = scratch[:kv_end], scratch[kv_end:w_end]
    x_buf, x_theirs, xt, pair, send_sem, recv_sem, load_sem = scratch[w_end:]
    x_load = pltpu.make_async_copy(x_ref, x_buf, load_sem.at[12])
    me = here()
    core = me["core"]
    rows, w_rows = kv_out.shape[0], w_out.shape[0]
    wide = 8 * w_rows
    net = Copies(send_sem, recv_sem)
    job = Scatter(me, net, *kv_bufs[:5], dict(zip(KV_RELAYED, kv_bufs[5:])), rows)
    w_job = Scatter(me, net, w_bufs[0], None, *w_bufs[1:4], dict(zip(W_RELAYED, w_bufs[4:])), w_rows)
    loads, swaps = {}, {}
    for n, key in enumerate(KEYS):
        for i in range(3):
            sel = job.at(i, None, key, None)
            src = part_ref.at[(*place(sel, core), pl.ds(*job.parts[i]), FULL)]
            dst = job.mine.at[job.ix(i, sel)]
            loads[i, key] = pltpu.make_async_copy(src, dst, load_sem.at[3 * n + i])
            loads[i, key].start()
    x_load.start()
    partner = meet(me)
    for key in KEYS:
        for d in KEYS if key == KEYS[0] else (None,):
            for i in range(3):
                sel = job.at(i, None, key, d)
                src = part_ref.at[(*place(sel, 1 - core), pl.ds(*job.parts[i]), FULL)]
                swaps[i, key, d] = net.send(src, job.other.at[job.ix(i, sel)], partner)

    def arrived(i, key, d):
        copy = swaps.pop((i, key, d if key == KEYS[0] else None), None)
        if copy is not None:
            copy.wait_recv()

    job.arrived = arrived

    def columns(j, which):
        first = (j // 4 * 8 + j % 4 * 2 + which) * wide
        return x_buf.at[:, pl.ds(pl.multiple_of(first, 128), wide)]

    x_load.wait()
    x_swaps = [net.send(columns(j, 1 - core), x_theirs.at[j], partner) for j in range(8)]
    for j in range(8):
        xt[j, :, :rows] = columns(j, core)[...].T

    def ready(i, key):
        loads[i, key].wait()

    def turn_inputs():
        for j in range(8):
            x_swaps[j].wait_recv()
            xt[j, :, rows:] = x_theirs[j].T

    def write(part, total):
        low = total.astype(kv_out.dtype)
        kv_out[pl.ds(*part), :] = low
        pair[pl.ds(*part), :] = low

    job.run(ready, write, turn_inputs)

    swap = net.send(pair.at[pl.ds(0, rows)], pair.at[pl.ds(rows, rows)], partner)
    swap.wait_recv()
    both = pair[...]
    for j in range(8):
        out = jnp.dot(xt[j], both, preferred_element_type=jnp.float32).astype(jnp.bfloat16)
        for xh in range(2):
            for y in range(4):
                first = (xh * 4 + y) * w_rows
                w_job.mine[2 * xh + j // 4, j % 4, y] = out[first : first + w_rows]

    def w_write(part, total):
        w_out[pl.ds(*part), :] = total

    w_job.run(lambda i, key: None, w_write, lambda: None)
    net.drain()


def scatter_grads(kv_part, layer_input):
    tokens, width = kv_part.shape[0], layer_input.shape[1]
    rows, w_rows = tokens // 128, width // 128
    vmem = pl.BlockSpec(memory_space=pltpu.VMEM)
    return pl.pallas_call(
        scatter_kernel,
        out_shape=(
            jax.ShapeDtypeStruct((rows, COLS), jnp.bfloat16),
            jax.ShapeDtypeStruct((w_rows, COLS), jnp.float32),
        ),
        in_specs=[pl.BlockSpec(memory_space=pl.ANY)] * 2,
        out_specs=(vmem, vmem),
        scratch_shapes=scatter_scratch(rows, 2, KV_RELAYED)
        + scatter_scratch(w_rows, 1, W_RELAYED)
        + [
            pltpu.VMEM((rows, width), jnp.bfloat16),
            pltpu.VMEM((8, rows, 8 * w_rows), jnp.bfloat16),
            pltpu.VMEM((8, 8 * w_rows, 2 * rows), jnp.bfloat16),
            pltpu.VMEM((2 * rows, COLS), jnp.bfloat16),
            pltpu.SemaphoreType.DMA((SCATTER_COPIES,)),
            pltpu.SemaphoreType.DMA((SCATTER_COPIES,)),
            pltpu.SemaphoreType.DMA((13,)),
        ],
        compiler_params=pltpu.CompilerParams(collective_id=1, has_side_effects=True),
        name="scatter_grads",
    )(kv_part.reshape(2, 4, 4, 4, rows, COLS), layer_input)


def copy_kernel(a, b, a_out, b_out):
    a_out[...] = a[...]
    b_out[...] = b[...]


def handed_on(a, b):
    vmem = pl.BlockSpec(memory_space=pltpu.VMEM)
    return pl.pallas_call(
        copy_kernel,
        out_shape=[jax.ShapeDtypeStruct(v.shape, v.dtype) for v in (a, b)],
        in_specs=[vmem] * 2,
        out_specs=[vmem] * 2,
        name="handed_on",
    )(a, b)


def per_device(
    layer_input, queries, keys_values, attn_out, out_grad, log_sums, doc_ids, span_order
):
    query_grad, kv_part = window_grads(
        *gather_keys(keys_values, queries, out_grad, attn_out, log_sums, doc_ids, span_order)
    )
    return (query_grad, *handed_on(*scatter_grads(kv_part, layer_input)))


def solution(mesh):
    rows = P(("inner", "outer"), None)
    return jax.shard_map(
        per_device,
        mesh=mesh,
        in_specs=(rows, rows, rows, rows, rows, P(None, ("inner", "outer")), P(), P()),
        out_specs=(rows, rows, rows),
        check_vma=False,
    )
```
